32 devices in a mesh: rep: 2 (over core), shard: 16 (over z, y, x).
Axes of the slice: x: 2, y: 2, z: 4, core: 2. Of those that a mesh axis runs over, the one named last changes fastest.
Arguments:
- text_rows: bfloat16 [64, 512, 768], P(('rep', 'shard')), may hold values from -6 to 6
- slot_ids: int32 [64, 512], P(('rep', 'shard')), may hold values from 0 to 128, as said below
- seg_count: int32 [64], P(('rep', 'shard')), may hold values from 5 to 128, as said below
- w_qkv: bfloat16 [768, 2304], P('shard'), may hold values from -0.21875 to 0.21875
- qv_bias: bfloat16 [1536], P('shard'), may hold values from -3 to 3
- w_out: bfloat16 [768, 768], P('shard'), may hold values from -0.625 to 0.625
- out_bias: bfloat16 [768], P('shard'), may hold values from -3 to 3
- ln1_gain: bfloat16 [768], P('shard'), may hold values from 0.5 to 1.5
- ln1_shift: bfloat16 [768], P('shard'), may hold values from -3 to 3
- w_up: bfloat16 [768, 3072], P('shard'), may hold values from -0.21875 to 0.21875
- up_bias: bfloat16 [3072], P('shard'), may hold values from -3 to 3
- w_down: bfloat16 [3072, 768], P('shard'), may hold values from -0.109375 to 0.109375
- down_bias: bfloat16 [768], P('shard'), may hold values from -3 to 3
- ln2_gain: bfloat16 [768], P('shard'), may hold values from 0.5 to 1.5
- ln2_shift: bfloat16 [768], P('shard'), may hold values from -3 to 3
- cotangent: bfloat16 [64, 640, 768], P(('rep', 'shard')), may hold values from -6 to 6
Outputs:
- layer_out: bfloat16 [64, 640, 768], P(('rep', 'shard'))
- grad_text: float32 [64, 512, 768], P(('rep', 'shard'))
- grad_w_qkv: float32 [768, 2304], P('shard')
- grad_qv_bias: float32 [1536], P('shard')
- grad_w_out: float32 [768, 768], P('shard')
- grad_out_bias: float32 [768], P('shard')
- grad_ln1_gain: float32 [768], P('shard')
- grad_ln1_shift: float32 [768], P('shard')
- grad_w_up: float32 [768, 3072], P('shard')
- grad_up_bias: float32 [3072], P('shard')
- grad_w_down: float32 [3072, 768], P('shard')
- grad_down_bias: float32 [768], P('shard')
- grad_ln2_gain: float32 [768], P('shard')
- grad_ln2_shift: float32 [768], P('shard')
The draws below stay inside these ranges and needn't reach their ends.
Inputs may be any that keep to these rules, and one draw needn't show every extreme that they name: `seg_count`: one document has exactly 128 segments. `slot_ids`: 128 marks a text row in no segment; any other value is below its document's seg_count.
All inputs are finite; a program needn't handle non-finite values.
Results may differ from the reference program's by a relative error of at most 0.012.
The reference program's roundings to bfloat16 on the way count: a program that leaves them out, or rounds other values in their place, can miss the bound.
Values may be sent and summed in bfloat16 or wider, within the bound.
No kernel may reach another device: no remote copies, remote signals or barrier semaphores. Data moves between devices by JAX's collectives and lax.ppermute only.
A program may use at most 192 MiB of HBM per device.

```python
import jax
import jax.numpy as jnp
from jax import lax

D = 768
HEADS = 12
HEAD_DIM = 64
FF = 3072
TEXT = 512
SLOTS = 128
ROWS = 640
DOCS = 64


def doc_counts(key):
    lowest = min(5, SLOTS)
    span = SLOTS - lowest + 1
    raw_draw = jax.random.randint(jax.random.fold_in(key, 11), (DOCS,), 0, span)
    counts = lowest + raw_draw * raw_draw * raw_draw // (span * span)
    return counts.at[0].set(SLOTS).astype(jnp.int32)


def draw_seg_count(key, part):
    return doc_counts(key)


def draw_slot_ids(key, part):
    counts = doc_counts(key)
    positions = jnp.arange(TEXT, dtype=jnp.int32)
    jitter = jax.random.randint(jax.random.fold_in(key, 17), (DOCS, TEXT), 0, 8)
    segment = (positions[None, :] + jitter) * counts[:, None] // (TEXT + 8)
    dropped = jax.random.randint(jax.random.fold_in(key, 23), (DOCS, TEXT), 0, 8) == 0
    return jnp.where(dropped, SLOTS, segment).astype(jnp.int32)


def steps_of(rng, shape, split, least, high):
    level, own = 1.0, jax.random.fold_in(rng, 6)
    for axis_at, blocks in split:
        steps = jnp.exp(jax.random.uniform(jax.random.fold_in(own, axis_at), (blocks,), jnp.float32, least / len(split), high / len(split)))
        level = level * jnp.repeat(steps, shape[axis_at] // blocks).reshape([-1 if axis == axis_at else 1 for axis in range(len(shape))])
    return level


def gaussian(stream_key, extent, scale, most, pieces=(), held_as=jnp.bfloat16):
    array = scale * jax.random.normal(stream_key, extent, jnp.float32)
    if pieces:
        array = array * steps_of(stream_key, extent, pieces, -0.22, 0.18)
    return jnp.clip(array, -most, most).astype(held_as)


def setup_inputs(seed: int = 0) -> dict:
    seeds = jax.random.split(jax.random.key(seed), 17)
    text_rows = gaussian(seeds[0], (DOCS, TEXT, D), 1.0, 6.0, ((0, 32),))
    slot_ids = draw_slot_ids(jax.random.fold_in(seeds[16], 71), 0)
    seg_count = draw_seg_count(jax.random.fold_in(seeds[16], 71), 0)
    w_qkv = gaussian(seeds[3], (D, 3 * D), D ** -0.5, 0.21875, ((0, 16),))
    qv_bias = gaussian(seeds[4], (2 * D,), 0.5, 3.0, ((0, 16),))
    w_out = gaussian(seeds[5], (D, D), (D // 8) ** -0.5, 0.625, ((0, 16),))
    out_bias = gaussian(seeds[6], (D,), 0.5, 3.0, ((0, 16),))
    ln1_gain = jnp.clip(1.0 + 0.1 * jax.random.normal(seeds[7], (D,), jnp.float32), 0.5, 1.5).astype(jnp.bfloat16)
    ln1_shift = gaussian(seeds[8], (D,), 0.5, 3.0, ((0, 16),))
    w_up = gaussian(seeds[9], (D, FF), D ** -0.5, 0.21875, ((0, 16),))
    up_bias = gaussian(seeds[10], (FF,), 0.5, 3.0, ((0, 16),))
    w_down = gaussian(seeds[11], (FF, D), FF ** -0.5, 0.109375, ((0, 16),))
    down_bias = gaussian(seeds[12], (D,), 0.5, 3.0, ((0, 16),))
    ln2_gain = jnp.clip(1.0 + 0.1 * jax.random.normal(seeds[13], (D,), jnp.float32), 0.5, 1.5).astype(jnp.bfloat16)
    ln2_shift = gaussian(seeds[14], (D,), 0.5, 3.0, ((0, 16),))
    cotangent = gaussian(seeds[15], (DOCS, ROWS, D), 1.0, 6.0, ((0, 32),))
    return dict(text_rows=text_rows, slot_ids=slot_ids, seg_count=seg_count, w_qkv=w_qkv, qv_bias=qv_bias, w_out=w_out, out_bias=out_bias, ln1_gain=ln1_gain, ln1_shift=ln1_shift, w_up=w_up, up_bias=up_bias, w_down=w_down, down_bias=down_bias, ln2_gain=ln2_gain, ln2_shift=ln2_shift, cotangent=cotangent)


layer_eps = 1e-05
score_scale = 0.125
masked_score = -1000000000.0

@jax.custom_vjp
def low(v):
    return lax.optimization_barrier(v.astype(jnp.bfloat16)).astype(jnp.float32)

@jax.custom_vjp
def low_back(v):
    return v

def low_keep(v):
    return (low(v), None)

def low_pass(kept, grad):
    return (grad,)

def back_keep(v):
    return (v, None)

def back_low(kept, grad):
    return (low(grad),)
low.defvjp(low_keep, low_pass)
low_back.defvjp(back_keep, back_low)

def hdot(left, right):
    return jnp.dot(left, right, precision=lax.Precision.HIGHEST, preferred_element_type=jnp.float32)

def layer_norm(values, gain_vec, shift_vec):
    average = lax.optimization_barrier(jnp.mean(values, axis=-1, keepdims=True))
    centred = values - average
    spread = lax.optimization_barrier(jnp.mean(centred * centred, axis=-1, keepdims=True))
    return centred * lax.rsqrt(spread + layer_eps) * gain_vec + shift_vec

def encode_doc(text_doc, doc_ids, doc_count, weights):
    w_qkv, qv_bias, w_out, out_bias, ln1_gain, ln1_shift, w_up, up_bias, w_down, down_bias, ln2_gain, ln2_shift = weights
    slot_range = jnp.arange(SLOTS, dtype=jnp.int32)
    one_hot = (doc_ids[None, :] == slot_range[:, None]).astype(jnp.float32)
    members = lax.optimization_barrier(jnp.sum(one_hot, axis=1, keepdims=True))
    summed = low_back(hdot(one_hot, text_doc))
    pooled = low(summed / jnp.sqrt(jnp.maximum(members, 1.0)))
    joined = jnp.concatenate([text_doc, pooled], axis=0)
    full_bias = jnp.concatenate([qv_bias[:D], jnp.zeros((D,), jnp.float32), qv_bias[D:]])
    projected = low(low_back(hdot(joined, w_qkv) + full_bias))
    queries = projected[:, :D].reshape(ROWS, HEADS, HEAD_DIM)
    key_rows = projected[:, D:2 * D].reshape(ROWS, HEADS, HEAD_DIM)
    value_rows = projected[:, 2 * D:].reshape(ROWS, HEADS, HEAD_DIM)
    scores = jnp.einsum('qhc,khc->hqk', queries, key_rows, precision=lax.Precision.HIGHEST) * score_scale
    scores = low_back(scores)
    key_live = jnp.concatenate([jnp.ones((TEXT,), jnp.bool_), slot_range < doc_count])
    scores = jnp.where(key_live[None, None, :], scores, masked_score)
    attn_probs = low(jax.nn.softmax(scores, axis=-1))
    context = jnp.einsum('hqk,khc->qhc', attn_probs, value_rows, precision=lax.Precision.HIGHEST).reshape(ROWS, D)
    context = low(low_back(context))
    attn_branch = low_back(hdot(context, w_out) + out_bias)
    normed1 = layer_norm(joined + attn_branch, ln1_gain, ln1_shift)
    up_out = low_back(hdot(low(normed1), w_up) + up_bias)
    active = low(jax.nn.gelu(up_out, approximate=False))
    down_out = low_back(hdot(active, w_down) + down_bias)
    return layer_norm(normed1 + down_out, ln2_gain, ln2_shift)

def reference(text_rows, slot_ids, seg_count, w_qkv, qv_bias, w_out, out_bias, ln1_gain, ln1_shift, w_up, up_bias, w_down, down_bias, ln2_gain, ln2_shift, cotangent):
    weights = tuple((member.astype(jnp.float32) for member in (w_qkv, qv_bias, w_out, out_bias, ln1_gain, ln1_shift, w_up, up_bias, w_down, down_bias, ln2_gain, ln2_shift)))
    text_float = text_rows.astype(jnp.float32)

    def forward(text_all, weight_set):
        doc_step = jax.checkpoint(lambda text_doc, doc_ids, doc_count: encode_doc(text_doc, doc_ids, doc_count, weight_set))
        return lax.map(lambda bundle: doc_step(bundle[0], bundle[1], bundle[2]), (text_all, slot_ids, seg_count))
    result, pullback = jax.vjp(forward, text_float, weights)
    grad_input, grad_set = pullback(cotangent.astype(jnp.float32))
    return (result.astype(jnp.bfloat16), grad_input, grad_set[0], grad_set[1], grad_set[2], grad_set[3], grad_set[4], grad_set[5], grad_set[6], grad_set[7], grad_set[8], grad_set[9], grad_set[10], grad_set[11])
```

```python
import math
from functools import partial

import jax
import jax.numpy as jnp
from jax import lax
from jax.experimental import pallas as pl
from jax.experimental.pallas import tpu as pltpu
from jax.sharding import PartitionSpec as P

HEADS = 12
SLOTS = 128
GROUPS = 3

layer_eps = 1e-05
score_scale = 0.125
masked_score = -1000000000.0
BF = jnp.bfloat16
F32 = jnp.float32
VMEM_LIMIT = 60 * 1024 * 1024

NT = (((1,), (1,)), ((), ()))
NN = (((1,), (0,)), ((), ()))
TN = (((0,), (0,)), ((), ()))


def mm(left, right, dims=NN):
    return lax.dot_general(left, right, dims, preferred_element_type=F32)


def params():
    return pltpu.CompilerParams(vmem_limit_bytes=VMEM_LIMIT)


def any_spec():
    return pl.BlockSpec(memory_space=pl.ANY)


def smem_spec():
    return pl.BlockSpec(memory_space=pltpu.SMEM)


def vmem_spec():
    return pl.BlockSpec(memory_space=pltpu.VMEM)


def halves_of(count):
    return 1 if count == 1 else 2


def load_pieces(piece_refs, place_ref, buf, sem, parts):
    whole = 2 // halves_of(place_ref.shape[1])
    at = 0
    for ref in piece_refs:
        rows = ref.shape[1]
        for i in range(ref.shape[0]):
            row = pl.multiple_of(place_ref[0, at] * rows, 16)
            for col, n, first in parts:
                col, n = col * whole, n * whole
                to = pl.multiple_of(place_ref[1, at] * n + first, 128)
                pltpu.make_async_copy(
                    ref.at[i, :, pl.ds(col, n)], buf.at[pl.ds(row, rows), pl.ds(to, n)], sem
                ).start()
            at += 1


def wait_all(buf, sem):
    pltpu.make_async_copy(buf, buf, sem).wait()


def store_pieces(buf, out_ref, place_ref, sem, n, col):
    rows = out_ref.shape[1]
    for i in range(out_ref.shape[0]):
        row = pl.multiple_of(place_ref[0, i] * rows, 16)
        at = pl.multiple_of(place_ref[1, i] * n, 128)
        pltpu.make_async_copy(
            buf.at[pl.ds(row, rows), pl.ds(at, n)], out_ref.at[i, :, pl.ds(col, n)], sem
        ).start()


def store_half(buf, out_ref, place_ref, sem, half, col):
    rows, n = out_ref.shape[1], buf.shape[1]
    count = out_ref.shape[0] // halves_of(out_ref.shape[0])
    first = (place_ref[1, 0] ^ half) * count
    for i in range(count):
        row = pl.multiple_of(place_ref[0, first + i] * rows, 16)
        pltpu.make_async_copy(
            buf.at[pl.ds(row, rows), :], out_ref.at[first + i, :, pl.ds(col, n)], sem
        ).start()


QKV_PARTS = tuple((g * 384, 384, g * 768) for g in range(GROUPS))


def mid_parts(width, ff):
    return ((0, width // 2, 0), (width // 2, ff // 2, width))


def norm_parts(values):
    average = jnp.mean(values, axis=-1, keepdims=True)
    centred = values - average
    inverse = lax.rsqrt(jnp.mean(centred * centred, axis=-1, keepdims=True) + layer_eps)
    return centred * inverse, inverse


def norm_backward(grad_norm, gain_vec, scaled, inverse):
    grad_scaled = grad_norm * gain_vec
    grad_mean = jnp.mean(grad_scaled, axis=-1, keepdims=True)
    second = jnp.mean(grad_scaled * scaled, axis=-1, keepdims=True)
    return inverse * (grad_scaled - grad_mean - scaled * second)


def put_sums(acc, sums_ref):
    sums_ref[...] = jnp.zeros_like(sums_ref)
    for i in range(acc.shape[0]):
        sums_ref[i : i + 1, :] = jnp.sum(acc[i], axis=0, keepdims=True)


def fold_rows(values):
    rows, cols = values.shape
    return jnp.sum(values.reshape(rows // 8, 8, cols), axis=0)


def one_hot_of(ids_row, dtype):
    slot = lax.broadcasted_iota(jnp.int32, (SLOTS, ids_row.shape[1]), 0)
    return jnp.where(slot == ids_row, 1.0, 0.0).astype(dtype)


def divisor_of(ids_row):
    members = jnp.sum(one_hot_of(ids_row, F32), axis=1, keepdims=True)
    return jnp.sqrt(jnp.maximum(members, 1.0))


def pool_kernel(ids_ref, text_ref, joined_ref):
    text_len = text_ref.shape[1]
    ids_row = ids_ref[0]
    summed = mm(one_hot_of(ids_row, BF), text_ref[0])
    joined_ref[0:text_len, :] = text_ref[0]
    joined_ref[text_len:, :] = (summed / divisor_of(ids_row)).astype(BF)


def pool(slot_ids, text_rows):
    docs, text_len, width = text_rows.shape
    rows = text_len + SLOTS
    return pl.pallas_call(
        pool_kernel,
        out_shape=jax.ShapeDtypeStruct((docs * rows, width), BF),
        grid=(docs,),
        in_specs=[
            pl.BlockSpec((1, 1, text_len), lambda d: (d, 0, 0)),
            pl.BlockSpec((1, text_len, width), lambda d: (d, 0, 0)),
        ],
        out_specs=pl.BlockSpec((rows, width), lambda d: (d, 0)),
        compiler_params=params(),
        name="pool",
    )(slot_ids.reshape(docs, 1, text_len), text_rows)


def head_mask(e, width=128, size=64):
    lane = lax.broadcasted_iota(jnp.int32, (1, width), 1)
    return (lane // size) == e


def mask_keys(scores, count, text_len):
    slot = lax.broadcasted_iota(jnp.int32, (1, SLOTS), 1)
    tail = jnp.where(slot < count, scores[:, text_len:], masked_score)
    return jnp.concatenate([scores[:, :text_len], tail], axis=1)


def attn_fwd_kernel(docs, rows, n_arrays, *refs):
    place_ref, count_ref, joined_ref, bias_ref = refs[:4]
    pieces = refs[4 : 4 + n_arrays]
    proj_ref, ctx_ref, wbuf, sem = refs[4 + n_arrays :]
    g = pl.program_id(0)
    width = joined_ref.shape[1]
    span = width // GROUPS

    @pl.when(g == 0)
    def _():
        load_pieces(pieces, place_ref, wbuf, sem, QKV_PARTS)
        wait_all(wbuf, sem)

    cols = pl.ds(pl.multiple_of(g * width, 128), width)
    proj_ref[0] = (mm(joined_ref[...], wbuf[:, cols]) + bias_ref[:, cols]).astype(BF)

    def doc_step(d, carry):
        at = pl.ds(pl.multiple_of(d * rows, 128), rows)
        count = count_ref[d]
        for pair in range(span // 128):
            lo = 128 * pair
            first = 3 * lo
            queries = proj_ref[0, at, first : first + 128] * BF(score_scale)
            keys = proj_ref[0, at, first + 128 : first + 256]
            values = proj_ref[0, at, first + 256 : first + 384]
            total = None
            for e in range(2):
                mask = head_mask(e)
                scores = mm(jnp.where(mask, queries, BF(0)), keys, NT)
                scores = mask_keys(scores, count, rows - SLOTS)
                top = jnp.max(scores, axis=1, keepdims=True)
                weights = jnp.exp(scores - top)
                norm = 1.0 / jnp.sum(weights, axis=1, keepdims=True)
                probs = (weights * norm).astype(BF)
                part = mm(probs, jnp.where(mask, values, BF(0)))
                total = part if total is None else total + part
            ctx_ref[at, lo : lo + 128] = total.astype(BF)
        return carry

    lax.fori_loop(0, docs, doc_step, 0)


def attn_fwd(place, seg_count, joined, bias, pieces):
    docs = seg_count.shape[0]
    total, width = joined.shape
    rows = total // docs
    span = width // GROUPS
    return pl.pallas_call(
        partial(attn_fwd_kernel, docs, rows, len(pieces)),
        out_shape=(
            jax.ShapeDtypeStruct((GROUPS, total, width), BF),
            jax.ShapeDtypeStruct((total, width), BF),
        ),
        grid=(GROUPS,),
        in_specs=[smem_spec(), smem_spec(), vmem_spec(), vmem_spec()] + [any_spec()] * len(pieces),
        out_specs=(
            pl.BlockSpec((1, total, width), lambda g: (g, 0, 0)),
            pl.BlockSpec((total, span), lambda g: (0, g)),
        ),
        scratch_shapes=[pltpu.VMEM((width, 3 * width), BF), pltpu.SemaphoreType.DMA(())],
        compiler_params=params(),
        name="attn_fwd",
    )(place, seg_count, joined, bias, *pieces)


def up_kernel(n_arrays, *refs):
    place_ref, joined_ref, ctx_ref, obias_ref, gain_ref, shift_ref, ubias_ref = refs[:7]
    pieces = refs[7 : 7 + n_arrays]
    scaled_ref, inv_ref, act_ref, slope_ref, wbuf, sem = refs[7 + n_arrays :]
    width = joined_ref.shape[1]

    @pl.when(pl.program_id(0) == 0)
    def _():
        load_pieces(pieces, place_ref, wbuf, sem, mid_parts(width, wbuf.shape[1] - width))
        wait_all(wbuf, sem)

    branch = mm(ctx_ref[...], wbuf[:, :width]) + obias_ref[...]
    scaled, inverse = norm_parts(joined_ref[...].astype(F32) + branch)
    scaled_ref[...] = scaled
    inv_ref[...] = inverse
    low = (scaled * gain_ref[...] + shift_ref[...]).astype(BF)
    ff = act_ref.shape[1]
    step = 768
    for c in range(0, ff, step):
        up = mm(low, wbuf[:, width + c : width + c + step]) + ubias_ref[:, c : c + step]
        half = 0.5 + 0.5 * lax.erf(up * math.sqrt(0.5))
        act_ref[:, c : c + step] = (up * half).astype(BF)
        slope_ref[:, c : c + step] = half + up * (
            jnp.exp(-0.5 * (up * up)) * (1.0 / math.sqrt(2.0 * math.pi))
        )


def up_call(place, joined, ctx, obias, gain, shift, ubias, pieces, block=256):
    total, width = joined.shape
    ff = ubias.shape[1]
    row = lambda i: (i, 0)
    return pl.pallas_call(
        partial(up_kernel, len(pieces)),
        out_shape=(
            jax.ShapeDtypeStruct((total, width), F32),
            jax.ShapeDtypeStruct((total, 1), F32),
            jax.ShapeDtypeStruct((total, ff), BF),
            jax.ShapeDtypeStruct((total, ff), F32),
        ),
        grid=(total // block,),
        in_specs=[
            smem_spec(),
            pl.BlockSpec((block, width), row),
            pl.BlockSpec((block, width), row),
        ]
        + [vmem_spec()] * 4
        + [any_spec()] * len(pieces),
        out_specs=(
            pl.BlockSpec((block, width), row),
            pl.BlockSpec((block, 1), row),
            pl.BlockSpec((block, ff), row),
            pl.BlockSpec((block, ff), row),
        ),
        scratch_shapes=[pltpu.VMEM((width, width + ff), BF), pltpu.SemaphoreType.DMA(())],
        compiler_params=params(),
        name="up",
    )(place, joined, ctx, obias, gain, shift, ubias, *pieces)


def down_kernel(n_arrays, n_rows, n_cols, *refs):
    place_ref, scaled_ref, act_ref, cot_ref, gain1_ref, shift1_ref, dbias_ref, gain_ref, shift_ref = refs[:9]
    pieces = refs[9 : 9 + n_arrays]
    out_ref, resid_ref, sums_ref, gw_ref, wbuf, low_buf, gbuf, acc, sem, osem = refs[9 + n_arrays :]
    step = pl.program_id(0)
    block = cot_ref.shape[0]
    ff = wbuf.shape[0]
    tile = ff // n_cols

    @pl.when(step == 0)
    def _():
        load_pieces(pieces, place_ref, wbuf, sem, ((0, wbuf.shape[1] // 2 * halves_of(place_ref.shape[1]), 0),))
        acc[...] = jnp.zeros_like(acc)
        wait_all(wbuf, sem)

    @pl.when(step < n_rows)
    def _():
        at = pl.ds(pl.multiple_of(step * block, block), block)
        down = mm(act_ref[at, :], wbuf[...]) + dbias_ref[...]
        normed1 = scaled_ref[...] * gain1_ref[...] + shift1_ref[...]
        scaled2, inverse2 = norm_parts(normed1 + down)
        out_ref[...] = (scaled2 * gain_ref[...] + shift_ref[...]).astype(BF)
        grad = cot_ref[...].astype(F32)
        resid = norm_backward(grad, gain_ref[...], scaled2, inverse2)
        resid_ref[...] = resid
        low = resid.astype(BF)
        low_buf[at, :] = low
        acc[0] += fold_rows(grad * scaled2)
        acc[1] += fold_rows(grad)
        acc[2] += fold_rows(low.astype(F32))

    @pl.when(step >= n_rows)
    def _():
        c = step - n_rows
        cols = pl.ds(pl.multiple_of(c * tile, 128), tile)
        gbuf[cols, :] = mm(act_ref[:, cols], low_buf[...], TN).astype(BF)

    @pl.when(step == n_rows + n_cols - 1)
    def _():
        store_pieces(gbuf, gw_ref, place_ref, osem, gbuf.shape[1], 0)
        put_sums(acc, sums_ref)
        wait_all(gbuf, osem)


def down_call(place, scaled1, act, cot, gain1, shift1, dbias, gain, shift, pieces, block=256, tile=384):
    total, width = scaled1.shape
    ff = act.shape[1]
    n_rows, n_cols = total // block, ff // tile
    row = lambda i: (jnp.minimum(i, n_rows - 1), 0)
    count = place.shape[1]
    return pl.pallas_call(
        partial(down_kernel, len(pieces), n_rows, n_cols),
        out_shape=(
            jax.ShapeDtypeStruct((total, width), BF),
            jax.ShapeDtypeStruct((total, width), F32),
            jax.ShapeDtypeStruct((8, width), F32),
            jax.ShapeDtypeStruct((count, ff // count, width), BF),
        ),
        grid=(n_rows + n_cols,),
        in_specs=[smem_spec(), pl.BlockSpec((block, width), row), vmem_spec(), pl.BlockSpec((block, width), row)]
        + [vmem_spec()] * 5
        + [any_spec()] * len(pieces),
        out_specs=(
            pl.BlockSpec((block, width), row),
            pl.BlockSpec((block, width), row),
            pl.BlockSpec((8, width), lambda i: (0, 0)),
            any_spec(),
        ),
        scratch_shapes=[
            pltpu.VMEM((ff, width), BF),
            pltpu.VMEM((total, width), BF),
            pltpu.VMEM((ff, width), BF),
            pltpu.VMEM((3, 8, width), F32),
            pltpu.SemaphoreType.DMA(()),
            pltpu.SemaphoreType.DMA(()),
        ],
        compiler_params=params(),
        name="down",
    )(place, scaled1, act, cot, gain1, shift1, dbias, gain, shift, *pieces)


def ffn_back_kernel(n_up, n_down, n_rows, n_cols, *refs):
    (uplace_ref, dplace_ref, resid_ref, slope_ref, scaled_ref, inv_ref, ctx_ref, gain_ref, shift_ref) = refs[:9]
    ups = refs[9 : 9 + n_up]
    downs = refs[9 + n_up : 9 + n_up + n_down]
    (resid1_ref, gctx_ref, sums_ref, usum_ref, gw_ref) = refs[9 + n_up + n_down : 14 + n_up + n_down]
    wup, wdown, gup, low, gattn, gbuf, acc, uacc, sem, dsem, osem = refs[14 + n_up + n_down :]
    step = pl.program_id(0)
    block, width = resid_ref.shape
    ff = wdown.shape[0]
    tile = gbuf.shape[1]

    @pl.when(step == 0)
    def _():
        load_pieces(downs, dplace_ref, wdown, dsem, ((0, width // 2 * halves_of(dplace_ref.shape[1]), 0),))
        load_pieces(ups, uplace_ref, wup, sem, mid_parts(width, ff))
        acc[...] = jnp.zeros_like(acc)
        uacc[...] = jnp.zeros_like(uacc)
        wait_all(wdown, dsem)
        wait_all(wup, sem)

    @pl.when(step < n_rows)
    def _():
        at = pl.ds(pl.multiple_of(step * block, block), block)
        resid = resid_ref[...]
        gdown = resid.astype(BF)
        chunk = 768
        gnorm = resid
        for c in range(0, ff, chunk):
            gact = mm(gdown, wdown[c : c + chunk, :], NT)
            up = (gact * slope_ref[:, c : c + chunk]).astype(BF)
            gup[at, c : c + chunk] = up
            uacc[:, c : c + chunk] += fold_rows(up.astype(F32))
        gnorm = resid + mm(gup[at, :], wup[:, width:], NT)
        scaled = scaled_ref[...]
        acc[0] += fold_rows(gnorm * scaled)
        acc[1] += fold_rows(gnorm)
        resid1 = norm_backward(gnorm, gain_ref[...], scaled, inv_ref[...])
        resid1_ref[...] = resid1
        attn = resid1.astype(BF)
        gattn[at, :] = attn
        acc[2] += fold_rows(attn.astype(F32))
        low[at, :] = (scaled * gain_ref[...] + shift_ref[...]).astype(BF)
        gctx_ref[...] = mm(attn, wup[:, :width], NT).astype(BF)

    halves = halves_of(uplace_ref.shape[1])

    @pl.when(step == n_rows)
    def _():
        put_sums(acc, sums_ref)
        usum_ref[...] = jnp.sum(uacc[...], axis=0, keepdims=True)
        gbuf[...] = mm(ctx_ref[...], gattn[...], TN).astype(BF)
        store_pieces(gbuf, gw_ref, uplace_ref, osem, width // halves, 0)
        wait_all(gbuf, osem)

    @pl.when(step > n_rows)
    def _():
        c = step - n_rows - 1
        cols = pl.ds(pl.multiple_of(c * tile, 128), tile)
        gbuf[...] = mm(low[...], gup[:, cols], TN).astype(BF)
        per = n_cols // halves
        at = pl.multiple_of(width // halves + (c % per) * tile, 128)
        store_half(gbuf, gw_ref, uplace_ref, osem, c // per, at)
        wait_all(gbuf, osem)


def ffn_back(uplace, dplace, resid2, slope, scaled1, inv1, ctx, gain, shift, ups, downs, block=256):
    total, width = resid2.shape
    ff = slope.shape[1]
    n_rows = total // block
    n_cols = ff // width
    row = lambda i: (jnp.minimum(i, n_rows - 1), 0)
    count = uplace.shape[1]
    halves = halves_of(count)
    return pl.pallas_call(
        partial(ffn_back_kernel, len(ups), len(downs), n_rows, n_cols),
        out_shape=(
            jax.ShapeDtypeStruct((total, width), F32),
            jax.ShapeDtypeStruct((total, width), BF),
            jax.ShapeDtypeStruct((8, width), F32),
            jax.ShapeDtypeStruct((1, ff), F32),
            jax.ShapeDtypeStruct((count, width * halves // count, (width + ff) // halves), BF),
        ),
        grid=(n_rows + 1 + n_cols,),
        in_specs=[
            smem_spec(),
            smem_spec(),
            pl.BlockSpec((block, width), row),
            pl.BlockSpec((block, ff), row),
            pl.BlockSpec((block, width), row),
            pl.BlockSpec((block, 1), row),
            vmem_spec(),
            vmem_spec(),
            vmem_spec(),
        ]
        + [any_spec()] * (len(ups) + len(downs)),
        out_specs=(
            pl.BlockSpec((block, width), row),
            pl.BlockSpec((block, width), row),
            pl.BlockSpec((8, width), lambda i: (0, 0)),
            pl.BlockSpec((1, ff), lambda i: (0, 0)),
            any_spec(),
        ),
        scratch_shapes=[
            pltpu.VMEM((width, width + ff), BF),
            pltpu.VMEM((ff, width), BF),
            pltpu.VMEM((total, ff), BF),
            pltpu.VMEM((total, width), BF),
            pltpu.VMEM((total, width), BF),
            pltpu.VMEM((width, width), BF),
            pltpu.VMEM((3, 8, width), F32),
            pltpu.VMEM((8, ff), F32),
            pltpu.SemaphoreType.DMA(()),
            pltpu.SemaphoreType.DMA(()),
            pltpu.SemaphoreType.DMA(()),
        ],
        compiler_params=params(),
        name="ffn_back",
    )(uplace, dplace, resid2, slope, scaled1, inv1, ctx, gain, shift, *ups, *downs)


def attn_back_kernel(docs, rows, *refs):
    place_ref, count_ref, joined_ref, proj_ref, gctx_ref, gproj_ref, sums_ref, gw_ref, gbuf, osem = refs
    width = joined_ref.shape[1]
    span = width // GROUPS
    text_len = rows - SLOTS

    def doc_step(d, carry):
        at = pl.ds(pl.multiple_of(d * rows, 128), rows)
        count = count_ref[d]
        slot = lax.broadcasted_iota(jnp.int32, (SLOTS, 1), 0)
        for pair in range(span // 128):
            lo = 128 * pair
            first = 3 * lo
            queries = proj_ref[0, at, first : first + 128] * BF(score_scale)
            keys = proj_ref[0, at, first + 128 : first + 256]
            values = proj_ref[0, at, first + 256 : first + 384]
            grads = gctx_ref[at, lo : lo + 128]
            keys_low = keys * BF(score_scale)
            dq = dk = dv = None
            for e in range(2):
                mask = head_mask(e)
                q_e = jnp.where(mask, queries, BF(0))
                g_e = jnp.where(mask, grads, BF(0))
                k_e = jnp.where(mask, keys_low, BF(0))
                scores = mm(keys, q_e, NT)
                tail = jnp.where(slot < count, scores[text_len:, :], masked_score)
                scores = jnp.concatenate([scores[:text_len, :], tail], axis=0)
                top = jnp.max(scores, axis=0, keepdims=True)
                weights = jnp.exp(scores - top)
                probs = weights * (1.0 / jnp.sum(weights, axis=0, keepdims=True))
                gprobs = mm(values, g_e, NT)
                dot = jnp.sum(probs * gprobs, axis=0, keepdims=True)
                gscores = (probs * (gprobs - dot)).astype(BF)
                dv_e = mm(probs.astype(BF), g_e)
                dk_e = mm(gscores, q_e)
                dq_e = mm(k_e, gscores, TN)
                dq = dq_e if dq is None else dq + dq_e
                dk = dk_e if dk is None else dk + dk_e
                dv = dv_e if dv is None else dv + dv_e
            gproj_ref[0, at, first : first + 128] = dq.T.astype(BF)
            gproj_ref[0, at, first + 128 : first + 256] = dk.astype(BF)
            gproj_ref[0, at, first + 256 : first + 384] = dv.astype(BF)
        return carry

    lax.fori_loop(0, docs, doc_step, 0)
    sums_ref[0] = jnp.sum(gproj_ref[0].astype(F32), axis=0, keepdims=True)
    gbuf[...] = mm(joined_ref[...], gproj_ref[0], TN).astype(BF)
    n = width // halves_of(gw_ref.shape[0])
    store_pieces(gbuf, gw_ref, place_ref, osem, n, pl.multiple_of(pl.program_id(0) * n, 128))
    wait_all(gbuf, osem)


def attn_back(place, seg_count, joined, proj, gctx, first=0, groups=GROUPS):
    docs = seg_count.shape[0]
    total, width = joined.shape
    rows = total // docs
    span = width // GROUPS
    count = place.shape[1]
    halves = halves_of(count)
    return pl.pallas_call(
        partial(attn_back_kernel, docs, rows),
        out_shape=(
            jax.ShapeDtypeStruct((groups, total, width), BF),
            jax.ShapeDtypeStruct((groups, 1, width), F32),
            jax.ShapeDtypeStruct((count, width * halves // count, groups * width // halves), BF),
        ),
        grid=(groups,),
        in_specs=[
            smem_spec(),
            smem_spec(),
            vmem_spec(),
            pl.BlockSpec((1, total, width), lambda g: (first + g, 0, 0)),
            pl.BlockSpec((total, span), lambda g: (0, first + g)),
        ],
        out_specs=(
            pl.BlockSpec((1, total, width), lambda g: (g, 0, 0)),
            pl.BlockSpec((1, 1, width), lambda g: (g, 0, 0)),
            any_spec(),
        ),
        scratch_shapes=[pltpu.VMEM((width, width), BF), pltpu.SemaphoreType.DMA(())],
        compiler_params=params(),
        name="attn_back",
    )(place, seg_count, joined, proj, gctx)


def text_kernel(n_arrays, n_grads, *refs):
    place_ref, ids_ref, resid_ref = refs[:3]
    grads = refs[3 : 3 + n_grads]
    pieces = refs[3 + n_grads : 3 + n_grads + n_arrays]
    out_ref, wbuf, sem = refs[3 + n_grads + n_arrays :]
    width = wbuf.shape[0]
    text_len = out_ref.shape[1]

    @pl.when(pl.program_id(0) == 0)
    def _():
        load_pieces(pieces, place_ref, wbuf, sem, QKV_PARTS)
        wait_all(wbuf, sem)

    total = resid_ref[...]
    g = 0
    for ref in grads:
        for i in range(ref.shape[0]):
            total = total + mm(ref[i], wbuf[:, g * width : (g + 1) * width], NT)
            g += 1
    ids_row = ids_ref[0]
    summed = (total[text_len:, :] / divisor_of(ids_row)).astype(BF)
    out_ref[0] = total[:text_len, :] + mm(one_hot_of(ids_row, BF), summed, TN)


def text_grad(place, slot_ids, resid1, grads, pieces):
    docs, text_len = slot_ids.shape
    total, width = resid1.shape
    rows = total // docs
    return pl.pallas_call(
        partial(text_kernel, len(pieces), len(grads)),
        out_shape=jax.ShapeDtypeStruct((docs, text_len, width), F32),
        grid=(docs,),
        in_specs=[
            smem_spec(),
            pl.BlockSpec((1, 1, text_len), lambda d: (d, 0, 0)),
            pl.BlockSpec((rows, width), lambda d: (d, 0)),
        ]
        + [pl.BlockSpec((g.shape[0], rows, width), lambda d: (0, d, 0)) for g in grads]
        + [any_spec()] * len(pieces),
        out_specs=pl.BlockSpec((1, text_len, width), lambda d: (d, 0, 0)),
        scratch_shapes=[pltpu.VMEM((width, 3 * width), BF), pltpu.SemaphoreType.DMA(())],
        compiler_params=params(),
        name="text_grad",
    )(place, slot_ids.reshape(docs, 1, text_len), resid1, *grads, *pieces)


AXES = ("rep", "shard")
CHIPS = 16


def flips(core):
    return (1, 2) if core == 0 else (2, 1)


def pairs(flip_of):
    return [
        (core * CHIPS + s, core * CHIPS + (s ^ flip_of(core)))
        for core in range(2)
        for s in range(CHIPS)
    ]


Z_PERMS = [pairs(lambda core, k=k: k << 2) for k in (1, 2, 3)]
FIRST = pairs(lambda core: flips(core)[0])
SECOND = pairs(lambda core: flips(core)[1])
SWAP = [(core * CHIPS + s, (1 - core) * CHIPS + s) for core in range(2) for s in range(CHIPS)]


def send(array, perm):
    return lax.ppermute(array, AXES, perm)


def place_table(core, shard):
    order = jnp.arange(2 * CHIPS, dtype=jnp.int32)
    other, second, first, far = order // 16, (order // 8) % 2, (order // 4) % 2, order % 4
    half = core ^ other
    bits = jnp.where(half == 0, second * 2 + first, first * 2 + second)
    return jnp.stack([shard ^ (far * 4) ^ bits, half])


def gather(own):
    column = jnp.concatenate([own] + [send(own, perm) for perm in Z_PERMS], axis=0)
    first = send(column, FIRST)
    held = [column, first, send(column, SECOND), send(first, SECOND)]
    return held + [send(part, SWAP) for part in held]


def add(left, right):
    return (left.astype(F32) + right.astype(F32)).astype(BF)


def scatter(pieces):
    got = send(pieces[16:], SWAP)
    keep, away = add(pieces[:8], got[:8]), add(pieces[8:16], got[8:])
    got = send(away, SECOND)
    keep, away = add(keep[:4], got[:4]), add(keep[4:], got[4:])
    got = send(away, FIRST)
    own = keep[0].astype(F32) + got[0].astype(F32)
    total = own
    parts = add(keep[1:], got[1:])
    for k, perm in enumerate(Z_PERMS):
        total = total + send(parts[k], perm).astype(F32)
    return total


def join_cores(core, mine):
    theirs = send(mine, SWAP)
    return jnp.where(core == 0, mine, theirs), jnp.where(core == 0, theirs, mine)


def to_pairs(array):
    width = array.shape[1] // 3
    return jnp.concatenate(
        [array[:, t * width + p : t * width + p + 128] for p in range(0, width, 128) for t in range(3)],
        axis=1,
    )


def from_pairs(array):
    width = array.shape[1] // 3
    return jnp.concatenate(
        [array[:, 3 * p + t * 128 : 3 * p + t * 128 + 128] for t in range(3) for p in range(0, width, 128)],
        axis=1,
    )


def half_of(array, core):
    n = array.shape[1] // 2
    return lax.dynamic_slice_in_dim(array, core * n, n, 1)


def body(
    text_rows,
    slot_ids,
    seg_count,
    w_qkv,
    qv_bias,
    w_out,
    out_bias,
    ln1_gain,
    ln1_shift,
    w_up,
    up_bias,
    w_down,
    down_bias,
    ln2_gain,
    ln2_shift,
    cotangent,
):
    docs, text_len, width = text_rows.shape
    rows = text_len + SLOTS
    core = lax.axis_index("rep")
    shard = lax.axis_index("shard")
    chips = lax.axis_size("shard")
    small = (qv_bias, out_bias, ln1_gain, ln1_shift, up_bias, down_bias, ln2_gain, ln2_shift)
    sizes = [v.shape[0] for v in small]
    starts = [sum(sizes[:i]) for i in range(len(sizes))]
    packed = jnp.concatenate(small)
    staged = chips == CHIPS and lax.axis_size("rep") == 2
    joined = pool(slot_ids, text_rows)
    if staged:
        part = w_qkv.shape[0]
        lines = 640 // 128
        note = jnp.pad(packed, (0, 640 - packed.shape[0])).reshape(lines, 128)
        note = jnp.pad(note, ((0, part - lines), (0, 0)))
        own = [
            lax.dynamic_slice_in_dim(w_qkv, t * width + (2 * g + core) * 128, 128, 1)
            for g in range(GROUPS)
            for t in range(3)
        ]
        qkv = gather(jnp.concatenate(own + [note], axis=1)[None])
        mid = gather(jnp.concatenate([half_of(w_out, core), half_of(w_up, core)], axis=1)[None])
        part = w_down.shape[0] // 2
        down = gather(lax.dynamic_slice_in_dim(w_down, core * part, part, 0)[None])
        place = place_table(core, shard)
        notes = jnp.concatenate([p[:, :lines, 1152:] for p in qkv[:4]], axis=0)
        notes = notes.reshape(CHIPS, lines * 128).astype(F32)
        back = jnp.arange(CHIPS, dtype=jnp.int32)[:, None] == place[0, :CHIPS][None, :]
        table = jnp.dot(back.astype(F32), notes, precision=lax.Precision.HIGHEST)
        down_place = jnp.stack([2 * place[0] + place[1], jnp.zeros_like(place[1])])
    else:
        whole = lambda w: [lax.all_gather(w, "shard", axis=0, tiled=True)[None]]
        qkv, down = whole(to_pairs(w_qkv)), whole(w_down)
        mid = whole(jnp.concatenate([w_out, w_up], axis=1))
        place = down_place = jnp.zeros((2, 1), jnp.int32)
        table = lax.all_gather(packed[None], "shard", axis=0, tiled=True).astype(F32)
    full = [table[:, a : a + n].reshape(1, chips * n) for a, n in zip(starts, sizes)]
    bias_qv, bias_out, gain_one, shift_one, bias_up, bias_down, gain_two, shift_two = full
    full_bias = jnp.concatenate(
        [bias_qv[:, :width], jnp.zeros((1, width), F32), bias_qv[:, width:]], axis=1
    )
    proj, context = attn_fwd(place, seg_count, joined, to_pairs(full_bias), qkv)
    scaled_one, inverse_one, active, slope = up_call(
        place, joined, context, bias_out, gain_one, shift_one, bias_up, mid
    )
    cot = cotangent.reshape(docs * rows, width)
    layer_out, resid_two, sums_two, gw_down = down_call(
        down_place, scaled_one, active, cot, gain_one, shift_one, bias_down, gain_two, shift_two, down
    )
    resid_one, grad_ctx, sums_one, sums_up, gw_mid = ffn_back(
        place, down_place, resid_two, slope, scaled_one, inverse_one, context, gain_one, shift_one, mid, down
    )
    grad_proj, sums_proj, gw_qkv = attn_back(place, seg_count, joined, proj, grad_ctx)
    grad_text = text_grad(place, slot_ids, resid_one, [grad_proj], qkv)

    if staged:
        g_down = jnp.concatenate(join_cores(core, scatter(gw_down)), axis=0)
        low, high = join_cores(core, scatter(gw_mid))
        n = width // 2
        g_out = jnp.concatenate([low[:, :n], high[:, :n]], axis=1)
        g_up = jnp.concatenate([low[:, n:], high[:, n:]], axis=1)
        ends = join_cores(core, scatter(gw_qkv))
        g_qkv = jnp.concatenate(
            [
                ends[p % 2][:, p // 2 * 384 + t * 128 : p // 2 * 384 + t * 128 + 128]
                for t in range(3)
                for p in range(2 * GROUPS)
            ],
            axis=1,
        )
    else:
        spread = lambda g: lax.psum(
            lax.psum_scatter(g[0].astype(F32), "shard", scatter_dimension=0, tiled=True), "rep"
        )
        g_down, g_mid, g_qkv = spread(gw_down), spread(gw_mid), from_pairs(spread(gw_qkv))
        g_out, g_up = g_mid[:, :width], g_mid[:, width:]
    sums_two, sums_one, sums_up = lax.psum((sums_two, sums_one, sums_up), AXES)
    sums_proj = from_pairs(lax.psum(sums_proj, AXES).reshape(1, 3 * width))
    mine = lambda v, n: lax.dynamic_slice_in_dim(v, shard * n, n, 0)
    part = width // chips
    g_bias = jnp.concatenate([sums_proj[0, :width], sums_proj[0, 2 * width :]])
    return (
        layer_out.reshape(docs, rows, width),
        grad_text,
        g_qkv,
        mine(g_bias, 2 * part),
        g_out,
        mine(sums_one[2], part),
        mine(sums_one[0], part),
        mine(sums_one[1], part),
        g_up,
        mine(sums_up[0], up_bias.shape[0]),
        g_down,
        mine(sums_two[2], part),
        mine(sums_two[0], part),
        mine(sums_two[1], part),
    )


def solution(mesh):
    in_specs = (
        P(("rep", "shard"), None, None),
        P(("rep", "shard"), None),
        P(("rep", "shard")),
        P("shard", None),
        P("shard"),
        P("shard", None),
        P("shard"),
        P("shard"),
        P("shard"),
        P("shard", None),
        P("shard"),
        P("shard", None),
        P("shard"),
        P("shard"),
        P("shard"),
        P(("rep", "shard"), None, None),
    )
    out_specs = (
        P(("rep", "shard"), None, None),
        P(("rep", "shard"), None, None),
        P("shard", None),
        P("shard"),
        P("shard", None),
        P("shard"),
        P("shard"),
        P("shard"),
        P("shard", None),
        P("shard"),
        P("shard", None),
        P("shard"),
        P("shard"),
        P("shard"),
    )
    return jax.shard_map(body, mesh=mesh, in_specs=in_specs, out_specs=out_specs, check_vma=False)
```

```python
import math
from functools import partial

import jax
import jax.numpy as jnp
from jax import lax
from jax.experimental import pallas as pl
from jax.experimental.pallas import tpu as pltpu
from jax.sharding import PartitionSpec as P

HEADS = 12
SLOTS = 128
GROUPS = 3
CHIPS = 16
NOTE_ROWS = 16

layer_eps = 1e-05
score_scale = 0.125
masked_score = -1000000000.0
BF = jnp.bfloat16
F32 = jnp.float32
VMEM_LIMIT = 60 * 1024 * 1024

NT = (((1,), (1,)), ((), ()))
NN = (((1,), (0,)), ((), ()))
TN = (((0,), (0,)), ((), ()))

QV, OUT, GAIN1, SHIFT1, UP, DOWN, GAIN2, SHIFT2 = range(8)


def mm(left, right, dims=NN):
    return lax.dot_general(left, right, dims, preferred_element_type=F32)


def call(kernel, name, flops, out_shape, in_specs, out_specs, scratch=(), grid=None):
    shapes = jax.tree.leaves(out_shape)
    moved = sum(math.prod(s.shape) * s.dtype.itemsize for s in shapes)
    return pl.pallas_call(
        kernel,
        out_shape=out_shape,
        grid=(1,) if grid is None else grid,
        in_specs=in_specs,
        out_specs=out_specs,
        scratch_shapes=list(scratch),
        compiler_params=pltpu.CompilerParams(vmem_limit_bytes=VMEM_LIMIT),
        cost_estimate=pl.CostEstimate(flops=int(flops), transcendentals=0, bytes_accessed=2 * moved),
        name=name,
    )


def struct(shape, dtype=BF):
    return jax.ShapeDtypeStruct(shape, dtype)


ANY = pl.BlockSpec(memory_space=pltpu.HBM)
SMEM = pl.BlockSpec(memory_space=pltpu.SMEM)
VMEM = pl.BlockSpec(memory_space=pltpu.VMEM)
DMA = pltpu.SemaphoreType.DMA(())


def halves_of(count):
    return 1 if count == 1 else 2


def place(at, count):
    if count == 1:
        return 0, 0
    other, second, first, far = at // 16, (at // 8) % 2, (at // 4) % 2, at % 4
    half = lax.axis_index("rep") ^ other
    bits = jnp.where(half == 0, second * 2 + first, first * 2 + second)
    return lax.axis_index("shard") ^ (far * 4) ^ bits, half


def aligned(value, by):
    return value if isinstance(value, int) else pl.multiple_of(value, by)


def load_pieces(piece_refs, buf, sem, parts, by_rows=False):
    count = sum(ref.shape[0] for ref in piece_refs)
    whole = 2 // halves_of(count)
    at = 0
    for ref in piece_refs:
        rows = ref.shape[1]
        for i in range(ref.shape[0]):
            chip, half = place(at, count)
            if by_rows:
                chip, half = chip * halves_of(count) + half, 0
            row = aligned(chip * rows, 16)
            for col, n, first in parts:
                if not by_rows:
                    col, n = col * whole, n * whole
                to = aligned(half * n + first, 128)
                pltpu.make_async_copy(
                    ref.at[i, :, pl.ds(col, n)], buf.at[pl.ds(row, rows), pl.ds(to, n)], sem
                ).start()
            at += 1


def wait_all(buf, sem):
    pltpu.make_async_copy(buf, buf, sem).wait()


def count_of(out_refs):
    return sum(ref.shape[0] for ref in out_refs)


def store_pieces(buf, out_refs, sem, n, col, by_rows=False):
    count = count_of(out_refs)
    at = 0
    for ref in out_refs:
        rows = ref.shape[1]
        for i in range(ref.shape[0]):
            chip, half = place(at, count)
            if by_rows:
                chip, half = chip * halves_of(count) + half, 0
            row = aligned(chip * rows, 16)
            pltpu.make_async_copy(
                buf.at[pl.ds(row, rows), pl.ds(aligned(half * n, 128), n)],
                ref.at[i, :, pl.ds(col, n)],
                sem,
            ).start()
            at += 1


def qkv_parts(first, groups):
    return tuple(((first + g) * 384, 384, g * 768) for g in range(groups))


def mid_parts(width, ff):
    return ((0, width // 2, 0), (width // 2, ff // 2, width))


def load_norm(table_ref, row, n):
    return table_ref[row : row + 1, :n]


def note_rows(sizes):
    rows, at = [], 0
    for n in sizes:
        rows.append(at)
        at += -(-n // 128)
    return rows, at


def fill_note(note_ref, index, rows, vectors, chip, sizes):
    for first, vector, n in zip(rows, vectors, sizes):
        for lane in range(0, n, 128):
            m = min(128, n - lane)
            part = vector[:, chip * n + lane : chip * n + lane + m]
            note_ref[index, first + lane // 128 : first + lane // 128 + 1, 0:m] = part.astype(note_ref.dtype)


def send_notes(notes, out_refs, sem):
    at = 0
    for ref in out_refs:
        for i in range(ref.shape[0]):
            chip, _ = place(at, count_of(out_refs))
            pltpu.make_async_copy(
                notes.at[chip], ref.at[i, :, pl.ds(ref.shape[2] - 128, 128)], sem
            ).start()
            at += 1


def wait_notes(notes, out_refs, sem):
    for _ in out_refs:
        pltpu.make_async_copy(notes, notes, sem).wait()


def piece_structs(count, rows, cols):
    halves = halves_of(count)
    return tuple(struct((count // halves, rows, cols)) for _ in range(halves))


def prepare_kernel(sizes, qkv_ref, out_ref, up_ref, down_ref, *refs):
    vectors, (own0, own12, mid, down) = refs[: len(sizes)], refs[len(sizes) :]
    core = lax.axis_index("rep")
    width = out_ref.shape[1]
    for g in range(GROUPS):
        for t in range(3):
            cols = pl.ds(pl.multiple_of(t * width + (2 * g + core) * 128, 128), 128)
            if g == 0:
                own0[0, :, t * 128 : (t + 1) * 128] = qkv_ref[:, cols]
            else:
                own12[0, :, (g - 1) * 384 + t * 128 : (g - 1) * 384 + (t + 1) * 128] = qkv_ref[:, cols]
    n = width // 2
    mid[0, :, :n] = out_ref[:, pl.ds(pl.multiple_of(core * n, 128), n)]
    n2 = up_ref.shape[1] // 2
    mid[0, :, n:] = up_ref[:, pl.ds(pl.multiple_of(core * n2, 128), n2)]
    n3 = down_ref.shape[0] // 2
    down[0] = down_ref[pl.ds(pl.multiple_of(core * n3, 16), n3), :]
    own0[0, :, 384:] = jnp.zeros((own0.shape[1], 128), BF)
    rows, _ = note_rows(sizes)
    for first, vector, size in zip(rows, vectors, sizes):
        for lane in range(0, size, 128):
            m = min(128, size - lane)
            own0[0, first + lane // 128 : first + lane // 128 + 1, 384 : 384 + m] = vector[:, lane : lane + m]


def prepare(w_qkv, w_out, w_up, w_down, small):
    rows = w_qkv.shape[0]
    sizes = [v.shape[0] for v in small]
    n = (w_out.shape[1] + w_up.shape[1]) // 2
    return call(
        partial(prepare_kernel, sizes),
        "prepare",
        0,
        (
            struct((1, rows, 512)),
            struct((1, rows, 768)),
            struct((1, rows, n)),
            struct((1, w_down.shape[0] // 2, w_down.shape[1])),
        ),
        [VMEM] * (4 + len(small)),
        (VMEM,) * 4,
    )(w_qkv, w_out, w_up, w_down, *[v.reshape(1, -1) for v in small])


def unpack_kernel(sizes, n_arrays, *refs):
    pieces, (table_ref, notes, sem) = refs[:n_arrays], refs[n_arrays:]
    at = 0
    for ref in pieces:
        for i in range(ref.shape[0]):
            chip, _ = place(at, 2 * CHIPS)
            pltpu.make_async_copy(
                ref.at[i, pl.ds(0, NOTE_ROWS), pl.ds(ref.shape[2] - 128, 128)], notes.at[chip], sem
            ).start()
            at += 1
    wait_all(notes, sem)
    table_ref[...] = jnp.zeros_like(table_ref)
    rows, _ = note_rows(sizes)
    for k, (first, n) in enumerate(zip(rows, sizes)):
        for chip in range(CHIPS):
            for lane in range(0, n, 128):
                m = min(128, n - lane)
                row = first + lane // 128
                table_ref[k : k + 1, chip * n + lane : chip * n + lane + m] = notes[
                    chip, row : row + 1, 0:m
                ].astype(F32)


def unpack(sizes, pieces, width):
    return call(
        partial(unpack_kernel, sizes, len(pieces)),
        "unpack",
        0,
        struct((8, width), F32),
        [ANY] * len(pieces),
        VMEM,
        [pltpu.VMEM((CHIPS, NOTE_ROWS, 128), BF), DMA],
    )(*pieces)


def norm_parts(values):
    average = jnp.mean(values, axis=-1, keepdims=True)
    centred = values - average
    inverse = lax.rsqrt(jnp.mean(centred * centred, axis=-1, keepdims=True) + layer_eps)
    return centred * inverse, inverse


def norm_backward(grad_norm, gain_vec, scaled, inverse):
    grad_scaled = grad_norm * gain_vec
    grad_mean = jnp.mean(grad_scaled, axis=-1, keepdims=True)
    second = jnp.mean(grad_scaled * scaled, axis=-1, keepdims=True)
    return inverse * (grad_scaled - grad_mean - scaled * second)


def fold_rows(values):
    rows, cols = values.shape
    return jnp.sum(values.reshape(rows // 8, 8, cols), axis=0)


def one_hot_of(ids_row, dtype):
    slot = lax.broadcasted_iota(jnp.int32, (SLOTS, ids_row.shape[1]), 0)
    return jnp.where(slot == ids_row, 1.0, 0.0).astype(dtype)


def divisor_of(ids_row):
    members = jnp.sum(one_hot_of(ids_row, F32), axis=1, keepdims=True)
    return jnp.sqrt(jnp.maximum(members, 1.0))


def pool_kernel(ids_ref, text_ref, joined_ref):
    text_len = text_ref.shape[1]
    ids_row = ids_ref[pl.ds(pl.program_id(0), 1), :]
    summed = mm(one_hot_of(ids_row, BF), text_ref[0])
    joined_ref[0:text_len, :] = text_ref[0]
    joined_ref[text_len:, :] = (summed / divisor_of(ids_row)).astype(BF)


def pool(slot_ids, text_rows):
    docs, text_len, width = text_rows.shape
    rows = text_len + SLOTS
    return call(
        pool_kernel,
        "pool",
        2 * docs * SLOTS * text_len * width,
        struct((docs * rows, width)),
        [VMEM, pl.BlockSpec((1, text_len, width), lambda d: (d, 0, 0))],
        pl.BlockSpec((rows, width), lambda d: (d, 0)),
        grid=(docs,),
    )(slot_ids, text_rows)


def head_mask(e, width=128, size=64):
    lane = lax.broadcasted_iota(jnp.int32, (1, width), 1)
    return (lane // size) == e


def mask_keys(scores, count, text_len):
    slot = lax.broadcasted_iota(jnp.int32, (1, SLOTS), 1)
    tail = jnp.where(slot < count, scores[:, text_len:], masked_score)
    return jnp.concatenate([scores[:, :text_len], tail], axis=1)


def attn_fwd_kernel(docs, rows, group, inside, n_arrays, count_ref, joined_ref, table_ref, *refs):
    pieces = refs[:n_arrays]
    proj_ref, ctx_ref, wbuf, sem = refs[n_arrays:]
    width = joined_ref.shape[1]
    span = width // GROUPS
    load_pieces(pieces, wbuf, sem, qkv_parts(inside, 1))
    bias = []
    for lo in range(group * span, (group + 1) * span, 128):
        bias += [
            table_ref[QV : QV + 1, lo : lo + 128],
            jnp.zeros((1, 128), F32),
            table_ref[QV : QV + 1, width + lo : width + lo + 128],
        ]
    bias = jnp.concatenate(bias, axis=1)
    wait_all(wbuf, sem)
    proj_ref[...] = (mm(joined_ref[...], wbuf[...]) + bias).astype(BF)

    def doc_step(d, carry):
        at = pl.ds(pl.multiple_of(d * rows, 128), rows)
        count = count_ref[d]
        for lo in range(0, span, 128):
            first = 3 * lo
            queries = proj_ref[at, first : first + 128] * BF(score_scale)
            keys = proj_ref[at, first + 128 : first + 256]
            values = proj_ref[at, first + 256 : first + 384]
            total = None
            for e in range(2):
                mask = head_mask(e)
                scores = mm(jnp.where(mask, queries, BF(0)), keys, NT)
                scores = mask_keys(scores, count, rows - SLOTS)
                top = jnp.max(scores, axis=1, keepdims=True)
                weights = jnp.exp(scores - top)
                norm = 1.0 / jnp.sum(weights, axis=1, keepdims=True)
                probs = (weights * norm).astype(BF)
                part = mm(probs, jnp.where(mask, values, BF(0)))
                total = part if total is None else total + part
            ctx_ref[at, lo : lo + 128] = total.astype(BF)
        return carry

    lax.fori_loop(0, docs, doc_step, 0)


def attn_fwd(group, inside, seg_count, joined, table, pieces):
    docs = seg_count.shape[0]
    total, width = joined.shape
    rows = total // docs
    span = width // GROUPS
    return call(
        partial(attn_fwd_kernel, docs, rows, group, inside, len(pieces)),
        "attn_fwd",
        2 * total * width * width + 8 * total * rows * span,
        (struct((total, width)), struct((total, span))),
        [SMEM, VMEM, VMEM] + [ANY] * len(pieces),
        (VMEM, VMEM),
        [pltpu.VMEM((width, width), BF), DMA],
    )(seg_count, joined, table, *pieces)


def up_kernel(n_arrays, joined_ref, ctx0, ctx1, ctx2, table_ref, *refs):
    pieces = refs[:n_arrays]
    scaled_ref, inv_ref, low_ref, act_ref, slope_ref, wbuf, sem = refs[n_arrays:]
    width = joined_ref.shape[1]
    ff = act_ref.shape[1]

    @pl.when(pl.program_id(0) == 0)
    def _():
        load_pieces(pieces, wbuf, sem, mid_parts(width, ff))
        wait_all(wbuf, sem)

    ctx = jnp.concatenate([ctx0[...], ctx1[...], ctx2[...]], axis=1)
    branch = mm(ctx, wbuf[:, :width]) + load_norm(table_ref, OUT, width)
    scaled, inverse = norm_parts(joined_ref[...].astype(F32) + branch)
    scaled_ref[...] = scaled
    inv_ref[...] = inverse
    low = (scaled * load_norm(table_ref, GAIN1, width) + load_norm(table_ref, SHIFT1, width)).astype(BF)
    low_ref[...] = low
    step = 768
    for c in range(0, ff, step):
        up = mm(low, wbuf[:, width + c : width + c + step]) + table_ref[UP : UP + 1, c : c + step]
        half = 0.5 + 0.5 * lax.erf(up * math.sqrt(0.5))
        act_ref[:, c : c + step] = (up * half).astype(BF)
        slope_ref[:, c : c + step] = half + up * (
            jnp.exp(-0.5 * (up * up)) * (1.0 / math.sqrt(2.0 * math.pi))
        )


def up_call(joined, ctx, table, pieces, ff, block=256):
    total, width = joined.shape
    row = lambda i: (i, 0)
    wide = lambda n: pl.BlockSpec((block, n), row)
    return call(
        partial(up_kernel, len(pieces)),
        "up",
        2 * total * width * (width + ff),
        (
            struct((total, width), F32),
            struct((total, 1), F32),
            struct((total, width)),
            struct((total, ff)),
            struct((total, ff), F32),
        ),
        [wide(width)] + [wide(width // GROUPS)] * 3 + [VMEM] + [ANY] * len(pieces),
        (wide(width), wide(1), wide(width), wide(ff), wide(ff)),
        [pltpu.VMEM((width, width + ff), BF), DMA],
        (total // block,),
    )(joined, *ctx, table, *pieces)


def put_sums(acc, sums_ref):
    sums_ref[...] = jnp.zeros_like(sums_ref)
    for i in range(acc.shape[0]):
        sums_ref[i : i + 1, :] = jnp.sum(acc[i], axis=0, keepdims=True)


def down_kernel(n_arrays, n_out, n_rows, n_cols, scaled_ref, act_ref, cot_ref, table_ref, *refs):
    pieces = refs[:n_arrays]
    out_ref, resid_ref, sums_ref = refs[n_arrays : n_arrays + 3]
    gw_refs = refs[n_arrays + 3 : n_arrays + 3 + n_out]
    wbuf, low_buf, gbuf, acc, sem, osem = refs[n_arrays + 3 + n_out :]
    step = pl.program_id(0)
    block, width = cot_ref.shape
    ff = wbuf.shape[0]
    tile = ff // n_cols
    vec = lambda row: load_norm(table_ref, row, width)

    @pl.when(step == 0)
    def _():
        load_pieces(pieces, wbuf, sem, ((0, width, 0),), by_rows=True)
        acc[...] = jnp.zeros_like(acc)
        wait_all(wbuf, sem)

    @pl.when(step < n_rows)
    def _():
        at = pl.ds(pl.multiple_of(step * block, block), block)
        down = mm(act_ref[at, :], wbuf[...]) + vec(DOWN)
        normed1 = scaled_ref[...] * vec(GAIN1) + vec(SHIFT1)
        scaled2, inverse2 = norm_parts(normed1 + down)
        out_ref[...] = (scaled2 * vec(GAIN2) + vec(SHIFT2)).astype(BF)
        grad = cot_ref[...].astype(F32)
        resid = norm_backward(grad, vec(GAIN2), scaled2, inverse2)
        resid_ref[...] = resid
        low = resid.astype(BF)
        low_buf[at, :] = low
        acc[0] += fold_rows(grad * scaled2)
        acc[1] += fold_rows(grad)
        acc[2] += fold_rows(low.astype(F32))

    @pl.when(step >= n_rows)
    def _():
        c = step - n_rows
        cols = pl.ds(pl.multiple_of(c * tile, 128), tile)
        gbuf[cols, :] = mm(act_ref[:, cols], low_buf[...], TN).astype(BF)

    @pl.when(step == n_rows + n_cols - 1)
    def _():
        store_pieces(gbuf, gw_refs, osem, width, 0, by_rows=True)
        put_sums(acc, sums_ref)
        wait_all(gbuf, osem)


def down_call(scaled1, act, cot, table, pieces, block=256, tile=384):
    total, width = scaled1.shape
    ff = act.shape[1]
    n_rows, n_cols = total // block, ff // tile
    row = lambda i: (jnp.minimum(i, n_rows - 1), 0)
    count = sum(p.shape[0] for p in pieces)
    wide = pl.BlockSpec((block, width), row)
    gw = piece_structs(count, ff // count, width)
    out, resid, sums, *gw = call(
        partial(down_kernel, len(pieces), len(gw), n_rows, n_cols),
        "down",
        4 * total * width * ff,
        (
            struct((total, width)),
            struct((total, width), F32),
            struct((8, width), F32),
        )
        + gw,
        [wide, VMEM, wide, VMEM] + [ANY] * len(pieces),
        (wide, wide, pl.BlockSpec((8, width), lambda i: (0, 0))) + (ANY,) * len(gw),
        [
            pltpu.VMEM((ff, width), BF),
            pltpu.VMEM((total, width), BF),
            pltpu.VMEM((ff, width), BF),
            pltpu.VMEM((3, 8, width), F32),
            DMA,
            DMA,
        ],
        (n_rows + n_cols,),
    )(scaled1, act, cot, table, *pieces)
    return out, resid, sums, gw


def ffn_kernel(n_up, n_down, n_rows, resid_ref, slope_ref, scaled_ref, inv_ref, table_ref, *refs):
    ups, downs = refs[:n_up], refs[n_up : n_up + n_down]
    resid1_ref, attn_ref, gctx_ref, gup_ref, sums_ref, usum_ref = refs[n_up + n_down : 6 + n_up + n_down]
    wup, wdown, acc, uacc, sem, dsem = refs[6 + n_up + n_down :]
    step = pl.program_id(0)
    width = resid_ref.shape[1]
    ff = wdown.shape[0]
    gain = load_norm(table_ref, GAIN1, width)

    @pl.when(step == 0)
    def _():
        load_pieces(downs, wdown, dsem, ((0, width, 0),), by_rows=True)
        load_pieces(ups, wup, sem, mid_parts(width, ff))
        acc[...] = jnp.zeros_like(acc)
        uacc[...] = jnp.zeros_like(uacc)
        wait_all(wdown, dsem)
        wait_all(wup, sem)

    resid = resid_ref[...]
    gdown = resid.astype(BF)
    chunk = 768
    for c in range(0, ff, chunk):
        gact = mm(gdown, wdown[c : c + chunk, :], NT)
        up = (gact * slope_ref[:, c : c + chunk]).astype(BF)
        gup_ref[:, c : c + chunk] = up
        uacc[:, c : c + chunk] += fold_rows(up.astype(F32))
    gnorm = resid + mm(gup_ref[...], wup[:, width:], NT)
    scaled = scaled_ref[...]
    acc[0] += fold_rows(gnorm * scaled)
    acc[1] += fold_rows(gnorm)
    resid1 = norm_backward(gnorm, gain, scaled, inv_ref[...])
    resid1_ref[...] = resid1
    attn = resid1.astype(BF)
    attn_ref[...] = attn
    acc[2] += fold_rows(attn.astype(F32))
    gctx_ref[...] = mm(attn, wup[:, :width], NT).astype(BF)

    @pl.when(step == n_rows - 1)
    def _():
        put_sums(acc, sums_ref)
        usum_ref[...] = jnp.sum(uacc[...], axis=0, keepdims=True)


def ffn_call(resid2, slope, scaled1, inv1, table, ups, downs, block=256):
    total, width = resid2.shape
    ff = slope.shape[1]
    n_rows = total // block
    row = lambda i: (i, 0)
    wide = lambda n: pl.BlockSpec((block, n), row)
    fixed = lambda *shape: pl.BlockSpec(shape, lambda i: (0, 0))
    return call(
        partial(ffn_kernel, len(ups), len(downs), n_rows),
        "ffn_back",
        2 * total * width * (width + 2 * ff),
        (
            struct((total, width), F32),
            struct((total, width)),
            struct((total, width)),
            struct((total, ff)),
            struct((8, width), F32),
            struct((1, ff), F32),
        ),
        [wide(width), wide(ff), wide(width), wide(1), VMEM] + [ANY] * (len(ups) + len(downs)),
        (wide(width), wide(width), wide(width), wide(ff), fixed(8, width), fixed(1, ff)),
        [
            pltpu.VMEM((width, width + ff), BF),
            pltpu.VMEM((ff, width), BF),
            pltpu.VMEM((3, 8, width), F32),
            pltpu.VMEM((8, ff), F32),
            DMA,
            DMA,
        ],
        (n_rows,),
    )(resid2, slope, scaled1, inv1, table, *ups, *downs)


def mid_grad_kernel(sizes, n_out, n_cols, ctx0, ctx1, ctx2, attn_ref, low_ref, gup_ref, *refs):
    sums, refs = (refs[:3], refs[3:]) if sizes else ((), refs)
    gw_refs, refs = refs[:n_out], refs[n_out:]
    gbuf, osem = refs[:2]
    step = pl.program_id(0)
    width = attn_ref.shape[1]
    halves = len(gw_refs)

    def multiply():
        gbuf[...] = mm(low_ref[...], gup_ref[...], TN).astype(BF)

    def flush(refs, first_half, col):
        rows = refs[0].shape[1]
        for i in range(refs[0].shape[0]):
            for other, ref in enumerate(refs):
                chip, half = place(i + other * refs[0].shape[0], count_of(refs))

                @pl.when(half == first_half)
                def _():
                    pltpu.make_async_copy(
                        gbuf.at[pl.ds(aligned(chip * rows, 16), rows), :],
                        ref.at[i, :, pl.ds(col, width)],
                        osem,
                    ).start()

    @pl.when(step == 0)
    def _():
        for g, ctx in enumerate((ctx0, ctx1, ctx2)):
            n = ctx.shape[1]
            gbuf[g * n : (g + 1) * n, :] = mm(ctx[...], attn_ref[...], TN).astype(BF)
        store_pieces(gbuf, gw_refs, osem, width // halves, 0)
        if sizes:
            notes, nsem = refs[2:]
            sums2_ref, sums1_ref, usum_ref = sums
            notes[...] = jnp.zeros_like(notes)
            vectors = [usum_ref[...]]
            vectors += [ref[i : i + 1, :] for ref in (sums1_ref, sums2_ref) for i in range(3)]
            rows, _ = note_rows(sizes)
            for chip in range(CHIPS):
                fill_note(notes, chip, rows, vectors, chip, sizes)
            send_notes(notes, gw_refs, nsem)
            wait_notes(notes, gw_refs, nsem)
        wait_all(gbuf, osem)

    @pl.when(step > 0)
    def _():
        c = step - 1
        multiply()
        per = n_cols // halves
        at = pl.multiple_of(width // halves + (c % per) * width, 128)
        flush(gw_refs, c // per, at)
        wait_all(gbuf, osem)


def mid_grad(ctx, attn, low, gup, count, sums=()):
    total, width = attn.shape
    ff = gup.shape[1]
    n_cols = ff // width
    halves = halves_of(count)
    sizes = [ff // CHIPS] + [width // CHIPS] * 6 if sums else []
    note = 128 if sums else 0
    scratch = [pltpu.VMEM((width, width), BF), DMA]
    scratch += [pltpu.VMEM((CHIPS, width // CHIPS, 128), BF), DMA] if sums else []
    gw = piece_structs(count, width * halves // count, (width + ff) // halves + note)
    return call(
        partial(mid_grad_kernel, sizes, len(gw), n_cols),
        "mid_grad",
        2 * total * width * (width + ff),
        gw,
        [VMEM] * 5 + [pl.BlockSpec((total, width), lambda i: (0, jnp.maximum(i - 1, 0)))] + [VMEM] * len(sums),
        (ANY,) * len(gw),
        scratch,
        (1 + n_cols,),
    )(*ctx, attn, low, gup, *sums)


def attn_back_kernel(docs, rows, n_sums, n_out, count_ref, joined_ref, proj_ref, gctx_ref, *refs):
    earlier, refs = refs[:n_sums], refs[n_sums:]
    gproj_ref, sums_ref = refs[:2]
    gw_refs, refs = refs[2 : 2 + n_out], refs[2 + n_out :]
    gbuf, osem = refs[:2]
    width = joined_ref.shape[1]
    span = width // GROUPS
    text_len = rows - SLOTS

    def doc_step(d, carry):
        at = pl.ds(pl.multiple_of(d * rows, 128), rows)
        count = count_ref[d]
        slot = lax.broadcasted_iota(jnp.int32, (SLOTS, 1), 0)
        for lo in range(0, span, 128):
            first = 3 * lo
            queries = proj_ref[at, first : first + 128] * BF(score_scale)
            keys = proj_ref[at, first + 128 : first + 256]
            values = proj_ref[at, first + 256 : first + 384]
            grads = gctx_ref[at, lo : lo + 128]
            keys_low = keys * BF(score_scale)
            dq = dk = dv = None
            for e in range(2):
                mask = head_mask(e)
                q_e = jnp.where(mask, queries, BF(0))
                g_e = jnp.where(mask, grads, BF(0))
                k_e = jnp.where(mask, keys_low, BF(0))
                scores = mm(keys, q_e, NT)
                tail = jnp.where(slot < count, scores[text_len:, :], masked_score)
                scores = jnp.concatenate([scores[:text_len, :], tail], axis=0)
                top = jnp.max(scores, axis=0, keepdims=True)
                weights = jnp.exp(scores - top)
                probs = weights * (1.0 / jnp.sum(weights, axis=0, keepdims=True))
                gprobs = mm(values, g_e, NT)
                dot = jnp.sum(probs * gprobs, axis=0, keepdims=True)
                gscores = (probs * (gprobs - dot)).astype(BF)
                dv_e = mm(probs.astype(BF), g_e)
                dk_e = mm(gscores, q_e)
                dq_e = mm(k_e, gscores, TN)
                dq = dq_e if dq is None else dq + dq_e
                dk = dk_e if dk is None else dk + dk_e
                dv = dv_e if dv is None else dv + dv_e
            gproj_ref[at, first : first + 128] = dq.T.astype(BF)
            gproj_ref[at, first + 128 : first + 256] = dk.astype(BF)
            gproj_ref[at, first + 256 : first + 384] = dv.astype(BF)
        return carry

    lax.fori_loop(0, docs, doc_step, 0)
    total = jnp.sum(gproj_ref[...].astype(F32), axis=0, keepdims=True)
    sums_ref[...] = total
    gbuf[...] = mm(joined_ref[...], gproj_ref[...], TN).astype(BF)
    store_pieces(gbuf, gw_refs, osem, width // len(gw_refs), 0)
    if n_sums:
        notes, nsem = refs[2:]
        parts = [ref[...] for ref in earlier] + [total]
        vector = jnp.concatenate(
            [p[:, at + t : at + t + 128] for t in (0, 256) for p in parts for at in range(0, width, 384)],
            axis=1,
        )
        notes[...] = jnp.zeros_like(notes)
        size = 2 * width // CHIPS
        for chip in range(CHIPS):
            notes[chip, 0:1, 0:size] = vector[:, chip * size : (chip + 1) * size].astype(BF)
        send_notes(notes, gw_refs, nsem)
        wait_notes(notes, gw_refs, nsem)
    wait_all(gbuf, osem)


def attn_back(group, seg_count, joined, proj, gctx, count, sums=()):
    docs = seg_count.shape[0]
    total, width = joined.shape
    rows = total // docs
    span = width // GROUPS
    halves = halves_of(count)
    note = 128 if sums else 0
    scratch = [pltpu.VMEM((width, width), BF), DMA]
    scratch += [pltpu.VMEM((CHIPS, width // CHIPS, 128), BF), DMA] if sums else []
    gw = piece_structs(count, width * halves // count, width // halves + note)
    gproj, total_sums, *gw = call(
        partial(attn_back_kernel, docs, rows, len(sums), len(gw)),
        "attn_back",
        2 * total * width * width + 20 * total * rows * span,
        (
            struct((total, width)),
            struct((1, width), F32),
        )
        + gw,
        [SMEM, VMEM, VMEM, pl.BlockSpec((total, span), lambda i: (0, group))] + [VMEM] * len(sums),
        (VMEM, VMEM) + (ANY,) * len(gw),
        scratch,
    )(seg_count, joined, proj, gctx, *sums)
    return gproj, total_sums, gw


def text_kernel(shape, ids_ref, resid_ref, *refs):
    grads = refs[:GROUPS]
    sets, refs = [], refs[GROUPS:]
    for n_arrays in shape:
        sets.append(refs[:n_arrays])
        refs = refs[n_arrays:]
    out_ref, sem = refs[0], refs[-1]
    bufs = refs[1:-1]
    width = resid_ref.shape[1]
    text_len = out_ref.shape[1]

    @pl.when(pl.program_id(0) == 0)
    def _():
        for pieces, buf in zip(sets, bufs):
            load_pieces(pieces, buf, sem, qkv_parts(0, buf.shape[1] // width))
            wait_all(buf, sem)

    total = resid_ref[...]
    g = 0
    for buf in bufs:
        for i in range(buf.shape[1] // width):
            total = total + mm(grads[g][...], buf[:, i * width : (i + 1) * width], NT)
            g += 1
    ids_row = ids_ref[pl.ds(pl.program_id(0), 1), :]
    summed = (total[text_len:, :] / divisor_of(ids_row)).astype(BF)
    out_ref[0] = total[:text_len, :] + mm(one_hot_of(ids_row, BF), summed, TN)


def text_grad(slot_ids, resid1, grads, sets):
    docs, text_len = slot_ids.shape
    total, width = resid1.shape
    rows = total // docs
    row = pl.BlockSpec((rows, width), lambda d: (d, 0))
    return call(
        partial(text_kernel, [len(pieces) for pieces, _ in sets]),
        "text_grad",
        6 * total * width * width,
        struct((docs, text_len, width), F32),
        [VMEM, row] + [row] * len(grads) + [ANY] * sum(len(pieces) for pieces, _ in sets),
        pl.BlockSpec((1, text_len, width), lambda d: (d, 0, 0)),
        [pltpu.VMEM((width, groups * width), BF) for _, groups in sets] + [DMA],
        (docs,),
    )(slot_ids, resid1, *grads, *[piece for pieces, _ in sets for piece in pieces])


AXES = ("rep", "shard")


def flips(core):
    return (1, 2) if core == 0 else (2, 1)


def pairs(flip_of):
    return [
        (core * CHIPS + s, core * CHIPS + (s ^ flip_of(core)))
        for core in range(2)
        for s in range(CHIPS)
    ]


Z_PERMS = [pairs(lambda core, k=k: k << 2) for k in (1, 2, 3)]
FIRST = pairs(lambda core: flips(core)[0])
SECOND = pairs(lambda core: flips(core)[1])
SWAP = [(core * CHIPS + s, (1 - core) * CHIPS + s) for core in range(2) for s in range(CHIPS)]


def send(array, perm):
    return lax.ppermute(array, AXES, perm)


def after(value, *earlier):
    return lax.optimization_barrier((value, *earlier))[0] if earlier else value


def add(left, right):
    return (left.astype(F32) + right.astype(F32)).astype(BF)


class Gather:
    def __init__(self, own):
        self.own = own

    def far(self, *earlier):
        self.own = after(self.own, *earlier)
        self.got = [send(self.own, perm) for perm in Z_PERMS]

    def first(self, *earlier):
        self.column = jnp.concatenate([self.own] + [after(part, *earlier) for part in self.got], axis=0)
        self.got = send(self.column, FIRST)
        self.swapped = [send(self.column, SWAP)]

    def second(self, *earlier):
        self.near = after(self.got, *earlier)
        self.got = [send(self.column, SECOND), send(self.near, SECOND)]
        self.swapped += [send(self.near, SWAP)]

    def swap(self, *earlier):
        self.got = [after(part, *earlier) for part in self.got]
        self.swapped += [send(part, SWAP) for part in self.got]
        self.all = [self.column, self.near] + self.got + self.swapped


class Scatter:
    def __init__(self):
        self.arrays, self.got = [], []

    def swap(self, pair):
        self.arrays.append(pair[0])
        self.got.append(send(pair[1], SWAP))

    def second(self, *earlier):
        both = [(kept, after(got, *earlier)) for kept, got in zip(self.arrays, self.got)]
        joined = lambda parts: parts[0] if len(parts) == 1 else jnp.concatenate(parts, axis=2)
        self.away = joined([add(p[8:], g[8:]) for p, g in both])
        self.keep = joined([add(p[:8], g[:8]) for p, g in both])
        self.got = send(self.away, SECOND)

    def first(self, *earlier):
        got = after(self.got, *earlier)
        self.away = add(self.keep[4:], got[4:])
        self.keep = add(self.keep[:4], got[:4])
        self.got = send(self.away, FIRST)

    def far(self, *earlier):
        got = after(self.got, *earlier)
        self.away = [add(self.keep[k], got[k]) for k in (1, 2, 3)]
        self.own = self.keep[0].astype(F32) + got[0].astype(F32)
        self.got = [send(part, perm) for part, perm in zip(self.away, Z_PERMS)]

    def total(self, *earlier):
        self.mine = self.own
        for part in self.got:
            self.mine = self.mine + after(part, *earlier).astype(F32)
        self.theirs = send(self.mine, SWAP)


def to_pairs(array):
    width = array.shape[1] // 3
    return jnp.concatenate(
        [array[:, t * width + p : t * width + p + 128] for p in range(0, width, 128) for t in range(3)],
        axis=1,
    )


def from_pairs(array):
    width = array.shape[1] // 3
    return jnp.concatenate(
        [array[:, 3 * p + t * 128 : 3 * p + t * 128 + 128] for t in range(3) for p in range(0, width, 128)],
        axis=1,
    )


def finish_mid_kernel(sizes, mine_ref, theirs_ref, out_ref, up_ref, *vector_refs):
    core = lax.axis_index("rep")
    n = out_ref.shape[1] // 2
    m = up_ref.shape[1] // 2
    for ref, half in ((mine_ref, core), (theirs_ref, 1 - core)):
        out_ref[:, pl.ds(pl.multiple_of(half * n, 128), n)] = ref[:, :n]
        up_ref[:, pl.ds(pl.multiple_of(half * m, 128), m)] = ref[:, n : n + m]
    rows, total = note_rows(sizes)
    note = jnp.where(core == 0, mine_ref[0:NOTE_ROWS, n + m :], theirs_ref[0:NOTE_ROWS, n + m :])
    for first, size, ref in zip(rows, sizes, vector_refs):
        for lane in range(0, size, 128):
            k = min(128, size - lane)
            ref[0:1, lane : lane + k] = note[first + lane // 128 : first + lane // 128 + 1, 0:k]


def finish_mid(mine, theirs, width, ff):
    rows = mine.shape[0]
    sizes = [ff // CHIPS] + [width // CHIPS] * 6
    return call(
        partial(finish_mid_kernel, sizes),
        "finish_mid",
        0,
        (struct((rows, width), F32), struct((rows, ff), F32)) + tuple(struct((1, n), F32) for n in sizes),
        [VMEM, VMEM],
        (VMEM,) * (2 + len(sizes)),
    )(mine, theirs)


def finish_qkv_kernel(groups, *refs):
    pairs_of = [(refs[2 * i], refs[2 * i + 1]) for i in range(len(groups))]
    out_ref, bias_ref = refs[2 * len(groups) :]
    core = lax.axis_index("rep")
    width = out_ref.shape[1] // 3
    g = 0
    for n, (mine_ref, theirs_ref) in zip(groups, pairs_of):
        for i in range(n):
            for ref, half in ((mine_ref, core), (theirs_ref, 1 - core)):
                for t in range(3):
                    to = pl.ds(pl.multiple_of(t * width + (2 * g + half) * 128, 128), 128)
                    out_ref[:, to] = ref[:, i * 384 + t * 128 : i * 384 + (t + 1) * 128]
            g += 1
    mine_ref, theirs_ref = pairs_of[-1]
    k = bias_ref.shape[1]
    at = mine_ref.shape[1] - 128
    bias_ref[...] = jnp.where(core == 0, mine_ref[0:1, at : at + k], theirs_ref[0:1, at : at + k])


def finish_qkv(parts, groups, width):
    rows = parts[0].shape[0]
    return call(
        partial(finish_qkv_kernel, groups),
        "finish_qkv",
        0,
        (struct((rows, 3 * width), F32), struct((1, 2 * width // CHIPS), F32)),
        [VMEM] * len(parts),
        (VMEM, VMEM),
    )(*parts)


def body(
    text_rows,
    slot_ids,
    seg_count,
    w_qkv,
    qv_bias,
    w_out,
    out_bias,
    ln1_gain,
    ln1_shift,
    w_up,
    up_bias,
    w_down,
    down_bias,
    ln2_gain,
    ln2_shift,
    cotangent,
):
    docs, text_len, width = text_rows.shape
    rows = text_len + SLOTS
    ff = w_up.shape[1]
    chips = lax.axis_size("shard")
    small = (qv_bias, out_bias, ln1_gain, ln1_shift, up_bias, down_bias, ln2_gain, ln2_shift)
    sizes = [v.shape[0] for v in small]
    cot = cotangent.reshape(docs * rows, width)
    if chips != CHIPS or lax.axis_size("rep") != 2:
        return plain(text_rows, slot_ids, seg_count, w_qkv, w_out, w_up, w_down, small, cot)

    core = lax.axis_index("rep")
    own_q0, own_q12, own_mid, own_down = prepare(w_qkv, w_out, w_up, w_down, small)
    q0, q12, mid, down = Gather(own_q0), Gather(own_q12), Gather(own_mid), Gather(own_down)
    q0.far()
    joined = pool(slot_ids, text_rows)
    q0.first(joined)
    q12.far(q0.column)
    q0.second()
    q12.first(q0.near)
    q0.swap()
    table = unpack(sizes, [q0.column, q0.near] + q0.got, ff)
    mid.far(q12.column)
    q12.second(q0.got[1])
    proj0, ctx0 = attn_fwd(0, 0, seg_count, after(joined, q12.near), table, q0.all)
    q12.swap(ctx0)
    mid.first(ctx0)
    down.far(ctx0)
    proj1, ctx1 = attn_fwd(1, 0, seg_count, after(joined, ctx0, mid.column), table, q12.all)
    mid.second(ctx1)
    down.first(ctx1)
    proj2, ctx2 = attn_fwd(2, 1, seg_count, after(joined, ctx1, mid.near, down.column), table, q12.all)
    mid.swap(ctx2)
    down.second(ctx2)
    ctx = (ctx0, ctx1, ctx2)
    scaled_one, inverse_one, low, active, slope = up_call(after(joined, down.near), ctx, table, mid.all, ff)
    down.swap(active)
    layer_out, resid_two, sums_two, gw_down = down_call(scaled_one, active, cot, table, down.all)

    s_down, s_mid, s_qkv = Scatter(), Scatter(), Scatter()
    s_down.swap(gw_down)
    resid_one, attn, grad_ctx, grad_up, sums_one, sums_up = ffn_call(
        resid_two, slope, scaled_one, inverse_one, table, mid.all, down.all
    )
    s_down.second(attn)
    gw_mid = mid_grad(
        ctx, after(attn, s_down.away), low, grad_up, 2 * CHIPS, (sums_two, sums_one, sums_up)
    )
    s_down.first(gw_mid[0])
    s_mid.swap(gw_mid)
    gp0, sp0, gw0 = attn_back(
        0, seg_count, joined, proj0, after(grad_ctx, s_down.away), 2 * CHIPS
    )
    s_down.far(gp0)
    s_mid.second(gp0)
    s_qkv.swap(gw0)
    gp1, sp1, gw1 = attn_back(
        1, seg_count, joined, proj1, after(grad_ctx, gp0, *s_down.away, s_mid.away), 2 * CHIPS
    )
    s_down.total(gp1)
    s_mid.first(gp1)
    s_qkv.swap(gw1)
    gp2, sp2, gw2 = attn_back(
        2, seg_count, joined, proj2, after(grad_ctx, gp1, s_mid.away, s_down.mine), 2 * CHIPS, (sp0, sp1)
    )
    s_mid.far(gp2)
    s_qkv.swap(gw2)
    s_qkv.second()
    grad_text = text_grad(
        slot_ids, after(resid_one, *s_mid.away, s_qkv.away), (gp0, gp1, gp2), ((q0.all, 1), (q12.all, 2))
    )
    s_qkv.first(grad_text)
    s_mid.total(grad_text)
    low_half = jnp.where(core == 0, s_down.mine, s_down.theirs)
    high_half = jnp.where(core == 0, s_down.theirs, s_down.mine)
    g_down = jnp.concatenate([low_half, high_half], axis=0)
    g_out, g_up, *vectors = finish_mid(s_mid.mine, s_mid.theirs, width, ff)
    b_up, b_out, b_gain1, b_shift1, b_down, b_gain2, b_shift2 = [
        vectors[i][0] for i in (0, 3, 1, 2, 6, 4, 5)
    ]
    s_qkv.far()
    s_qkv.total()
    g_qkv, g_bias = finish_qkv([s_qkv.mine, s_qkv.theirs], (3,), width)
    return (
        layer_out.reshape(docs, rows, width),
        grad_text,
        g_qkv,
        g_bias[0],
        g_out,
        b_out,
        b_gain1,
        b_shift1,
        g_up,
        b_up,
        g_down,
        b_down,
        b_gain2,
        b_shift2,
    )


def plain(text_rows, slot_ids, seg_count, w_qkv, w_out, w_up, w_down, small, cot):
    docs, text_len, width = text_rows.shape
    rows = text_len + SLOTS
    ff = w_up.shape[1]
    chips = lax.axis_size("shard")
    shard = lax.axis_index("shard")
    whole = lambda w: [lax.all_gather(w, "shard", axis=0, tiled=True)[None]]
    qkv, down = whole(to_pairs(w_qkv)), whole(w_down)
    mid = whole(jnp.concatenate([w_out, w_up], axis=1))
    sizes = [v.shape[0] for v in small]
    starts = [sum(sizes[:i]) for i in range(len(sizes))]
    notes = lax.all_gather(jnp.concatenate(small)[None], "shard", axis=0, tiled=True).astype(F32)
    full = [notes[:, a : a + n].reshape(1, chips * n) for a, n in zip(starts, sizes)]
    table = jnp.concatenate([jnp.pad(v, ((0, 0), (0, ff - v.shape[1]))) for v in full], axis=0)
    joined = pool(slot_ids, text_rows)
    proj, ctx = zip(*[attn_fwd(g, g, seg_count, joined, table, qkv) for g in range(GROUPS)])
    scaled_one, inverse_one, low, active, slope = up_call(joined, ctx, table, mid, ff)
    layer_out, resid_two, sums_two, gw_down = down_call(scaled_one, active, cot, table, down)
    resid_one, attn, grad_ctx, grad_up, sums_one, sums_up = ffn_call(
        resid_two, slope, scaled_one, inverse_one, table, mid, down
    )
    gw_mid = mid_grad(ctx, attn, low, grad_up, 1)
    back = [attn_back(g, seg_count, joined, proj[g], grad_ctx, 1) for g in range(GROUPS)]
    grad_text = text_grad(slot_ids, resid_one, [b[0] for b in back], ((qkv, GROUPS),))
    spread = lambda g: lax.psum(
        lax.psum_scatter(g.astype(F32), "shard", scatter_dimension=0, tiled=True), "rep"
    )
    g_down, g_mid = spread(gw_down[0][0]), spread(gw_mid[0][0])
    g_qkv = from_pairs(spread(jnp.concatenate([b[2][0][0] for b in back], axis=1)))
    sums_two, sums_one, sums_up = lax.psum((sums_two, sums_one, sums_up), AXES)
    sums_proj = from_pairs(lax.psum(jnp.concatenate([b[1] for b in back], axis=1), AXES))
    mine = lambda v: lax.dynamic_slice_in_dim(v, shard * (v.shape[0] // chips), v.shape[0] // chips, 0)
    return (
        layer_out.reshape(docs, rows, width),
        grad_text,
        g_qkv,
        mine(jnp.concatenate([sums_proj[0, :width], sums_proj[0, 2 * width :]])),
        g_mid[:, :width],
        mine(sums_one[2]),
        mine(sums_one[0]),
        mine(sums_one[1]),
        g_mid[:, width:],
        mine(sums_up[0]),
        g_down,
        mine(sums_two[2]),
        mine(sums_two[0]),
        mine(sums_two[1]),
    )


def solution(mesh):
    in_specs = (
        P(("rep", "shard"), None, None),
        P(("rep", "shard"), None),
        P(("rep", "shard")),
        P("shard", None),
        P("shard"),
        P("shard", None),
        P("shard"),
        P("shard"),
        P("shard"),
        P("shard", None),
        P("shard"),
        P("shard", None),
        P("shard"),
        P("shard"),
        P("shard"),
        P(("rep", "shard"), None, None),
    )
    out_specs = (
        P(("rep", "shard"), None, None),
        P(("rep", "shard"), None, None),
        P("shard", None),
        P("shard"),
        P("shard", None),
        P("shard"),
        P("shard"),
        P("shard"),
        P("shard", None),
        P("shard"),
        P("shard", None),
        P("shard"),
        P("shard"),
        P("shard"),
    )
    return jax.shard_map(body, mesh=mesh, in_specs=in_specs, out_specs=out_specs, check_vma=False)
```

```python
import math
from functools import partial

import jax
import jax.numpy as jnp
from jax import lax
from jax.experimental import pallas as pl
from jax.experimental.pallas import tpu as pltpu
from jax.sharding import PartitionSpec as P

HEADS = 12
SLOTS = 128
GROUPS = 3
CHIPS = 16
NOTE_ROWS = 16

layer_eps = 1e-05
score_scale = 0.125
masked_score = -1000000000.0
BF = jnp.bfloat16
F32 = jnp.float32
MICROSECOND = 1153 * 10**6

NT = (((1,), (1,)), ((), ()))
NN = (((1,), (0,)), ((), ()))
TN = (((0,), (0,)), ((), ()))

QV, OUT, GAIN1, SHIFT1, UP, DOWN, GAIN2, SHIFT2 = range(8)


def mm(left, right, dims=NN):
    return lax.dot_general(left, right, dims, preferred_element_type=F32)


def call(kernel, name, cost, out_shape, in_specs, out_specs, scratch=(), room=12, aliases={}, grid=()):
    held = sum(math.prod(m.shape) * m.dtype.itemsize for m in scratch if m.memory_space == pltpu.VMEM)
    limit = 60 * 2**20 if grid else held + room * 2**20
    shapes = jax.tree.leaves(out_shape)
    moved = sum(math.prod(s.shape) * s.dtype.itemsize for s in shapes)
    return pl.pallas_call(
        kernel,
        out_shape=out_shape,
        grid=grid,
        in_specs=in_specs,
        out_specs=out_specs,
        scratch_shapes=list(scratch),
        input_output_aliases=aliases,
        compiler_params=pltpu.CompilerParams(vmem_limit_bytes=limit),
        cost_estimate=pl.CostEstimate(flops=int(cost), transcendentals=0, bytes_accessed=2 * moved),
        name=name,
    )


def struct(shape, dtype=BF):
    return jax.ShapeDtypeStruct(shape, dtype)


ANY = pl.BlockSpec(memory_space=pl.ANY)
HBM = pl.BlockSpec(memory_space=pltpu.HBM)
SMEM = pl.BlockSpec(memory_space=pltpu.SMEM)
VMEM = pl.BlockSpec(memory_space=pltpu.VMEM)
DMA = pltpu.SemaphoreType.DMA(())


def halves_of(count):
    return 1 if count == 1 else 2


def place(at, count):
    if count == 1:
        return 0, 0
    other, second, first, far = at // 16, (at // 8) % 2, (at // 4) % 2, at % 4
    half = lax.axis_index("rep") ^ other
    bits = jnp.where(half == 0, second * 2 + first, first * 2 + second)
    return lax.axis_index("shard") ^ (far * 4) ^ bits, half


def aligned(value, by):
    return value if isinstance(value, int) else pl.multiple_of(value, by)


def load_pieces(piece_refs, buf, sem, parts, by_rows=False):
    count = sum(ref.shape[0] for ref in piece_refs)
    whole = 2 // halves_of(count)
    at = 0
    for ref in piece_refs:
        rows = ref.shape[1]
        for i in range(ref.shape[0]):
            chip, half = place(at, count)
            if by_rows:
                chip, half = chip * halves_of(count) + half, 0
            row = aligned(chip * rows, 16)
            for col, n, first in parts:
                if not by_rows:
                    col, n = col * whole, n * whole
                to = aligned(half * n + first, 128)
                pltpu.make_async_copy(
                    ref.at[i, :, pl.ds(col, n)], buf.at[pl.ds(row, rows), pl.ds(to, n)], sem
                ).start()
            at += 1


def fetch(source, target, sem):
    copy = pltpu.make_async_copy(source, target, sem)
    copy.start()
    return copy


def blocks_of(total, block):
    return [pl.ds(first, block) for first in range(0, total, block)]


def sems(n):
    return pltpu.SemaphoreType.DMA((n,))


def slot_of(chip, half):
    apart = lax.axis_index("shard") ^ chip
    far, high, low = apart // 4, (apart // 2) % 2, apart % 2
    return jnp.where(half == 0, high * 8 + low * 4, low * 8 + high * 4) + far


def store_piece(source, out_refs, chip, half, col, sem):
    n = source.shape[1]
    for other, ref in enumerate(out_refs):

        @pl.when(lax.axis_index("rep") ^ half == other)
        def _():
            fetch(source, ref.at[slot_of(chip, half), :, pl.ds(col, n)], sem)


def store_rows(buf, first, rows, out_refs, sem, n):
    if len(out_refs) == 1:
        at = pl.ds(pl.multiple_of(first, 16), rows)
        fetch(buf.at[at, :], out_refs[0].at[0, at, :], sem)
        return
    piece = out_refs[0].shape[1]
    for k in range(0, rows, piece):
        at = pl.ds(pl.multiple_of(first + k, 16), piece)
        for half in range(2):
            source = buf.at[at, pl.ds(half * n, n)]
            store_piece(source, out_refs, (first + k) // piece, half, 0, sem)


def store_row_halves(buf, first, rows, out_refs, sem):
    if len(out_refs) == 1:
        at = pl.ds(pl.multiple_of(first, 16), rows)
        fetch(buf.at[at, :], out_refs[0].at[0, at, :], sem)
        return
    piece = out_refs[0].shape[1]
    for n, k in enumerate(range(0, rows, piece)):
        at = pl.ds(pl.multiple_of(first + k, 16), piece)
        store_piece(buf.at[at, :], out_refs, (first + k) // piece // 2, n % 2, 0, sem)


def rows_at(i, block):
    return pl.ds(pl.multiple_of(i * block, block), block)


def wait_all(buf, sem):
    pltpu.make_async_copy(buf, buf, sem).wait()


def count_of(out_refs):
    return sum(ref.shape[0] for ref in out_refs)


def store_pieces(buf, out_refs, sem, n, col, by_rows=False):
    count = count_of(out_refs)
    at = 0
    for ref in out_refs:
        rows = ref.shape[1]
        for i in range(ref.shape[0]):
            chip, half = place(at, count)
            if by_rows:
                chip, half = chip * halves_of(count) + half, 0
            row = aligned(chip * rows, 16)
            pltpu.make_async_copy(
                buf.at[pl.ds(row, rows), pl.ds(aligned(half * n, 128), n)],
                ref.at[i, :, pl.ds(col, n)],
                sem,
            ).start()
            at += 1


def qkv_parts(first, groups):
    return tuple(((first + g) * 384, 384, g * 768) for g in range(groups))


def mid_parts(width, ff):
    return ((0, width // 2, 0), (width // 2, ff // 2, width))


def load_norm(table_ref, row, n):
    return table_ref[row : row + 1, :n]


def note_rows(sizes):
    rows, at = [], 0
    for n in sizes:
        rows.append(at)
        at += -(-n // 128)
    return rows, at


def fill_note(note_ref, index, rows, vectors, chip, sizes):
    for first, vector, n in zip(rows, vectors, sizes):
        for lane in range(0, n, 128):
            m = min(128, n - lane)
            part = vector[:, chip * n + lane : chip * n + lane + m]
            note_ref[index, first + lane // 128 : first + lane // 128 + 1, 0:m] = part.astype(note_ref.dtype)


def send_notes(notes, out_refs, sem):
    at = 0
    for ref in out_refs:
        for i in range(ref.shape[0]):
            chip, _ = place(at, count_of(out_refs))
            pltpu.make_async_copy(
                notes.at[chip], ref.at[i, :, pl.ds(ref.shape[2] - 128, 128)], sem
            ).start()
            at += 1


def wait_notes(notes, out_refs, sem):
    for _ in out_refs:
        pltpu.make_async_copy(notes, notes, sem).wait()


def piece_structs(count, rows, cols):
    halves = halves_of(count)
    return tuple(struct((count // halves, rows, cols)) for _ in range(halves))


def prepare_kernel(sizes, qkv_ref, out_ref, up_ref, down_ref, *refs):
    vectors, (qkv, mid, down) = refs[: len(sizes)], refs[len(sizes) :]
    core = lax.axis_index("rep")
    width = out_ref.shape[1]
    for g in range(GROUPS):
        for t in range(3):
            cols = pl.ds(pl.multiple_of(t * width + (2 * g + core) * 128, 128), 128)
            qkv[0, :, g * 384 + t * 128 : g * 384 + (t + 1) * 128] = qkv_ref[:, cols]
    n = width // 2
    mid[0, :, :n] = out_ref[:, pl.ds(pl.multiple_of(core * n, 128), n)]
    n2 = up_ref.shape[1] // 2
    mid[0, :, n : n + n2] = up_ref[:, pl.ds(pl.multiple_of(core * n2, 128), n2)]
    n3 = down.shape[1]
    down[0] = down_ref[pl.ds(pl.multiple_of(core * n3, 16), n3), :]
    last = qkv.shape[2] - 128
    qkv[0, :, last:] = jnp.zeros((qkv.shape[1], 128), BF)
    rows, _ = note_rows(sizes)
    for first, vector, size in zip(rows, vectors, sizes):
        for lane in range(0, size, 128):
            m = min(128, size - lane)
            row = first + lane // 128
            qkv[0, row : row + 1, last : last + m] = vector[:, lane : lane + m]


def prepare(w_qkv, w_out, w_up, w_down, small):
    rows = w_qkv.shape[0]
    sizes = [v.shape[0] for v in small]
    half = w_down.shape[0] // 2
    shapes = (
        (1, rows, w_qkv.shape[1] // 2 + 128),
        (1, rows, (w_out.shape[1] + w_up.shape[1]) // 2),
        (1, half, w_down.shape[1]),
    )
    given = (w_qkv, w_out, w_up, w_down, *[v.reshape(1, -1) for v in small])
    whole = lambda shape: pl.BlockSpec(shape, lambda i: (0,) * len(shape))
    return call(
        partial(prepare_kernel, sizes),
        "prepare",
        MICROSECOND,
        tuple(struct(shape) for shape in shapes),
        [whole(v.shape) for v in given],
        tuple(whole(shape) for shape in shapes),
        grid=(1,),
    )(*given)


def unpack_kernel(sizes, n_arrays, *refs):
    pieces, (table_ref, notes, sem) = refs[:n_arrays], refs[n_arrays:]
    at = 0
    for ref in pieces:
        for i in range(ref.shape[0]):
            chip, _ = place(at, 2 * CHIPS)
            pltpu.make_async_copy(
                ref.at[i, pl.ds(0, NOTE_ROWS), pl.ds(ref.shape[2] - 128, 128)], notes.at[chip], sem
            ).start()
            at += 1
    wait_all(notes, sem)
    table_ref[...] = jnp.zeros_like(table_ref)
    rows, _ = note_rows(sizes)
    for k, (first, n) in enumerate(zip(rows, sizes)):
        for chip in range(CHIPS):
            for lane in range(0, n, 128):
                m = min(128, n - lane)
                row = first + lane // 128
                table_ref[k : k + 1, chip * n + lane : chip * n + lane + m] = notes[
                    chip, row : row + 1, 0:m
                ].astype(F32)


def unpack(sizes, pieces, width):
    return call(
        partial(unpack_kernel, sizes, len(pieces)),
        "unpack",
        0,
        struct((8, width), F32),
        [HBM] * len(pieces),
        VMEM,
        [pltpu.VMEM((CHIPS, NOTE_ROWS, 128), BF), DMA],
    )(*pieces)


def norm_parts(values):
    average = jnp.mean(values, axis=-1, keepdims=True)
    centred = values - average
    inverse = lax.rsqrt(jnp.mean(centred * centred, axis=-1, keepdims=True) + layer_eps)
    return centred * inverse, inverse


def norm_backward(grad_norm, gain_vec, scaled, inverse):
    grad_scaled = grad_norm * gain_vec
    grad_mean = jnp.mean(grad_scaled, axis=-1, keepdims=True)
    second = jnp.mean(grad_scaled * scaled, axis=-1, keepdims=True)
    return inverse * (grad_scaled - grad_mean - scaled * second)


def fold_rows(values):
    rows, cols = values.shape
    return jnp.sum(values.reshape(rows // 8, 8, cols), axis=0)


def one_hot_of(ids_row, dtype):
    slot = lax.broadcasted_iota(jnp.int32, (SLOTS, ids_row.shape[1]), 0)
    return jnp.where(slot == ids_row, 1.0, 0.0).astype(dtype)


def divisor_of(ids_row):
    members = jnp.sum(one_hot_of(ids_row, F32), axis=1, keepdims=True)
    return jnp.sqrt(jnp.maximum(members, 1.0))


def pool_kernel(ids_ref, text_ref, joined_ref):
    text_len = text_ref.shape[1]
    ids_row = ids_ref[pl.ds(pl.program_id(0), 1), :]
    summed = mm(one_hot_of(ids_row, BF), text_ref[0])
    joined_ref[0:text_len, :] = text_ref[0]
    joined_ref[text_len:, :] = (summed / divisor_of(ids_row)).astype(BF)


def pool(slot_ids, text_rows):
    docs, text_len, width = text_rows.shape
    rows = text_len + SLOTS
    return call(
        pool_kernel,
        "pool",
        3 * MICROSECOND,
        struct((docs * rows, width)),
        [VMEM, pl.BlockSpec((1, text_len, width), lambda d: (d, 0, 0))],
        pl.BlockSpec((rows, width), lambda d: (d, 0)),
        grid=(docs,),
    )(slot_ids, text_rows)


QUERIES = 128


def both_heads(rows):
    first = lax.broadcasted_iota(jnp.int32, (1, 128), 1) < 64
    zero = BF(0)
    return jnp.concatenate([jnp.where(first, rows, zero), jnp.where(first, zero, rows)], axis=0)


def own_lanes(product):
    n = product.shape[1] // 2
    first = lax.broadcasted_iota(jnp.int32, (128, 1), 0) < 64
    return jnp.where(first, product[:, :n], product[:, n:])


def masked(scores, count, text_len):
    slot = lax.broadcasted_iota(jnp.int32, (SLOTS, 1), 0)
    tail = jnp.where(slot < count, scores[text_len:, :], masked_score)
    return jnp.concatenate([scores[:text_len, :], tail], axis=0)


def attn_fwd_kernel(docs, rows, group, inside, n_arrays, count_ref, joined_ref, table_ref, *refs):
    pieces = refs[:n_arrays]
    proj_ref, ctx_ref, lse_ref, wbuf, probs_buf, sem = refs[n_arrays:]
    width = joined_ref.shape[1]
    span = width // GROUPS
    load_pieces(pieces, wbuf, sem, qkv_parts(inside, 1))
    bias = []
    for lo in range(group * span, (group + 1) * span, 128):
        bias += [
            table_ref[QV : QV + 1, lo : lo + 128],
            jnp.zeros((1, 128), F32),
            table_ref[QV : QV + 1, width + lo : width + lo + 128],
        ]
    bias = jnp.concatenate(bias, axis=1)
    wait_all(wbuf, sem)
    proj_ref[...] = (mm(joined_ref[...], wbuf[...]) + bias).astype(BF)

    def doc_step(d, carry):
        base = pl.multiple_of(d * rows, 128)
        at = pl.ds(base, rows)
        count = count_ref[d]
        for lo in range(0, span, 128):
            first = 3 * lo
            keys = proj_ref[at, first + 128 : first + 256]
            values = proj_ref[at, first + 256 : first + 384]
            tops = []
            for block in range(0, rows, QUERIES):
                here = pl.ds(pl.multiple_of(base + block, 128), QUERIES)
                queries = both_heads(proj_ref[here, first : first + 128] * BF(score_scale))
                scores = masked(mm(keys, queries, NT), count, rows - SLOTS)
                top = jnp.max(scores, axis=0, keepdims=True)
                weights = jnp.exp(scores - top)
                total = jnp.sum(weights, axis=0, keepdims=True)
                cols = slice(2 * block, 2 * block + 2 * QUERIES)
                probs_buf[lo // 128, :, cols] = (weights * (1.0 / total)).astype(BF)
                tops.append(top + jnp.log(total))
            lse_ref[d, lo // 128] = jnp.concatenate(tops, axis=1)
            context = mm(values.T, probs_buf[lo // 128])
            for block in range(0, rows, QUERIES):
                here = pl.ds(pl.multiple_of(base + block, 128), QUERIES)
                part = own_lanes(context[:, 2 * block : 2 * block + 2 * QUERIES])
                ctx_ref[here, lo : lo + 128] = part.T.astype(BF)
        return carry

    lax.fori_loop(0, docs, doc_step, 0)


def attn_fwd(group, inside, seg_count, joined, table, pieces):
    docs = seg_count.shape[0]
    total, width = joined.shape
    rows = total // docs
    span = width // GROUPS
    return call(
        partial(attn_fwd_kernel, docs, rows, group, inside, len(pieces)),
        "attn_fwd",
        10 * MICROSECOND,
        (
            struct((total, width)),
            struct((total, span)),
            struct((docs, span // 128, 1, 2 * rows), F32),
        ),
        [SMEM, VMEM, VMEM] + [HBM] * len(pieces),
        (VMEM,) * 3,
        [pltpu.VMEM((width, width), BF), pltpu.VMEM((span // 128, rows, 2 * rows), BF), DMA],
    )(seg_count, joined, table, *pieces)


def load_mid(pieces, wmid, sem):
    width = wmid.shape[0]
    load_pieces(pieces, wmid, sem, mid_parts(width, wmid.shape[1] - width))


def load_down(pieces, wdown, sem):
    load_pieces(pieces, wdown, sem, ((0, wdown.shape[1], 0),), by_rows=True)


def forward_kernel(n_mid, n_down, n_out, n_rows, n_cols, joined_ref, ctx0, ctx1, ctx2, cot_ref, table_ref, *refs):
    pieces, downs, refs = refs[:n_mid], refs[n_mid : n_mid + n_down], refs[n_mid + n_down :]
    scaled_ref, inv_ref, low_ref, slope_ref, out_ref, resid_ref, sums_ref = refs[:7]
    gw_refs, refs = refs[7 : 7 + n_out], refs[7 + n_out :]
    wmid, wdown, act, low_buf, gbuf, acc, sem, down_sem, gw_sem = refs
    step = pl.program_id(0)
    block, width = joined_ref.shape
    ff = wdown.shape[0]
    tile = ff // n_cols
    chunk = 768
    vec = lambda row: load_norm(table_ref, row, width)

    @pl.when(step == 0)
    def _():
        load_mid(pieces, wmid, sem)
        load_down(downs, wdown, down_sem)
        acc[...] = jnp.zeros_like(acc)
        wait_all(wmid, sem)
        wait_all(wdown, down_sem)

    @pl.when(step < n_rows)
    def _():
        at = rows_at(step, block)
        ctx = jnp.concatenate([ctx0[...], ctx1[...], ctx2[...]], axis=1)
        branch = mm(ctx, wmid[:, :width]) + vec(OUT)
        scaled, inverse = norm_parts(joined_ref[...].astype(F32) + branch)
        scaled_ref[...] = scaled
        inv_ref[...] = inverse
        normed1 = scaled * vec(GAIN1) + vec(SHIFT1)
        low = normed1.astype(BF)
        low_ref[...] = low
        down = vec(DOWN)
        for c in range(0, ff, chunk):
            cols = slice(c, c + chunk)
            up = mm(low, wmid[:, width + c : width + c + chunk]) + table_ref[UP : UP + 1, cols]
            half = 0.5 + 0.5 * lax.erf(up * math.sqrt(0.5))
            slope_ref[:, cols] = half + up * (
                jnp.exp(-0.5 * (up * up)) * (1.0 / math.sqrt(2.0 * math.pi))
            )
            active = (up * half).astype(BF)
            act[at, cols] = active
            down = down + mm(active, wdown[cols, :])
        scaled2, inverse2 = norm_parts(normed1 + down)
        out_ref[...] = (scaled2 * vec(GAIN2) + vec(SHIFT2)).astype(BF)
        grad = cot_ref[...].astype(F32)
        resid = norm_backward(grad, vec(GAIN2), scaled2, inverse2)
        resid_ref[...] = resid
        rounded = resid.astype(BF)
        low_buf[at, :] = rounded
        acc[0] += fold_rows(grad * scaled2)
        acc[1] += fold_rows(grad)
        acc[2] += fold_rows(rounded.astype(F32))

    @pl.when(step >= n_rows)
    def _():
        c = step - n_rows
        at = rows_at(c, tile)
        gbuf[at, :] = mm(act[:, at], low_buf[...], TN).astype(BF)
        store_row_halves(gbuf, c * tile, tile, gw_refs, gw_sem)

    @pl.when(step == n_rows + n_cols - 1)
    def _():
        put_sums([acc[i] for i in range(3)], sums_ref)
        wait_all(gbuf, gw_sem)


def put_sums(sums, sums_ref):
    sums_ref[...] = jnp.zeros_like(sums_ref)
    for i, partial_sums in enumerate(sums):
        sums_ref[i : i + 1, :] = jnp.sum(partial_sums, axis=0, keepdims=True)


def forward_call(joined, ctx, cot, table, pieces, downs, ff, block=256, tile=384):
    total, width = joined.shape
    count = sum(p.shape[0] for p in pieces)
    gw = piece_structs(count, ff // count, width)
    n_rows, n_cols = total // block, ff // tile
    row = lambda i: (jnp.minimum(i, n_rows - 1), 0)
    wide = lambda n: pl.BlockSpec((block, n), row)
    fixed = lambda *shape: pl.BlockSpec(shape, lambda i: (0, 0))
    scaled, inverse, low, slope, out, resid, sums, *gw = call(
        partial(forward_kernel, len(pieces), len(downs), len(gw), n_rows, n_cols),
        "forward",
        36 * MICROSECOND,
        (
            struct((total, width), F32),
            struct((total, 1), F32),
            struct((total, width)),
            struct((total, ff), F32),
            struct((total, width)),
            struct((total, width), F32),
            struct((8, width), F32),
        )
        + gw,
        [wide(width)] + [wide(width // GROUPS)] * GROUPS + [wide(width), fixed(8, ff)]
        + [HBM] * (len(pieces) + len(downs)),
        (wide(width), wide(1), wide(width), wide(ff), wide(width), wide(width), fixed(8, width))
        + (HBM,) * len(gw),
        [
            pltpu.VMEM((width, width + ff), BF),
            pltpu.VMEM((ff, width), BF),
            pltpu.VMEM((total, ff), BF),
            pltpu.VMEM((total, width), BF),
            pltpu.VMEM((ff, width), BF),
            pltpu.VMEM((3, 8, width), F32),
            DMA,
            DMA,
            DMA,
        ],
        grid=(n_rows + n_cols,),
    )(joined, *ctx, cot, table, *pieces, *downs)
    return scaled, inverse, low, slope, out, resid, sums, gw


def store_tile(buf, out_refs, sem, half, col):
    if len(out_refs) == 1:
        fetch(buf, out_refs[0].at[0, :, pl.ds(col, buf.shape[1])], sem)
        return
    rows = out_refs[0].shape[1]
    for chip in range(buf.shape[0] // rows):
        store_piece(buf.at[pl.ds(chip * rows, rows), :], out_refs, chip, half, col, sem)


def ffn_kernel(n_down, n_rows, resid_ref, slope_ref, *refs):
    downs, (gup_ref, usum_ref, wdown, acc, sem) = refs[:n_down], refs[n_down:]
    step = pl.program_id(0)
    ff = wdown.shape[0]
    chunk = 768

    @pl.when(step == 0)
    def _():
        load_down(downs, wdown, sem)
        acc[...] = jnp.zeros_like(acc)
        wait_all(wdown, sem)

    gdown = resid_ref[...].astype(BF)
    for c in range(0, ff, chunk):
        cols = slice(c, c + chunk)
        up = (mm(gdown, wdown[cols, :], NT) * slope_ref[:, cols]).astype(BF)
        gup_ref[:, cols] = up
        acc[:, cols] += fold_rows(up.astype(F32))

    @pl.when(step == n_rows - 1)
    def _():
        usum_ref[...] = jnp.sum(acc[...], axis=0, keepdims=True)


def ffn_call(resid2, slope, downs, block=256):
    total, width = resid2.shape
    ff = slope.shape[1]
    n_rows = total // block
    wide = lambda n: pl.BlockSpec((block, n), lambda i: (i, 0))
    return call(
        partial(ffn_kernel, len(downs), n_rows),
        "ffn_back",
        13 * MICROSECOND,
        (struct((total, ff)), struct((1, ff), F32)),
        [wide(width), wide(ff)] + [HBM] * len(downs),
        (wide(ff), pl.BlockSpec((1, ff), lambda i: (0, 0))),
        [pltpu.VMEM((ff, width), BF), pltpu.VMEM((8, ff), F32), DMA],
        grid=(n_rows,),
    )(resid2, slope, *downs)


def up_grad_kernel(n_out, low_ref, gup_ref, *refs):
    gw_refs, (buf, sem) = refs[:n_out], refs[n_out:]
    c = pl.program_id(0)
    width = low_ref.shape[1]
    per = pl.num_programs(0) // n_out
    buf[c] = mm(low_ref[...], gup_ref[...], TN).astype(BF)
    store_tile(buf.at[c], gw_refs, sem, c // per, pl.multiple_of((c % per) * width, 128))

    @pl.when(c == pl.num_programs(0) - 1)
    def _():
        wait_all(buf, sem)


def up_grad(low, gup, count):
    total, width = low.shape
    ff = gup.shape[1]
    halves = halves_of(count)
    gw = piece_structs(count, width * halves // count, ff // halves)
    return call(
        partial(up_grad_kernel, len(gw)),
        "up_grad",
        10 * MICROSECOND,
        gw,
        [pl.BlockSpec((total, width), lambda i: (0, 0)), pl.BlockSpec((total, width), lambda i: (0, i))],
        (HBM,) * len(gw),
        [pltpu.VMEM((ff // width, width, width), BF), DMA],
        grid=(ff // width,),
    )(low, gup)


def norm_kernel(sizes, n_mid, n_out, n_rows, resid_ref, gup_ref, scaled_ref, inv_ref, *refs):
    ctxs, table_ref, refs = refs[:GROUPS], refs[GROUPS], refs[GROUPS + 1 :]
    given, refs = (refs[:2], refs[2:]) if sizes else ((), refs)
    pieces, refs = refs[:n_mid], refs[n_mid:]
    resid1_ref, gctx0, gctx1, gctx2, sums_ref = refs[:5]
    gw_refs, refs = refs[5 : 5 + n_out], refs[5 + n_out :]
    wmid, attn, gout, acc, sem, out_sem = refs[:6]
    step = pl.program_id(0)
    block, width = resid_ref.shape
    span = width // GROUPS
    halves = len(gw_refs)
    vec = lambda row: load_norm(table_ref, row, width)

    @pl.when(step == 0)
    def _():
        load_mid(pieces, wmid, sem)
        acc[...] = jnp.zeros_like(acc)
        wait_all(wmid, sem)

    @pl.when(step < n_rows)
    def _():
        gnorm = resid_ref[...] + mm(gup_ref[...], wmid[:, width:], NT)
        scaled = scaled_ref[...]
        resid1 = norm_backward(gnorm, vec(GAIN1), scaled, inv_ref[...])
        resid1_ref[...] = resid1
        rounded = resid1.astype(BF)
        attn[rows_at(step, block), :] = rounded
        acc[0] += fold_rows(gnorm * scaled)
        acc[1] += fold_rows(gnorm)
        acc[2] += fold_rows(rounded.astype(F32))
        gctx = mm(rounded, wmid[:, :width], NT).astype(BF)
        for g, ref in enumerate((gctx0, gctx1, gctx2)):
            ref[...] = gctx[:, g * span : (g + 1) * span]

    @pl.when(step == n_rows)
    def _():
        for g, ctx in enumerate(ctxs):
            gout[g * span : (g + 1) * span, :] = mm(ctx[...], attn[...], TN).astype(BF)
        store_pieces(gout, gw_refs, out_sem, width // halves, 0)
        put_sums([acc[i] for i in range(3)], sums_ref)
        if sizes:
            notes, nsem = refs[6:]
            sums2_ref, usum_ref = given
            notes[...] = jnp.zeros_like(notes)
            vectors = [usum_ref[...]]
            vectors += [ref[i : i + 1, :] for ref in (sums_ref, sums2_ref) for i in range(3)]
            rows, _ = note_rows(sizes)
            for chip in range(CHIPS):
                fill_note(notes, chip, rows, vectors, chip, sizes)
            send_notes(notes, gw_refs, nsem)
            wait_notes(notes, gw_refs, nsem)
        wait_all(gout, out_sem)


def norm_call(resid2, gup, scaled1, inv1, ctx, table, pieces, given=(), block=256):
    total, width = resid2.shape
    ff = gup.shape[1]
    count = sum(p.shape[0] for p in pieces)
    halves = halves_of(count)
    sizes = [ff // CHIPS] + [width // CHIPS] * 6 if given else []
    n_rows = total // block
    row = lambda i: (jnp.minimum(i, n_rows - 1), 0)
    wide = lambda n: pl.BlockSpec((block, n), row)
    fixed = lambda *shape: pl.BlockSpec(shape, lambda i: (0, 0))
    scratch = [
        pltpu.VMEM((width, width + ff), BF),
        pltpu.VMEM((total, width), BF),
        pltpu.VMEM((width, width), BF),
        pltpu.VMEM((3, 8, width), F32),
        DMA,
        DMA,
    ]
    scratch += [pltpu.VMEM((CHIPS, width // CHIPS, 128), BF), DMA] if sizes else []
    gw = piece_structs(count, width * halves // count, width // halves + (128 if sizes else 0))
    resid1, gctx0, gctx1, gctx2, sums, *gw = call(
        partial(norm_kernel, sizes, len(pieces), len(gw), n_rows),
        "norm_back",
        17 * MICROSECOND,
        (struct((total, width), F32),)
        + (struct((total, width // GROUPS)),) * GROUPS
        + (struct((8, width), F32),)
        + gw,
        [wide(width), wide(ff), wide(width), wide(1)]
        + [fixed(total, width // GROUPS)] * GROUPS
        + [fixed(8, ff)]
        + [fixed(*v.shape) for v in given]
        + [HBM] * len(pieces),
        (wide(width),) + (wide(width // GROUPS),) * GROUPS + (fixed(8, width),) + (HBM,) * len(gw),
        scratch,
        grid=(n_rows + 1,),
    )(resid2, gup, scaled1, inv1, *ctx, table, *given, *pieces)
    return resid1, (gctx0, gctx1, gctx2), sums, gw


def attn_back_kernel(docs, rows, n_sums, n_out, count_ref, joined_ref, proj_ref, gctx_ref, lse_ref, *refs):
    earlier, refs = refs[:n_sums], refs[n_sums:]
    gproj_ref, sums_ref = refs[:2]
    gw_refs, refs = refs[2 : 2 + n_out], refs[2 + n_out :]
    gbuf, osem, probs_buf, gscores_buf = refs[:4]
    width = joined_ref.shape[1]
    span = width // GROUPS

    def doc_step(d, carry):
        base = pl.multiple_of(d * rows, 128)
        at = pl.ds(base, rows)
        count = count_ref[d]
        for lo in range(0, span, 128):
            pair, first = lo // 128, 3 * lo
            keys = proj_ref[at, first + 128 : first + 256]
            values = proj_ref[at, first + 256 : first + 384]
            all_queries, all_grads = [], []
            for block in range(0, rows, QUERIES):
                here = pl.ds(pl.multiple_of(base + block, 128), QUERIES)
                cols = slice(2 * block, 2 * block + 2 * QUERIES)
                queries = both_heads(proj_ref[here, first : first + 128] * BF(score_scale))
                grads = both_heads(gctx_ref[here, lo : lo + 128])
                scores = masked(mm(keys, queries, NT), count, rows - SLOTS)
                probs = jnp.exp(scores - lse_ref[d, pair, :, cols])
                gprobs = mm(values, grads, NT)
                dot = jnp.sum(probs * gprobs, axis=0, keepdims=True)
                probs_buf[pair, :, cols] = probs.astype(BF)
                gscores_buf[pair, :, cols] = (probs * (gprobs - dot)).astype(BF)
                all_queries.append(queries)
                all_grads.append(grads)
            gscores = gscores_buf[pair]
            dv = mm(probs_buf[pair], jnp.concatenate(all_grads, axis=0))
            dk = mm(gscores, jnp.concatenate(all_queries, axis=0))
            dq = mm((keys * BF(score_scale)).T, gscores)
            gproj_ref[at, first + 128 : first + 256] = dk.astype(BF)
            gproj_ref[at, first + 256 : first + 384] = dv.astype(BF)
            for block in range(0, rows, QUERIES):
                here = pl.ds(pl.multiple_of(base + block, 128), QUERIES)
                part = own_lanes(dq[:, 2 * block : 2 * block + 2 * QUERIES])
                gproj_ref[here, first : first + 128] = part.T.astype(BF)
        return carry

    lax.fori_loop(0, docs, doc_step, 0)
    half_width = width // 2

    def grad_step(r, carry):
        at = rows_at(r, half_width)
        gbuf[at, :] = mm(joined_ref[:, at], gproj_ref[...], TN).astype(BF)
        store_rows(gbuf, r * half_width, half_width, gw_refs, osem, half_width)
        return carry

    lax.fori_loop(0, 2, grad_step, 0)
    total = jnp.sum(gproj_ref[...].astype(F32), axis=0, keepdims=True)
    sums_ref[...] = total
    if n_sums:
        notes, nsem = refs[4:]
        parts = [ref[...] for ref in earlier] + [total]
        vector = jnp.concatenate(
            [p[:, at + t : at + t + 128] for t in (0, 256) for p in parts for at in range(0, width, 384)],
            axis=1,
        )
        notes[...] = jnp.zeros_like(notes)
        size = 2 * width // CHIPS
        for chip in range(CHIPS):
            notes[chip, 0:1, 0:size] = vector[:, chip * size : (chip + 1) * size].astype(BF)
        send_notes(notes, gw_refs, nsem)
        wait_notes(notes, gw_refs, nsem)
    wait_all(gbuf, osem)


def attn_back(seg_count, joined, proj, gctx, lse, count, sums=()):
    docs = seg_count.shape[0]
    total, width = joined.shape
    rows = total // docs
    span = width // GROUPS
    halves = halves_of(count)
    note = 128 if sums else 0
    scratch = [pltpu.VMEM((width, width), BF), DMA]
    scratch += [pltpu.VMEM((span // 128, rows, 2 * rows), BF)] * 2
    scratch += [pltpu.VMEM((CHIPS, width // CHIPS, 128), BF), DMA] if sums else []
    gw = piece_structs(count, width * halves // count, width // halves + note)
    gproj, total_sums, *gw = call(
        partial(attn_back_kernel, docs, rows, len(sums), len(gw)),
        "attn_back",
        14 * MICROSECOND,
        (
            struct((total, width)),
            struct((1, width), F32),
        )
        + gw,
        [SMEM] + [VMEM] * (4 + len(sums)),
        (VMEM, VMEM) + (HBM,) * len(gw),
        scratch,
    )(seg_count, joined, proj, gctx, lse, *sums)
    return gproj, total_sums, gw


def text_kernel(doc, shape, ids_ref, resid_ref, *refs):
    grads = refs[:GROUPS]
    sets, refs = [], refs[GROUPS:]
    for n_arrays in shape:
        sets.append(refs[:n_arrays])
        refs = refs[n_arrays:]
    n = len(shape)
    out_hbm, out_ref, out_sem = refs[-2 * n - 3 : -2 * n]
    bufs, piece_sems = refs[-2 * n : -n], refs[-n:]
    width = resid_ref.shape[1]
    text_len = out_ref.shape[0]
    at = pl.ds(doc * (text_len + SLOTS), text_len + SLOTS)
    for pieces, buf, sem in zip(sets, bufs, piece_sems):
        load_pieces(pieces, buf, sem, qkv_parts(0, buf.shape[1] // width))
    ids_row = ids_ref[doc : doc + 1, :]
    divisor = divisor_of(ids_row)
    total, g = resid_ref[at, :], 0
    for buf, sem in zip(bufs, piece_sems):
        wait_all(buf, sem)
        for i in range(buf.shape[1] // width):
            total = total + mm(grads[g][at, :], buf[:, i * width : (i + 1) * width], NT)
            g += 1
    summed = (total[text_len:, :] / divisor).astype(BF)
    out_ref[...] = total[:text_len, :] + mm(one_hot_of(ids_row, BF), summed, TN)
    fetch(out_ref, out_hbm.at[doc], out_sem).wait()


def text_grad(doc, slot_ids, resid1, grads, sets, earlier=None):
    docs, text_len = slot_ids.shape
    total, width = resid1.shape
    pieces = [piece for pieces, _ in sets for piece in pieces]
    given = () if earlier is None else (earlier,)
    return call(
        partial(text_kernel, doc, [len(pieces) for pieces, _ in sets]),
        "text_grad",
        7 * MICROSECOND,
        struct((docs, text_len, width), F32),
        [VMEM] * (2 + len(grads)) + [HBM] * len(pieces) + [HBM] * len(given),
        HBM,
        [pltpu.VMEM((text_len, width), F32), DMA]
        + [pltpu.VMEM((width, groups * width), BF) for _, groups in sets]
        + [DMA] * len(sets),
        room=14,
        aliases={2 + len(grads) + len(pieces): 0} if given else {},
    )(slot_ids, resid1, *grads, *pieces, *given)


AXES = ("rep", "shard")


def flips(core):
    return (1, 2) if core == 0 else (2, 1)


def pairs(flip_of):
    return [
        (core * CHIPS + s, core * CHIPS + (s ^ flip_of(core)))
        for core in range(2)
        for s in range(CHIPS)
    ]


Z_PERMS = [pairs(lambda core, k=k: k << 2) for k in (1, 2, 3)]
FIRST = pairs(lambda core: flips(core)[0])
SECOND = pairs(lambda core: flips(core)[1])
SWAP = [(core * CHIPS + s, (1 - core) * CHIPS + s) for core in range(2) for s in range(CHIPS)]


def send(array, perm):
    return lax.ppermute(array, AXES, perm)


def after(value, *earlier):
    return lax.optimization_barrier((value, *earlier))[0] if earlier else value


def add(left, right):
    return (left.astype(F32) + right.astype(F32)).astype(BF)


class Gather:
    def __init__(self, own):
        self.own = own

    def far(self, *earlier):
        self.own = after(self.own, *earlier)
        self.got = [send(self.own, perm) for perm in Z_PERMS]

    def first(self, *earlier):
        self.got_first = self.got[0]
        self.column = jnp.concatenate([self.own] + [after(part, *earlier) for part in self.got], axis=0)
        self.got = send(self.column, FIRST)
        self.swapped = [send(self.column, SWAP)]

    def second(self, *earlier):
        self.near = after(self.got, *earlier)
        self.got = [send(self.column, SECOND), send(self.near, SECOND)]
        self.swapped += [send(self.near, SWAP)]

    def swap(self, *earlier):
        self.got = [after(part, *earlier) for part in self.got]
        self.swapped += [send(part, SWAP) for part in self.got]
        self.all = [self.column, self.near] + self.got + self.swapped


class Scatter:
    def __init__(self):
        self.terms = []

    def swap(self, pair):
        self.terms.append([pair[0], send(pair[1], SWAP)])

    def summed(self, at, dtype=BF):
        sums, col = [], 0
        for terms in self.terms:
            n = terms[0].shape[2]
            total = sum(term[at].astype(F32) for term in terms)
            total += sum(whole[at, :, col : col + n].astype(F32) for whole in self.whole)
            sums.append(total.astype(dtype))
            col += n
        return sums[0] if len(sums) == 1 else jnp.concatenate(sums, axis=2)

    def second(self, *earlier):
        self.terms = [[kept, after(got, *earlier)] for kept, got in self.terms]
        self.whole = []
        self.away = self.summed(slice(8, 16))
        self.got = send(self.away, SECOND)

    def first(self, *earlier):
        self.whole.append(after(self.got, *earlier))
        self.away = self.summed(slice(4, 8))
        self.got = send(self.away, FIRST)

    def far(self, *earlier):
        self.whole.append(after(self.got, *earlier))
        self.away = [self.summed(slice(k, k + 1)) for k in (1, 2, 3)]
        self.got = [send(part, perm) for part, perm in zip(self.away, Z_PERMS)]

    def total(self, *earlier):
        mine = self.summed(slice(0, 1), F32)
        for part in self.got:
            mine = mine + after(part, *earlier).astype(F32)
        self.mine = mine[0]
        self.theirs = send(self.mine, SWAP)


def to_pairs(array):
    width = array.shape[1] // 3
    return jnp.concatenate(
        [array[:, t * width + p : t * width + p + 128] for p in range(0, width, 128) for t in range(3)],
        axis=1,
    )


def from_pairs(array):
    width = array.shape[1] // 3
    return jnp.concatenate(
        [array[:, 3 * p + t * 128 : 3 * p + t * 128 + 128] for t in range(3) for p in range(0, width, 128)],
        axis=1,
    )


def finish_mid_kernel(sizes, mine_ref, theirs_ref, out_ref, up_ref, *vector_refs):
    core = lax.axis_index("rep")
    n = out_ref.shape[1] // 2
    m = up_ref.shape[1] // 2
    for ref, half in ((mine_ref, core), (theirs_ref, 1 - core)):
        up_ref[:, pl.ds(pl.multiple_of(half * m, 128), m)] = ref[:, :m]
        out_ref[:, pl.ds(pl.multiple_of(half * n, 128), n)] = ref[:, m : m + n]
    rows, total = note_rows(sizes)
    note = jnp.where(core == 0, mine_ref[0:NOTE_ROWS, n + m :], theirs_ref[0:NOTE_ROWS, n + m :])
    for first, size, ref in zip(rows, sizes, vector_refs):
        for lane in range(0, size, 128):
            k = min(128, size - lane)
            ref[0:1, lane : lane + k] = note[first + lane // 128 : first + lane // 128 + 1, 0:k]


def finish_mid(mine, theirs, width, ff):
    rows = mine.shape[0]
    sizes = [ff // CHIPS] + [width // CHIPS] * 6
    return call(
        partial(finish_mid_kernel, sizes),
        "finish_mid",
        0,
        (struct((rows, width), F32), struct((rows, ff), F32)) + tuple(struct((1, n), F32) for n in sizes),
        [VMEM, VMEM],
        (VMEM,) * (2 + len(sizes)),
    )(mine, theirs)


def finish_qkv_kernel(groups, *refs):
    pairs_of = [(refs[2 * i], refs[2 * i + 1]) for i in range(len(groups))]
    out_ref, bias_ref = refs[2 * len(groups) :]
    core = lax.axis_index("rep")
    width = out_ref.shape[1] // 3
    g = 0
    for n, (mine_ref, theirs_ref) in zip(groups, pairs_of):
        for i in range(n):
            for ref, half in ((mine_ref, core), (theirs_ref, 1 - core)):
                for t in range(3):
                    to = pl.ds(pl.multiple_of(t * width + (2 * g + half) * 128, 128), 128)
                    out_ref[:, to] = ref[:, i * 384 + t * 128 : i * 384 + (t + 1) * 128]
            g += 1
    mine_ref, theirs_ref = pairs_of[-1]
    k = bias_ref.shape[1]
    at = mine_ref.shape[1] - 128
    bias_ref[...] = jnp.where(core == 0, mine_ref[0:1, at : at + k], theirs_ref[0:1, at : at + k])


def finish_qkv(parts, groups, width):
    rows = parts[0].shape[0]
    return call(
        partial(finish_qkv_kernel, groups),
        "finish_qkv",
        0,
        (struct((rows, 3 * width), F32), struct((1, 2 * width // CHIPS), F32)),
        [VMEM] * len(parts),
        (VMEM, VMEM),
    )(*parts)


def body(
    text_rows,
    slot_ids,
    seg_count,
    w_qkv,
    qv_bias,
    w_out,
    out_bias,
    ln1_gain,
    ln1_shift,
    w_up,
    up_bias,
    w_down,
    down_bias,
    ln2_gain,
    ln2_shift,
    cotangent,
):
    docs, text_len, width = text_rows.shape
    rows = text_len + SLOTS
    ff = w_up.shape[1]
    chips = lax.axis_size("shard")
    small = (qv_bias, out_bias, ln1_gain, ln1_shift, up_bias, down_bias, ln2_gain, ln2_shift)
    sizes = [v.shape[0] for v in small]
    cot = cotangent.reshape(docs * rows, width)
    if chips != CHIPS or lax.axis_size("rep") != 2:
        return plain(text_rows, slot_ids, seg_count, w_qkv, w_out, w_up, w_down, small, cot)

    core = lax.axis_index("rep")
    own_qkv, own_mid, own_down = prepare(w_qkv, w_out, w_up, w_down, small)
    qkv, mid, down = Gather(own_qkv), Gather(own_mid), Gather(own_down)
    qkv.far()
    joined = pool(slot_ids, text_rows)
    qkv.first(joined)
    mid.far(qkv.got_first)
    qkv.second(mid.got[0])
    qkv.swap(*mid.got[1:])
    mid.first()
    down.far(mid.column)
    table = unpack(sizes, [qkv.column, qkv.near] + qkv.got, ff)
    proj0, ctx0, lse0 = attn_fwd(0, 0, seg_count, after(joined, mid.column), table, qkv.all)
    mid.second(ctx0)
    proj1, ctx1, lse1 = attn_fwd(1, 1, seg_count, after(joined, ctx0, mid.near), table, qkv.all)
    down.first(ctx1)
    proj2, ctx2, lse2 = attn_fwd(2, 2, seg_count, after(joined, ctx1, down.column), table, qkv.all)
    mid.swap(ctx2)
    down.second(ctx2)
    down.swap()
    ctx = (ctx0, ctx1, ctx2)
    scaled_one, inverse_one, low, slope, layer_out, resid_two, sums_two, gw_down = forward_call(
        joined, ctx, cot, table, mid.all, down.all, ff
    )
    s_down, s_mid, s_qkv = Scatter(), Scatter(), Scatter()
    s_down.swap(gw_down)
    grad_up, sums_up = ffn_call(resid_two, slope, down.all)
    s_down.second(grad_up)
    gw_up = up_grad(after(low, s_down.away), grad_up, 2 * CHIPS)
    s_mid.swap(gw_up)
    resid_one, grad_ctx, _, gw_out = norm_call(
        after(resid_two, gw_up[0]), grad_up, scaled_one, inverse_one, ctx, table, mid.all, (sums_two, sums_up)
    )
    s_down.first(resid_one)
    s_mid.swap(gw_out)
    s_mid.second(resid_one)
    gp0, sp0, gw0 = attn_back(
        seg_count, joined, proj0, after(grad_ctx[0], s_down.away, s_mid.away), lse0, 2 * CHIPS
    )
    s_down.far(gp0)
    s_qkv.swap(gw0)
    gp1, sp1, gw1 = attn_back(
        seg_count, joined, proj1, after(grad_ctx[1], gp0, *s_down.away), lse1, 2 * CHIPS
    )
    s_mid.first(gp1)
    s_down.total(gp1)
    s_qkv.swap(gw1)
    gp2, sp2, gw2 = attn_back(
        seg_count, joined, proj2, after(grad_ctx[2], gp1, s_mid.away, s_down.mine), lse2, 2 * CHIPS, (sp0, sp1)
    )
    s_mid.far(gp2)
    s_qkv.swap(gw2)
    s_qkv.second()
    grads, sets = (gp0, gp1, gp2), ((qkv.all, 3),)
    grad_text = text_grad(0, slot_ids, after(resid_one, *s_mid.away, s_qkv.away), grads, sets)
    s_qkv.first(grad_text)
    grad_text = text_grad(1, slot_ids, after(resid_one, s_qkv.away), grads, sets, grad_text)
    s_mid.total(grad_text)
    s_qkv.far(grad_text, s_mid.mine)
    s_qkv.total()
    low_half = jnp.where(core == 0, s_down.mine, s_down.theirs)
    high_half = jnp.where(core == 0, s_down.theirs, s_down.mine)
    g_down = jnp.concatenate([low_half, high_half], axis=0)
    g_out, g_up, *vectors = finish_mid(s_mid.mine, s_mid.theirs, width, ff)
    b_up, b_out, b_gain1, b_shift1, b_down, b_gain2, b_shift2 = [
        vectors[i][0] for i in (0, 3, 1, 2, 6, 4, 5)
    ]
    g_qkv, g_bias = finish_qkv([s_qkv.mine, s_qkv.theirs], (3,), width)
    return (
        layer_out.reshape(docs, rows, width),
        grad_text,
        g_qkv,
        g_bias[0],
        g_out,
        b_out,
        b_gain1,
        b_shift1,
        g_up,
        b_up,
        g_down,
        b_down,
        b_gain2,
        b_shift2,
    )


def plain(text_rows, slot_ids, seg_count, w_qkv, w_out, w_up, w_down, small, cot):
    docs, text_len, width = text_rows.shape
    rows = text_len + SLOTS
    ff = w_up.shape[1]
    chips = lax.axis_size("shard")
    shard = lax.axis_index("shard")
    whole = lambda w: [lax.all_gather(w, "shard", axis=0, tiled=True)[None]]
    qkv, down = whole(to_pairs(w_qkv)), whole(w_down)
    mid = whole(jnp.concatenate([w_out, w_up], axis=1))
    sizes = [v.shape[0] for v in small]
    starts = [sum(sizes[:i]) for i in range(len(sizes))]
    notes = lax.all_gather(jnp.concatenate(small)[None], "shard", axis=0, tiled=True).astype(F32)
    full = [notes[:, a : a + n].reshape(1, chips * n) for a, n in zip(starts, sizes)]
    table = jnp.concatenate([jnp.pad(v, ((0, 0), (0, ff - v.shape[1]))) for v in full], axis=0)
    joined = pool(slot_ids, text_rows)
    proj, ctx, lse = zip(*[attn_fwd(g, g, seg_count, joined, table, qkv) for g in range(GROUPS)])
    scaled_one, inverse_one, low, slope, layer_out, resid_two, sums_two, gw_down = forward_call(
        joined, ctx, cot, table, mid, down, ff
    )
    grad_up, sums_up = ffn_call(resid_two, slope, down)
    gw_up = up_grad(low, grad_up, 1)
    resid_one, grad_ctx, sums_one, gw_out = norm_call(
        resid_two, grad_up, scaled_one, inverse_one, ctx, table, mid
    )
    back = [attn_back(seg_count, joined, proj[g], grad_ctx[g], lse[g], 1) for g in range(GROUPS)]
    grad_text = None
    for doc in range(docs):
        grads = [b[0] for b in back]
        grad_text = text_grad(doc, slot_ids, resid_one, grads, ((qkv, GROUPS),), grad_text)
    spread = lambda g: lax.psum(
        lax.psum_scatter(g.astype(F32), "shard", scatter_dimension=0, tiled=True), "rep"
    )
    g_down, g_out, g_up = spread(gw_down[0][0]), spread(gw_out[0][0]), spread(gw_up[0][0])
    g_qkv = from_pairs(spread(jnp.concatenate([b[2][0][0] for b in back], axis=1)))
    sums_two, sums_one, sums_up = lax.psum((sums_two, sums_one, sums_up), AXES)
    sums_proj = from_pairs(lax.psum(jnp.concatenate([b[1] for b in back], axis=1), AXES))
    mine = lambda v: lax.dynamic_slice_in_dim(v, shard * (v.shape[0] // chips), v.shape[0] // chips, 0)
    return (
        layer_out.reshape(docs, rows, width),
        grad_text,
        g_qkv,
        mine(jnp.concatenate([sums_proj[0, :width], sums_proj[0, 2 * width :]])),
        g_out,
        mine(sums_one[2]),
        mine(sums_one[0]),
        mine(sums_one[1]),
        g_up,
        mine(sums_up[0]),
        g_down,
        mine(sums_two[2]),
        mine(sums_two[0]),
        mine(sums_two[1]),
    )


def solution(mesh):
    in_specs = (
        P(("rep", "shard"), None, None),
        P(("rep", "shard"), None),
        P(("rep", "shard")),
        P("shard", None),
        P("shard"),
        P("shard", None),
        P("shard"),
        P("shard"),
        P("shard"),
        P("shard", None),
        P("shard"),
        P("shard", None),
        P("shard"),
        P("shard"),
        P("shard"),
        P(("rep", "shard"), None, None),
    )
    out_specs = (
        P(("rep", "shard"), None, None),
        P(("rep", "shard"), None, None),
        P("shard", None),
        P("shard"),
        P("shard", None),
        P("shard"),
        P("shard"),
        P("shard"),
        P("shard", None),
        P("shard"),
        P("shard", None),
        P("shard"),
        P("shard"),
        P("shard"),
    )
    return jax.shard_map(body, mesh=mesh, in_specs=in_specs, out_specs=out_specs, check_vma=False)
```

```python
import math
from functools import partial

import jax
import jax.numpy as jnp
from jax import lax
from jax.experimental import pallas as pl
from jax.experimental.pallas import tpu as pltpu
from jax.sharding import PartitionSpec as P

HEADS = 12
SLOTS = 128
GROUPS = 3
CHIPS = 16
NOTE_ROWS = 16

layer_eps = 1e-05
score_scale = 0.125
masked_score = -1000000000.0
BF = jnp.bfloat16
F32 = jnp.float32
MICROSECOND = 5000 * 10**6

NT = (((1,), (1,)), ((), ()))
NN = (((1,), (0,)), ((), ()))
TN = (((0,), (0,)), ((), ()))

QV, OUT, GAIN1, SHIFT1, UP, DOWN, GAIN2, SHIFT2 = range(8)


def mm(left, right, dims=NN):
    return lax.dot_general(left, right, dims, preferred_element_type=F32)


def call(kernel, name, cost, out_shape, in_specs, out_specs, scratch=(), room=12, aliases={}, grid=()):
    held = sum(math.prod(m.shape) * m.dtype.itemsize for m in scratch if m.memory_space == pltpu.VMEM)
    limit = 60 * 2**20 if grid else held + room * 2**20
    shapes = jax.tree.leaves(out_shape)
    moved = sum(math.prod(s.shape) * s.dtype.itemsize for s in shapes)
    return pl.pallas_call(
        kernel,
        out_shape=out_shape,
        grid=grid,
        in_specs=in_specs,
        out_specs=out_specs,
        scratch_shapes=list(scratch),
        input_output_aliases=aliases,
        compiler_params=pltpu.CompilerParams(vmem_limit_bytes=limit),
        cost_estimate=pl.CostEstimate(flops=int(cost), transcendentals=0, bytes_accessed=2 * moved),
        name=name,
    )


def struct(shape, dtype=BF):
    return jax.ShapeDtypeStruct(shape, dtype)


ANY = pl.BlockSpec(memory_space=pl.ANY)
HBM = pl.BlockSpec(memory_space=pltpu.HBM)
SMEM = pl.BlockSpec(memory_space=pltpu.SMEM)
VMEM = pl.BlockSpec(memory_space=pltpu.VMEM)
DMA = pltpu.SemaphoreType.DMA(())


def halves_of(count):
    return 1 if count == 1 else 2


def place(at, count):
    if count == 1:
        return 0, 0
    other, second, first, far = at // 16, (at // 8) % 2, (at // 4) % 2, at % 4
    half = lax.axis_index("rep") ^ other
    bits = jnp.where(half == 0, second * 2 + first, first * 2 + second)
    return lax.axis_index("shard") ^ (far * 4) ^ bits, half


def aligned(value, by):
    return value if isinstance(value, int) else pl.multiple_of(value, by)


def load_pieces(piece_refs, buf, sem, parts, by_rows=False):
    count = sum(ref.shape[0] for ref in piece_refs)
    whole = 2 // halves_of(count)
    at = 0
    for ref in piece_refs:
        rows = ref.shape[1]
        for i in range(ref.shape[0]):
            chip, half = place(at, count)
            if by_rows:
                chip, half = chip * halves_of(count) + half, 0
            row = aligned(chip * rows, 16)
            for col, n, first in parts:
                if not by_rows:
                    col, n = col * whole, n * whole
                to = aligned(half * n + first, 128)
                pltpu.make_async_copy(
                    ref.at[i, :, pl.ds(col, n)], buf.at[pl.ds(row, rows), pl.ds(to, n)], sem
                ).start()
            at += 1


def fetch(source, target, sem):
    copy = pltpu.make_async_copy(source, target, sem)
    copy.start()
    return copy


def blocks_of(total, block):
    return [pl.ds(first, block) for first in range(0, total, block)]


def sems(n):
    return pltpu.SemaphoreType.DMA((n,))


def slot_of(chip, half):
    apart = lax.axis_index("shard") ^ chip
    far, high, low = apart // 4, (apart // 2) % 2, apart % 2
    return jnp.where(half == 0, high * 8 + low * 4, low * 8 + high * 4) + far


def store_piece(source, out_refs, chip, half, col, sem):
    n = source.shape[1]
    for other, ref in enumerate(out_refs):

        @pl.when(lax.axis_index("rep") ^ half == other)
        def _():
            fetch(source, ref.at[slot_of(chip, half), :, pl.ds(col, n)], sem)


def store_rows(buf, first, rows, out_refs, sem, n):
    if len(out_refs) == 1:
        at = pl.ds(pl.multiple_of(first, 16), rows)
        fetch(buf.at[at, :], out_refs[0].at[0, at, :], sem)
        return
    piece = out_refs[0].shape[1]
    for k in range(0, rows, piece):
        at = pl.ds(pl.multiple_of(first + k, 16), piece)
        for half in range(2):
            source = buf.at[at, pl.ds(half * n, n)]
            store_piece(source, out_refs, (first + k) // piece, half, 0, sem)


def store_row_halves(buf, first, rows, out_refs, sem):
    if len(out_refs) == 1:
        at = pl.ds(pl.multiple_of(first, 16), rows)
        fetch(buf.at[at, :], out_refs[0].at[0, at, :], sem)
        return
    piece = out_refs[0].shape[1]
    for n, k in enumerate(range(0, rows, piece)):
        at = pl.ds(pl.multiple_of(first + k, 16), piece)
        store_piece(buf.at[at, :], out_refs, (first + k) // piece // 2, n % 2, 0, sem)


def rows_at(i, block):
    return pl.ds(pl.multiple_of(i * block, block), block)


def wait_all(buf, sem):
    pltpu.make_async_copy(buf, buf, sem).wait()


def count_of(out_refs):
    return sum(ref.shape[0] for ref in out_refs)


def store_pieces(buf, out_refs, sem, n, col, by_rows=False):
    count = count_of(out_refs)
    at = 0
    for ref in out_refs:
        rows = ref.shape[1]
        for i in range(ref.shape[0]):
            chip, half = place(at, count)
            if by_rows:
                chip, half = chip * halves_of(count) + half, 0
            row = aligned(chip * rows, 16)
            pltpu.make_async_copy(
                buf.at[pl.ds(row, rows), pl.ds(aligned(half * n, 128), n)],
                ref.at[i, :, pl.ds(col, n)],
                sem,
            ).start()
            at += 1


def qkv_parts(first, groups):
    return tuple(((first + g) * 384, 384, g * 768) for g in range(groups))


def mid_parts(width, ff):
    return ((0, width // 2, 0), (width // 2, ff // 2, width))


def load_norm(table_ref, row, n):
    return table_ref[row : row + 1, :n]


def note_rows(sizes):
    rows, at = [], 0
    for n in sizes:
        rows.append(at)
        at += -(-n // 128)
    return rows, at


def fill_note(note_ref, index, rows, vectors, chip, sizes):
    for first, vector, n in zip(rows, vectors, sizes):
        for lane in range(0, n, 128):
            m = min(128, n - lane)
            part = vector[:, chip * n + lane : chip * n + lane + m]
            note_ref[index, first + lane // 128 : first + lane // 128 + 1, 0:m] = part.astype(note_ref.dtype)


def send_notes(notes, out_refs, sem):
    at = 0
    for ref in out_refs:
        for i in range(ref.shape[0]):
            chip, _ = place(at, count_of(out_refs))
            pltpu.make_async_copy(
                notes.at[chip], ref.at[i, :, pl.ds(ref.shape[2] - 128, 128)], sem
            ).start()
            at += 1


def wait_notes(notes, out_refs, sem):
    for _ in out_refs:
        pltpu.make_async_copy(notes, notes, sem).wait()


def piece_structs(count, rows, cols):
    halves = halves_of(count)
    return tuple(struct((count // halves, rows, cols)) for _ in range(halves))


def prepare_kernel(sizes, qkv_ref, out_ref, up_ref, down_ref, *refs):
    vectors, (qkv, mid, down) = refs[: len(sizes)], refs[len(sizes) :]
    core = lax.axis_index("rep")
    width = out_ref.shape[1]
    for g in range(GROUPS):
        for t in range(3):
            cols = pl.ds(pl.multiple_of(t * width + (2 * g + core) * 128, 128), 128)
            qkv[0, :, g * 384 + t * 128 : g * 384 + (t + 1) * 128] = qkv_ref[:, cols]
    n = width // 2
    mid[0, :, :n] = out_ref[:, pl.ds(pl.multiple_of(core * n, 128), n)]
    n2 = up_ref.shape[1] // 2
    mid[0, :, n : n + n2] = up_ref[:, pl.ds(pl.multiple_of(core * n2, 128), n2)]
    n3 = down.shape[1]
    down[0] = down_ref[pl.ds(pl.multiple_of(core * n3, 16), n3), :]
    last = qkv.shape[2] - 128
    qkv[0, :, last:] = jnp.zeros((qkv.shape[1], 128), BF)
    rows, _ = note_rows(sizes)
    for first, vector, size in zip(rows, vectors, sizes):
        for lane in range(0, size, 128):
            m = min(128, size - lane)
            row = first + lane // 128
            qkv[0, row : row + 1, last : last + m] = vector[:, lane : lane + m]


def prepare(w_qkv, w_out, w_up, w_down, small):
    rows = w_qkv.shape[0]
    sizes = [v.shape[0] for v in small]
    half = w_down.shape[0] // 2
    shapes = (
        (1, rows, w_qkv.shape[1] // 2 + 128),
        (1, rows, (w_out.shape[1] + w_up.shape[1]) // 2),
        (1, half, w_down.shape[1]),
    )
    given = (w_qkv, w_out, w_up, w_down, *[v.reshape(1, -1) for v in small])
    whole = lambda shape: pl.BlockSpec(shape, lambda i: (0,) * len(shape))
    return call(
        partial(prepare_kernel, sizes),
        "prepare",
        MICROSECOND,
        tuple(struct(shape) for shape in shapes),
        [whole(v.shape) for v in given],
        tuple(whole(shape) for shape in shapes),
        grid=(1,),
    )(*given)


def unpack_kernel(sizes, n_arrays, *refs):
    pieces, (table_ref, notes, sem) = refs[:n_arrays], refs[n_arrays:]
    at = 0
    for ref in pieces:
        for i in range(ref.shape[0]):
            chip, _ = place(at, 2 * CHIPS)
            pltpu.make_async_copy(
                ref.at[i, pl.ds(0, NOTE_ROWS), pl.ds(ref.shape[2] - 128, 128)], notes.at[chip], sem
            ).start()
            at += 1
    wait_all(notes, sem)
    table_ref[...] = jnp.zeros_like(table_ref)
    rows, _ = note_rows(sizes)
    for k, (first, n) in enumerate(zip(rows, sizes)):
        for chip in range(CHIPS):
            for lane in range(0, n, 128):
                m = min(128, n - lane)
                row = first + lane // 128
                table_ref[k : k + 1, chip * n + lane : chip * n + lane + m] = notes[
                    chip, row : row + 1, 0:m
                ].astype(F32)


def unpack(sizes, pieces, width):
    return call(
        partial(unpack_kernel, sizes, len(pieces)),
        "unpack",
        0,
        struct((8, width), F32),
        [HBM] * len(pieces),
        VMEM,
        [pltpu.VMEM((CHIPS, NOTE_ROWS, 128), BF), DMA],
    )(*pieces)


def norm_parts(values):
    average = jnp.mean(values, axis=-1, keepdims=True)
    centred = values - average
    inverse = lax.rsqrt(jnp.mean(centred * centred, axis=-1, keepdims=True) + layer_eps)
    return centred * inverse, inverse


def norm_backward(grad_norm, gain_vec, scaled, inverse):
    grad_scaled = grad_norm * gain_vec
    grad_mean = jnp.mean(grad_scaled, axis=-1, keepdims=True)
    second = jnp.mean(grad_scaled * scaled, axis=-1, keepdims=True)
    return inverse * (grad_scaled - grad_mean - scaled * second)


def fold_rows(values):
    rows, cols = values.shape
    return jnp.sum(values.reshape(rows // 8, 8, cols), axis=0)


def one_hot_of(ids_row, dtype):
    slot = lax.broadcasted_iota(jnp.int32, (SLOTS, ids_row.shape[1]), 0)
    return jnp.where(slot == ids_row, 1.0, 0.0).astype(dtype)


def divisor_of(ids_row):
    members = jnp.sum(one_hot_of(ids_row, F32), axis=1, keepdims=True)
    return jnp.sqrt(jnp.maximum(members, 1.0))


def pool_kernel(ids_ref, text_ref, joined_ref):
    text_len = text_ref.shape[1]
    ids_row = ids_ref[pl.ds(pl.program_id(0), 1), :]
    summed = mm(one_hot_of(ids_row, BF), text_ref[0])
    joined_ref[0:text_len, :] = text_ref[0]
    joined_ref[text_len:, :] = (summed / divisor_of(ids_row)).astype(BF)


def pool(slot_ids, text_rows):
    docs, text_len, width = text_rows.shape
    rows = text_len + SLOTS
    return call(
        pool_kernel,
        "pool",
        3 * MICROSECOND,
        struct((docs * rows, width)),
        [VMEM, pl.BlockSpec((1, text_len, width), lambda d: (d, 0, 0))],
        pl.BlockSpec((rows, width), lambda d: (d, 0)),
        grid=(docs,),
    )(slot_ids, text_rows)


QUERIES = 128


def both_heads(rows):
    first = lax.broadcasted_iota(jnp.int32, (1, 128), 1) < 64
    zero = BF(0)
    return jnp.concatenate([jnp.where(first, rows, zero), jnp.where(first, zero, rows)], axis=0)


def own_lanes(product):
    n = product.shape[1] // 2
    first = lax.broadcasted_iota(jnp.int32, (128, 1), 0) < 64
    return jnp.where(first, product[:, :n], product[:, n:])


def masked(scores, count, text_len):
    slot = lax.broadcasted_iota(jnp.int32, (SLOTS, 1), 0)
    tail = jnp.where(slot < count, scores[text_len:, :], masked_score)
    return jnp.concatenate([scores[:text_len, :], tail], axis=0)


def attn_fwd_kernel(docs, rows, group, inside, n_arrays, count_ref, joined_ref, table_ref, *refs):
    pieces = refs[:n_arrays]
    proj_hbm, ctx_ref, lse_ref, wbuf, proj_ref, probs_buf, sem, out_sem = refs[n_arrays:]
    width = joined_ref.shape[1]
    span = width // GROUPS
    load_pieces(pieces, wbuf, sem, qkv_parts(inside, 1))
    bias = []
    for lo in range(group * span, (group + 1) * span, 128):
        bias += [
            table_ref[QV : QV + 1, lo : lo + 128],
            jnp.zeros((1, 128), F32),
            table_ref[QV : QV + 1, width + lo : width + lo + 128],
        ]
    bias = jnp.concatenate(bias, axis=1)
    wait_all(wbuf, sem)
    proj_ref[...] = (mm(joined_ref[...], wbuf[...]) + bias).astype(BF)
    departure = fetch(proj_ref, proj_hbm, out_sem)

    def doc_step(d, carry):
        base = pl.multiple_of(d * rows, 128)
        at = pl.ds(base, rows)
        count = count_ref[d]
        for lo in range(0, span, 128):
            first = 3 * lo
            keys = proj_ref[at, first + 128 : first + 256]
            values = proj_ref[at, first + 256 : first + 384]
            tops = []
            for block in range(0, rows, QUERIES):
                here = pl.ds(pl.multiple_of(base + block, 128), QUERIES)
                queries = both_heads(proj_ref[here, first : first + 128] * BF(score_scale))
                scores = masked(mm(keys, queries, NT), count, rows - SLOTS)
                top = jnp.max(scores, axis=0, keepdims=True)
                weights = jnp.exp(scores - top)
                total = jnp.sum(weights, axis=0, keepdims=True)
                cols = slice(2 * block, 2 * block + 2 * QUERIES)
                probs_buf[lo // 128, :, cols] = (weights * (1.0 / total)).astype(BF)
                tops.append(top + jnp.log(total))
            lse_ref[d, lo // 128] = jnp.concatenate(tops, axis=1)
            context = mm(values.T, probs_buf[lo // 128])
            for block in range(0, rows, QUERIES):
                here = pl.ds(pl.multiple_of(base + block, 128), QUERIES)
                part = own_lanes(context[:, 2 * block : 2 * block + 2 * QUERIES])
                ctx_ref[here, lo : lo + 128] = part.T.astype(BF)
        return carry

    lax.fori_loop(0, docs, doc_step, 0)
    departure.wait()


def attn_fwd(group, inside, seg_count, joined, table, pieces):
    docs = seg_count.shape[0]
    total, width = joined.shape
    rows = total // docs
    span = width // GROUPS
    return call(
        partial(attn_fwd_kernel, docs, rows, group, inside, len(pieces)),
        "attn_fwd",
        10 * MICROSECOND,
        (
            pltpu.HBM((total, width), BF),
            struct((total, span)),
            struct((docs, span // 128, 1, 2 * rows), F32),
        ),
        [SMEM, VMEM, VMEM] + [HBM] * len(pieces),
        (HBM, VMEM, VMEM),
        [
            pltpu.VMEM((width, width), BF),
            pltpu.VMEM((total, width), BF),
            pltpu.VMEM((span // 128, rows, 2 * rows), BF),
            DMA,
            DMA,
        ],
    )(seg_count, joined, table, *pieces)


def load_mid(pieces, wmid, sem):
    width = wmid.shape[0]
    load_pieces(pieces, wmid, sem, mid_parts(width, wmid.shape[1] - width))


def load_down(pieces, wdown, sem):
    load_pieces(pieces, wdown, sem, ((0, wdown.shape[1], 0),), by_rows=True)


def forward_kernel(n_mid, n_down, n_out, n_rows, n_cols, joined_ref, ctx0, ctx1, ctx2, cot_ref, table_ref, *refs):
    pieces, downs, refs = refs[:n_mid], refs[n_mid : n_mid + n_down], refs[n_mid + n_down :]
    low_ref, gup_ref, out_ref, resid_ref, attn_ref, gctx0, gctx1, gctx2, sums_ref, usum_ref = refs[:10]
    gw_refs, refs = refs[10 : 10 + n_out], refs[10 + n_out :]
    wmid, wdown, act, low_buf, gbuf, slope, acc, up_acc, sem, down_sem, gw_sem = refs
    step = pl.program_id(0)
    block, width = joined_ref.shape
    ff = wdown.shape[0]
    tile = ff // n_cols
    chunk = 768
    vec = lambda row: load_norm(table_ref, row, width)

    @pl.when(step == 0)
    def _():
        load_mid(pieces, wmid, sem)
        load_down(downs, wdown, down_sem)
        acc[...] = jnp.zeros_like(acc)
        up_acc[...] = jnp.zeros_like(up_acc)
        wait_all(wmid, sem)

    @pl.when(step < n_rows)
    def _():
        at = rows_at(step, block)
        ctx = jnp.concatenate([ctx0[...], ctx1[...], ctx2[...]], axis=1)
        branch = mm(ctx, wmid[:, :width]) + vec(OUT)
        scaled, inverse = norm_parts(joined_ref[...].astype(F32) + branch)
        normed1 = scaled * vec(GAIN1) + vec(SHIFT1)
        low = normed1.astype(BF)
        low_ref[...] = low
        down = vec(DOWN)
        for c in range(0, ff, chunk):
            cols = slice(c, c + chunk)
            up = mm(low, wmid[:, width + c : width + c + chunk]) + table_ref[UP : UP + 1, cols]
            half = 0.5 + 0.5 * lax.erf(up * math.sqrt(0.5))
            slope[:, cols] = half + up * (
                jnp.exp(-0.5 * (up * up)) * (1.0 / math.sqrt(2.0 * math.pi))
            )
            active = (up * half).astype(BF)
            act[at, cols] = active
            if c == 0:

                @pl.when(step == 0)
                def _():
                    wait_all(wdown, down_sem)

            down = down + mm(active, wdown[cols, :])
        scaled2, inverse2 = norm_parts(normed1 + down)
        out_ref[...] = (scaled2 * vec(GAIN2) + vec(SHIFT2)).astype(BF)
        grad = cot_ref[...].astype(F32)
        resid = norm_backward(grad, vec(GAIN2), scaled2, inverse2)
        rounded = resid.astype(BF)
        low_buf[at, :] = rounded
        acc[0] += fold_rows(grad * scaled2)
        acc[1] += fold_rows(grad)
        acc[2] += fold_rows(rounded.astype(F32))
        for c in range(0, ff, chunk):
            cols = slice(c, c + chunk)
            gup = (mm(rounded, wdown[cols, :], NT) * slope[:, cols]).astype(BF)
            gup_ref[:, cols] = gup
            up_acc[:, cols] += fold_rows(gup.astype(F32))
            resid = resid + mm(gup, wmid[:, width + c : width + c + chunk], NT)
        acc[3] += fold_rows(resid * scaled)
        acc[4] += fold_rows(resid)
        resid1 = norm_backward(resid, vec(GAIN1), scaled, inverse)
        resid_ref[...] = resid1
        attn = resid1.astype(BF)
        attn_ref[...] = attn
        acc[5] += fold_rows(attn.astype(F32))
        gctx = mm(attn, wmid[:, :width], NT).astype(BF)
        span = width // GROUPS
        for g, ref in enumerate((gctx0, gctx1, gctx2)):
            ref[...] = gctx[:, g * span : (g + 1) * span]

    @pl.when(step >= n_rows)
    def _():
        c = step - n_rows
        at = rows_at(c, tile)
        gbuf[at, :] = mm(act[:, at], low_buf[...], TN).astype(BF)
        store_row_halves(gbuf, c * tile, tile, gw_refs, gw_sem)

    @pl.when(step == n_rows + n_cols - 1)
    def _():
        put_sums([acc[i] for i in range(6)], sums_ref)
        usum_ref[...] = jnp.sum(up_acc[...], axis=0, keepdims=True)
        wait_all(gbuf, gw_sem)


def put_sums(sums, sums_ref):
    sums_ref[...] = jnp.zeros_like(sums_ref)
    for i, partial_sums in enumerate(sums):
        sums_ref[i : i + 1, :] = jnp.sum(partial_sums, axis=0, keepdims=True)


def forward_call(joined, ctx, cot, table, pieces, downs, ff, block=256, tile=384):
    total, width = joined.shape
    count = sum(p.shape[0] for p in pieces)
    gw = piece_structs(count, ff // count, width)
    n_rows, n_cols = total // block, ff // tile
    row = lambda i: (jnp.minimum(i, n_rows - 1), 0)
    wide = lambda n: pl.BlockSpec((block, n), row)
    fixed = lambda *shape: pl.BlockSpec(shape, lambda i: (0, 0))
    low, gup, out, resid, attn, gctx0, gctx1, gctx2, sums, usum, *gw = call(
        partial(forward_kernel, len(pieces), len(downs), len(gw), n_rows, n_cols),
        "forward",
        56 * MICROSECOND,
        (
            struct((total, width)),
            struct((total, ff)),
            struct((total, width)),
            struct((total, width), F32),
            struct((total, width)),
        )
        + (struct((total, width // GROUPS)),) * GROUPS
        + (struct((8, width), F32), struct((1, ff), F32))
        + gw,
        [wide(width)] + [wide(width // GROUPS)] * GROUPS + [wide(width), fixed(8, ff)]
        + [HBM] * (len(pieces) + len(downs)),
        (wide(width), wide(ff), wide(width), wide(width), wide(width))
        + (wide(width // GROUPS),) * GROUPS
        + (fixed(8, width), fixed(1, ff))
        + (HBM,) * len(gw),
        [
            pltpu.VMEM((width, width + ff), BF),
            pltpu.VMEM((ff, width), BF),
            pltpu.VMEM((total, ff), BF),
            pltpu.VMEM((total, width), BF),
            pltpu.VMEM((ff, width), BF),
            pltpu.VMEM((block, ff), F32),
            pltpu.VMEM((6, 8, width), F32),
            pltpu.VMEM((8, ff), F32),
            DMA,
            DMA,
            DMA,
        ],
        grid=(n_rows + n_cols,),
    )(joined, *ctx, cot, table, *pieces, *downs)
    return low, gup, out, resid, attn, (gctx0, gctx1, gctx2), sums, usum, gw


def store_tile(buf, out_refs, sem, half, col):
    if len(out_refs) == 1:
        fetch(buf, out_refs[0].at[0, :, pl.ds(col, buf.shape[1])], sem)
        return
    rows = out_refs[0].shape[1]
    for chip in range(buf.shape[0] // rows):
        store_piece(buf.at[pl.ds(chip * rows, rows), :], out_refs, chip, half, col, sem)


def mid_grad_kernel(sizes, n_out, n_up, low_ref, gup_ref, ctx0, ctx1, ctx2, attn_ref, *refs):
    given, refs = (refs[:2], refs[2:]) if sizes else ((), refs)
    gw_refs, refs = refs[:n_out], refs[n_out:]
    buf, gout, sem, out_sem = refs[:4]
    c = pl.program_id(0)
    width = low_ref.shape[1]
    span = width // GROUPS
    per = n_up // n_out

    @pl.when(c < n_up)
    def _():
        buf[c] = mm(low_ref[...], gup_ref[...], TN).astype(BF)
        store_tile(buf.at[c], gw_refs, sem, c // per, pl.multiple_of((c % per) * width, 128))

    @pl.when(c == n_up)
    def _():
        for g, ctx in enumerate((ctx0, ctx1, ctx2)):
            gout[g * span : (g + 1) * span, :] = mm(ctx[...], attn_ref[...], TN).astype(BF)
        store_pieces(gout, gw_refs, out_sem, width // n_out, per * width)
        if sizes:
            notes, nsem = refs[4:]
            sums_ref, usum_ref = given
            notes[...] = jnp.zeros_like(notes)
            vectors = [usum_ref[...]] + [sums_ref[i : i + 1, :] for i in (3, 4, 5, 0, 1, 2)]
            rows, _ = note_rows(sizes)
            for chip in range(CHIPS):
                fill_note(notes, chip, rows, vectors, chip, sizes)
            send_notes(notes, gw_refs, nsem)
            wait_notes(notes, gw_refs, nsem)
        wait_all(gout, out_sem)
        wait_all(buf, sem)


def mid_grad(low, gup, ctx, attn, count, given=()):
    total, width = low.shape
    ff = gup.shape[1]
    halves = halves_of(count)
    n_up = ff // width
    sizes = [ff // CHIPS] + [width // CHIPS] * 6 if given else []
    gw = piece_structs(count, width * halves // count, (width + ff) // halves + (128 if given else 0))
    fixed = lambda *shape: pl.BlockSpec(shape, lambda i: (0, 0))
    scratch = [pltpu.VMEM((n_up, width, width), BF), pltpu.VMEM((width, width), BF), DMA, DMA]
    scratch += [pltpu.VMEM((CHIPS, width // CHIPS, 128), BF), DMA] if given else []
    return call(
        partial(mid_grad_kernel, sizes, len(gw), n_up),
        "mid_grad",
        13 * MICROSECOND,
        gw,
        [fixed(total, width), pl.BlockSpec((total, width), lambda i: (0, jnp.minimum(i, n_up - 1)))]
        + [fixed(total, width // GROUPS)] * GROUPS
        + [fixed(total, width)]
        + [fixed(*v.shape) for v in given],
        (HBM,) * len(gw),
        scratch,
        grid=(n_up + 1,),
    )(low, gup, *ctx, attn, *given)


def attn_back_kernel(docs, rows, n_sums, n_out, count_ref, joined_ref, proj_ref, gctx_ref, lse_ref, *refs):
    earlier, refs = refs[:n_sums], refs[n_sums:]
    gproj_ref, sums_ref = refs[:2]
    gw_refs, refs = refs[2 : 2 + n_out], refs[2 + n_out :]
    gbuf, osem, probs_buf, gscores_buf = refs[:4]
    width = joined_ref.shape[1]
    span = width // GROUPS

    def doc_step(d, carry):
        base = pl.multiple_of(d * rows, 128)
        at = pl.ds(base, rows)
        count = count_ref[d]
        for lo in range(0, span, 128):
            pair, first = lo // 128, 3 * lo
            keys = proj_ref[at, first + 128 : first + 256]
            values = proj_ref[at, first + 256 : first + 384]
            all_queries, all_grads = [], []
            for block in range(0, rows, QUERIES):
                here = pl.ds(pl.multiple_of(base + block, 128), QUERIES)
                cols = slice(2 * block, 2 * block + 2 * QUERIES)
                queries = both_heads(proj_ref[here, first : first + 128] * BF(score_scale))
                grads = both_heads(gctx_ref[here, lo : lo + 128])
                scores = masked(mm(keys, queries, NT), count, rows - SLOTS)
                probs = jnp.exp(scores - lse_ref[d, pair, :, cols])
                gprobs = mm(values, grads, NT)
                dot = jnp.sum(probs * gprobs, axis=0, keepdims=True)
                probs_buf[pair, :, cols] = probs.astype(BF)
                gscores_buf[pair, :, cols] = (probs * (gprobs - dot)).astype(BF)
                all_queries.append(queries)
                all_grads.append(grads)
            gscores = gscores_buf[pair]
            dv = mm(probs_buf[pair], jnp.concatenate(all_grads, axis=0))
            dk = mm(gscores, jnp.concatenate(all_queries, axis=0))
            dq = mm((keys * BF(score_scale)).T, gscores)
            gproj_ref[at, first + 128 : first + 256] = dk.astype(BF)
            gproj_ref[at, first + 256 : first + 384] = dv.astype(BF)
            for block in range(0, rows, QUERIES):
                here = pl.ds(pl.multiple_of(base + block, 128), QUERIES)
                part = own_lanes(dq[:, 2 * block : 2 * block + 2 * QUERIES])
                gproj_ref[here, first : first + 128] = part.T.astype(BF)
        return carry

    lax.fori_loop(0, docs, doc_step, 0)
    half_width = width // 2

    def grad_step(r, carry):
        at = rows_at(r, half_width)
        gbuf[at, :] = mm(joined_ref[:, at], gproj_ref[...], TN).astype(BF)
        store_rows(gbuf, r * half_width, half_width, gw_refs, osem, half_width)
        return carry

    lax.fori_loop(0, 2, grad_step, 0)
    total = jnp.sum(gproj_ref[...].astype(F32), axis=0, keepdims=True)
    sums_ref[...] = total
    if n_sums:
        notes, nsem = refs[4:]
        parts = [ref[...] for ref in earlier] + [total]
        vector = jnp.concatenate(
            [p[:, at + t : at + t + 128] for t in (0, 256) for p in parts for at in range(0, width, 384)],
            axis=1,
        )
        notes[...] = jnp.zeros_like(notes)
        size = 2 * width // CHIPS
        for chip in range(CHIPS):
            notes[chip, 0:1, 0:size] = vector[:, chip * size : (chip + 1) * size].astype(BF)
        send_notes(notes, gw_refs, nsem)
        wait_notes(notes, gw_refs, nsem)
    wait_all(gbuf, osem)


def attn_back(seg_count, joined, proj, gctx, lse, count, sums=()):
    docs = seg_count.shape[0]
    total, width = joined.shape
    rows = total // docs
    span = width // GROUPS
    halves = halves_of(count)
    note = 128 if sums else 0
    scratch = [pltpu.VMEM((width, width), BF), DMA]
    scratch += [pltpu.VMEM((span // 128, rows, 2 * rows), BF)] * 2
    scratch += [pltpu.VMEM((CHIPS, width // CHIPS, 128), BF), DMA] if sums else []
    gw = piece_structs(count, width * halves // count, width // halves + note)
    gproj, total_sums, *gw = call(
        partial(attn_back_kernel, docs, rows, len(sums), len(gw)),
        "attn_back",
        14 * MICROSECOND,
        (
            struct((total, width)),
            struct((1, width), F32),
        )
        + gw,
        [SMEM] + [VMEM] * (4 + len(sums)),
        (VMEM, VMEM) + (HBM,) * len(gw),
        scratch,
    )(seg_count, joined, proj, gctx, lse, *sums)
    return gproj, total_sums, gw


def text_kernel(doc, shape, ids_ref, resid_ref, *refs):
    grads = refs[:GROUPS]
    sets, refs = [], refs[GROUPS:]
    for n_arrays in shape:
        sets.append(refs[:n_arrays])
        refs = refs[n_arrays:]
    n = len(shape)
    out_hbm, out_ref, out_sem = refs[-2 * n - 3 : -2 * n]
    bufs, piece_sems = refs[-2 * n : -n], refs[-n:]
    width = resid_ref.shape[1]
    text_len = out_ref.shape[0]
    at = pl.ds(doc * (text_len + SLOTS), text_len + SLOTS)
    for pieces, buf, sem in zip(sets, bufs, piece_sems):
        load_pieces(pieces, buf, sem, qkv_parts(0, buf.shape[1] // width))
    ids_row = ids_ref[doc : doc + 1, :]
    divisor = divisor_of(ids_row)
    total, g = resid_ref[at, :], 0
    for buf, sem in zip(bufs, piece_sems):
        wait_all(buf, sem)
        for i in range(buf.shape[1] // width):
            total = total + mm(grads[g][at, :], buf[:, i * width : (i + 1) * width], NT)
            g += 1
    summed = (total[text_len:, :] / divisor).astype(BF)
    out_ref[...] = total[:text_len, :] + mm(one_hot_of(ids_row, BF), summed, TN)
    fetch(out_ref, out_hbm.at[doc], out_sem).wait()


def text_grad(doc, slot_ids, resid1, grads, sets, earlier=None):
    docs, text_len = slot_ids.shape
    total, width = resid1.shape
    pieces = [piece for pieces, _ in sets for piece in pieces]
    given = () if earlier is None else (earlier,)
    return call(
        partial(text_kernel, doc, [len(pieces) for pieces, _ in sets]),
        "text_grad",
        7 * MICROSECOND,
        struct((docs, text_len, width), F32),
        [VMEM] * (2 + len(grads)) + [HBM] * len(pieces) + [HBM] * len(given),
        HBM,
        [pltpu.VMEM((text_len, width), F32), DMA]
        + [pltpu.VMEM((width, groups * width), BF) for _, groups in sets]
        + [DMA] * len(sets),
        room=14,
        aliases={2 + len(grads) + len(pieces): 0} if given else {},
    )(slot_ids, resid1, *grads, *pieces, *given)


AXES = ("rep", "shard")


def flips(core):
    return (1, 2) if core == 0 else (2, 1)


def pairs(flip_of):
    return [
        (core * CHIPS + s, core * CHIPS + (s ^ flip_of(core)))
        for core in range(2)
        for s in range(CHIPS)
    ]


Z_PERMS = [pairs(lambda core, k=k: k << 2) for k in (1, 2, 3)]
FIRST = pairs(lambda core: flips(core)[0])
SECOND = pairs(lambda core: flips(core)[1])
SWAP = [(core * CHIPS + s, (1 - core) * CHIPS + s) for core in range(2) for s in range(CHIPS)]


def send(array, perm):
    return lax.ppermute(array, AXES, perm)


def after(value, *earlier):
    return lax.optimization_barrier((value, *earlier))[0] if earlier else value


def add(left, right):
    return (left.astype(F32) + right.astype(F32)).astype(BF)


class Gather:
    def __init__(self, own):
        self.own = own

    def far(self, *earlier):
        self.own = after(self.own, *earlier)
        self.got = [send(self.own, perm) for perm in Z_PERMS]

    def first(self, *earlier):
        self.got_first = self.got[0]
        self.column = jnp.concatenate([self.own] + [after(part, *earlier) for part in self.got], axis=0)
        self.got = send(self.column, FIRST)
        self.swapped = [send(self.column, SWAP)]

    def second(self, *earlier):
        self.near = after(self.got, *earlier)
        self.got = [send(self.column, SECOND), send(self.near, SECOND)]
        self.swapped += [send(self.near, SWAP)]

    def swap(self, *earlier):
        self.got = [after(part, *earlier) for part in self.got]
        self.swapped += [send(part, SWAP) for part in self.got]
        self.all = [self.column, self.near] + self.got + self.swapped


class Scatter:
    def __init__(self):
        self.parts, self.widths = [], []

    def swap(self, pair):
        self.parts.append([(pair[0], 0), (send(pair[1], SWAP), 0)])
        self.widths.append(pair[0].shape[2])

    def join(self, other):
        self.parts += other.parts
        self.widths += other.widths

    def receive(self, *earlier):
        got, col = after(self.got, *earlier), 0
        for part, n in zip(self.parts, self.widths):
            part.append((got, col))
            col += n

    def summed(self, at, dtype=BF):
        sums = [
            sum(term[at, :, col : col + n].astype(F32) for term, col in part).astype(dtype)
            for part, n in zip(self.parts, self.widths)
        ]
        return sums[0] if len(sums) == 1 else jnp.concatenate(sums, axis=2)

    def pass_on(self, at, perm):
        self.away = self.summed(at)
        self.got = send(self.away, perm)

    def second(self, *earlier):
        for part in self.parts:
            part[1] = (after(part[1][0], *earlier), 0)
        self.pass_on(slice(8, 16), SECOND)

    def first(self, *earlier):
        self.receive(*earlier)
        self.pass_on(slice(4, 8), FIRST)

    def far(self, *earlier):
        self.receive(*earlier)
        self.away = [self.summed(slice(k, k + 1)) for k in (1, 2, 3)]
        self.got = [send(part, perm) for part, perm in zip(self.away, Z_PERMS)]

    def total(self, *earlier):
        mine = self.summed(slice(0, 1), F32)
        for part in self.got:
            mine = mine + after(part, *earlier).astype(F32)
        self.mine = mine[0]
        self.theirs = send(self.mine, SWAP)


def to_pairs(array):
    width = array.shape[1] // 3
    return jnp.concatenate(
        [array[:, t * width + p : t * width + p + 128] for p in range(0, width, 128) for t in range(3)],
        axis=1,
    )


def from_pairs(array):
    width = array.shape[1] // 3
    return jnp.concatenate(
        [array[:, 3 * p + t * 128 : 3 * p + t * 128 + 128] for t in range(3) for p in range(0, width, 128)],
        axis=1,
    )


def finish_mid_kernel(sizes, mine_ref, theirs_ref, out_ref, up_ref, *vector_refs):
    core = lax.axis_index("rep")
    n = out_ref.shape[1] // 2
    m = up_ref.shape[1] // 2
    for ref, half in ((mine_ref, core), (theirs_ref, 1 - core)):
        up_ref[:, pl.ds(pl.multiple_of(half * m, 128), m)] = ref[:, :m]
        out_ref[:, pl.ds(pl.multiple_of(half * n, 128), n)] = ref[:, m : m + n]
    rows, total = note_rows(sizes)
    note = jnp.where(core == 0, mine_ref[0:NOTE_ROWS, n + m :], theirs_ref[0:NOTE_ROWS, n + m :])
    for first, size, ref in zip(rows, sizes, vector_refs):
        for lane in range(0, size, 128):
            k = min(128, size - lane)
            ref[0:1, lane : lane + k] = note[first + lane // 128 : first + lane // 128 + 1, 0:k]


def finish_mid(mine, theirs, width, ff):
    rows = mine.shape[0]
    sizes = [ff // CHIPS] + [width // CHIPS] * 6
    return call(
        partial(finish_mid_kernel, sizes),
        "finish_mid",
        0,
        (struct((rows, width), F32), struct((rows, ff), F32)) + tuple(struct((1, n), F32) for n in sizes),
        [VMEM, VMEM],
        (VMEM,) * (2 + len(sizes)),
    )(mine, theirs)


def finish_qkv_kernel(groups, *refs):
    pairs_of = [(refs[2 * i], refs[2 * i + 1]) for i in range(len(groups))]
    out_ref, bias_ref = refs[2 * len(groups) :]
    core = lax.axis_index("rep")
    width = out_ref.shape[1] // 3
    g = 0
    for n, (mine_ref, theirs_ref) in zip(groups, pairs_of):
        for i in range(n):
            for ref, half in ((mine_ref, core), (theirs_ref, 1 - core)):
                for t in range(3):
                    to = pl.ds(pl.multiple_of(t * width + (2 * g + half) * 128, 128), 128)
                    out_ref[:, to] = ref[:, i * 384 + t * 128 : i * 384 + (t + 1) * 128]
            g += 1
    mine_ref, theirs_ref = pairs_of[-1]
    k = bias_ref.shape[1]
    at = mine_ref.shape[1] - 128
    bias_ref[...] = jnp.where(core == 0, mine_ref[0:1, at : at + k], theirs_ref[0:1, at : at + k])


def finish_qkv(parts, groups, width):
    rows = parts[0].shape[0]
    return call(
        partial(finish_qkv_kernel, groups),
        "finish_qkv",
        0,
        (struct((rows, 3 * width), F32), struct((1, 2 * width // CHIPS), F32)),
        [VMEM] * len(parts),
        (VMEM, VMEM),
    )(*parts)


def body(
    text_rows,
    slot_ids,
    seg_count,
    w_qkv,
    qv_bias,
    w_out,
    out_bias,
    ln1_gain,
    ln1_shift,
    w_up,
    up_bias,
    w_down,
    down_bias,
    ln2_gain,
    ln2_shift,
    cotangent,
):
    docs, text_len, width = text_rows.shape
    rows = text_len + SLOTS
    ff = w_up.shape[1]
    chips = lax.axis_size("shard")
    small = (qv_bias, out_bias, ln1_gain, ln1_shift, up_bias, down_bias, ln2_gain, ln2_shift)
    sizes = [v.shape[0] for v in small]
    cot = cotangent.reshape(docs * rows, width)
    if chips != CHIPS or lax.axis_size("rep") != 2:
        return plain(text_rows, slot_ids, seg_count, w_qkv, w_out, w_up, w_down, small, cot)

    core = lax.axis_index("rep")
    own_qkv, own_mid, own_down = prepare(w_qkv, w_out, w_up, w_down, small)
    qkv, mid, down = Gather(own_qkv), Gather(own_mid), Gather(own_down)
    qkv.far()
    mid.far()
    joined = pool(slot_ids, text_rows)
    qkv.first(joined, mid.got[0])
    down.far(qkv.column)
    qkv.second(*mid.got[1:])
    mid.first()
    qkv.swap()
    table = unpack(sizes, [qkv.column, qkv.near] + qkv.got, ff)
    mid.second(*down.got)
    down.first()
    proj0, ctx0, lse0 = attn_fwd(0, 0, seg_count, after(joined, mid.near, down.column), table, qkv.all)
    proj1, ctx1, lse1 = attn_fwd(1, 1, seg_count, after(joined, ctx0), table, qkv.all)
    proj2, ctx2, lse2 = attn_fwd(2, 2, seg_count, after(joined, ctx1), table, qkv.all)
    down.second(ctx2)
    mid.swap()
    down.swap()
    ctx = (ctx0, ctx1, ctx2)
    low, grad_up, layer_out, resid_one, attn, grad_ctx, sums, sums_up, gw_down = forward_call(
        joined, ctx, cot, table, mid.all, down.all, ff
    )
    s_down, s_mid, s_qkv = Scatter(), Scatter(), Scatter()
    s_down.swap(gw_down)
    gw_mid = mid_grad(low, grad_up, ctx, attn, 2 * CHIPS, (sums, sums_up))
    s_down.second(gw_mid[0])
    s_mid.swap(gw_mid)
    gp0, sp0, gw0 = attn_back(
        seg_count, joined, proj0, after(grad_ctx[0], s_down.away), lse0, 2 * CHIPS
    )
    s_mid.second(gp0)
    s_down.first(gp0)
    s_qkv.swap(gw0)
    gp1, sp1, gw1 = attn_back(
        seg_count, joined, proj1, after(grad_ctx[1], gp0, s_down.away, s_mid.away), lse1, 2 * CHIPS
    )
    s_down.far(gp1)
    s_mid.first(gp1)
    s_qkv.swap(gw1)
    gp2, sp2, gw2 = attn_back(
        seg_count, joined, proj2, after(grad_ctx[2], gp1, *s_down.away, s_mid.away), lse2, 2 * CHIPS, (sp0, sp1)
    )
    s_mid.far(gp2)
    s_down.total(gp2)
    s_qkv.swap(gw2)
    s_qkv.second(gp2)
    grads, sets = (gp0, gp1, gp2), ((qkv.all, 3),)
    grad_text = text_grad(0, slot_ids, after(resid_one, *s_mid.away, s_qkv.away, s_down.mine), grads, sets)
    s_qkv.first(grad_text)
    grad_text = text_grad(1, slot_ids, after(resid_one, s_qkv.away), grads, sets, grad_text)
    s_mid.total(grad_text)
    s_qkv.far(grad_text)
    s_qkv.total()
    low_half = jnp.where(core == 0, s_down.mine, s_down.theirs)
    high_half = jnp.where(core == 0, s_down.theirs, s_down.mine)
    g_down = jnp.concatenate([low_half, high_half], axis=0)
    g_out, g_up, *vectors = finish_mid(s_mid.mine, s_mid.theirs, width, ff)
    b_up, b_out, b_gain1, b_shift1, b_down, b_gain2, b_shift2 = [
        vectors[i][0] for i in (0, 3, 1, 2, 6, 4, 5)
    ]
    g_qkv, g_bias = finish_qkv([s_qkv.mine, s_qkv.theirs], (3,), width)
    return (
        layer_out.reshape(docs, rows, width),
        grad_text,
        g_qkv,
        g_bias[0],
        g_out,
        b_out,
        b_gain1,
        b_shift1,
        g_up,
        b_up,
        g_down,
        b_down,
        b_gain2,
        b_shift2,
    )


def plain(text_rows, slot_ids, seg_count, w_qkv, w_out, w_up, w_down, small, cot):
    docs, text_len, width = text_rows.shape
    rows = text_len + SLOTS
    ff = w_up.shape[1]
    chips = lax.axis_size("shard")
    shard = lax.axis_index("shard")
    whole = lambda w: [lax.all_gather(w, "shard", axis=0, tiled=True)[None]]
    qkv, down = whole(to_pairs(w_qkv)), whole(w_down)
    mid = whole(jnp.concatenate([w_out, w_up], axis=1))
    sizes = [v.shape[0] for v in small]
    starts = [sum(sizes[:i]) for i in range(len(sizes))]
    notes = lax.all_gather(jnp.concatenate(small)[None], "shard", axis=0, tiled=True).astype(F32)
    full = [notes[:, a : a + n].reshape(1, chips * n) for a, n in zip(starts, sizes)]
    table = jnp.concatenate([jnp.pad(v, ((0, 0), (0, ff - v.shape[1]))) for v in full], axis=0)
    joined = pool(slot_ids, text_rows)
    proj, ctx, lse = zip(*[attn_fwd(g, g, seg_count, joined, table, qkv) for g in range(GROUPS)])
    low, grad_up, layer_out, resid_one, attn, grad_ctx, sums, sums_up, gw_down = forward_call(
        joined, ctx, cot, table, mid, down, ff
    )
    gw_mid = mid_grad(low, grad_up, ctx, attn, 1)
    back = [attn_back(seg_count, joined, proj[g], grad_ctx[g], lse[g], 1) for g in range(GROUPS)]
    grad_text = None
    for doc in range(docs):
        grads = [b[0] for b in back]
        grad_text = text_grad(doc, slot_ids, resid_one, grads, ((qkv, GROUPS),), grad_text)
    spread = lambda g: lax.psum(
        lax.psum_scatter(g.astype(F32), "shard", scatter_dimension=0, tiled=True), "rep"
    )
    g_down, g_mid = spread(gw_down[0][0]), spread(gw_mid[0][0])
    g_qkv = from_pairs(spread(jnp.concatenate([b[2][0][0] for b in back], axis=1)))
    sums, sums_up = lax.psum((sums, sums_up), AXES)
    sums_proj = from_pairs(lax.psum(jnp.concatenate([b[1] for b in back], axis=1), AXES))
    mine = lambda v: lax.dynamic_slice_in_dim(v, shard * (v.shape[0] // chips), v.shape[0] // chips, 0)
    return (
        layer_out.reshape(docs, rows, width),
        grad_text,
        g_qkv,
        mine(jnp.concatenate([sums_proj[0, :width], sums_proj[0, 2 * width :]])),
        g_mid[:, ff:],
        mine(sums[5]),
        mine(sums[3]),
        mine(sums[4]),
        g_mid[:, :ff],
        mine(sums_up[0]),
        g_down,
        mine(sums[2]),
        mine(sums[0]),
        mine(sums[1]),
    )


def solution(mesh):
    in_specs = (
        P(("rep", "shard"), None, None),
        P(("rep", "shard"), None),
        P(("rep", "shard")),
        P("shard", None),
        P("shard"),
        P("shard", None),
        P("shard"),
        P("shard"),
        P("shard"),
        P("shard", None),
        P("shard"),
        P("shard", None),
        P("shard"),
        P("shard"),
        P("shard"),
        P(("rep", "shard"), None, None),
    )
    out_specs = (
        P(("rep", "shard"), None, None),
        P(("rep", "shard"), None, None),
        P("shard", None),
        P("shard"),
        P("shard", None),
        P("shard"),
        P("shard"),
        P("shard"),
        P("shard", None),
        P("shard"),
        P("shard", None),
        P("shard"),
        P("shard"),
        P("shard"),
    )
    return jax.shard_map(body, mesh=mesh, in_specs=in_specs, out_specs=out_specs, check_vma=False)
```

```python
import math
from functools import partial

import jax
import jax.numpy as jnp
from jax import lax
from jax.experimental import pallas as pl
from jax.experimental.pallas import tpu as pltpu
from jax.sharding import PartitionSpec as P

HEADS = 12
SLOTS = 128
GROUPS = 3
CHIPS = 16
NOTE_ROWS = 16

layer_eps = 1e-05
score_scale = 0.125
masked_score = -1000000000.0
BF = jnp.bfloat16
F32 = jnp.float32
MICROSECOND = 2500 * 10**6

NT = (((1,), (1,)), ((), ()))
NN = (((1,), (0,)), ((), ()))
TN = (((0,), (0,)), ((), ()))

QV, OUT, GAIN1, SHIFT1, UP, DOWN, GAIN2, SHIFT2 = range(8)


def mm(left, right, dims=NN):
    return lax.dot_general(left, right, dims, preferred_element_type=F32)


def call(kernel, name, cost, out_shape, in_specs, out_specs, scratch=(), room=3, aliases={}, grid=()):
    held = sum(math.prod(m.shape) * m.dtype.itemsize for m in scratch if m.memory_space == pltpu.VMEM)
    limit = 60 * 2**20 if grid else held + room * 2**20
    shapes = jax.tree.leaves(out_shape)
    moved = sum(math.prod(s.shape) * s.dtype.itemsize for s in shapes)
    return pl.pallas_call(
        kernel,
        out_shape=out_shape,
        grid=grid,
        in_specs=in_specs,
        out_specs=out_specs,
        scratch_shapes=list(scratch),
        input_output_aliases=aliases,
        compiler_params=pltpu.CompilerParams(vmem_limit_bytes=limit),
        cost_estimate=pl.CostEstimate(flops=int(cost), transcendentals=0, bytes_accessed=2 * moved),
        name=name,
    )


def struct(shape, dtype=BF):
    return jax.ShapeDtypeStruct(shape, dtype)


ANY = pl.BlockSpec(memory_space=pl.ANY)
HBM = pl.BlockSpec(memory_space=pltpu.HBM)
SMEM = pl.BlockSpec(memory_space=pltpu.SMEM)
VMEM = pl.BlockSpec(memory_space=pltpu.VMEM)
DMA = pltpu.SemaphoreType.DMA(())


def halves_of(count):
    return 1 if count == 1 else 2


def place(at, count):
    if count == 1:
        return 0, 0
    other, second, first, far = at // 16, (at // 8) % 2, (at // 4) % 2, at % 4
    half = lax.axis_index("rep") ^ other
    bits = jnp.where(half == 0, second * 2 + first, first * 2 + second)
    return lax.axis_index("shard") ^ (far * 4) ^ bits, half


def aligned(value, by):
    return value if isinstance(value, int) else pl.multiple_of(value, by)


def load_pieces(piece_refs, buf, sem, parts, by_rows=False):
    count = sum(ref.shape[0] for ref in piece_refs)
    whole = 2 // halves_of(count)
    at = 0
    for ref in piece_refs:
        rows = ref.shape[1]
        for i in range(ref.shape[0]):
            chip, half = place(at, count)
            if by_rows:
                chip, half = chip * halves_of(count) + half, 0
            row = aligned(chip * rows, 16)
            for col, n, first in parts:
                if not by_rows:
                    col, n = col * whole, n * whole
                to = aligned(half * n + first, 128)
                pltpu.make_async_copy(
                    ref.at[i, :, pl.ds(col, n)], buf.at[pl.ds(row, rows), pl.ds(to, n)], sem
                ).start()
            at += 1


def fetch(source, target, sem):
    copy = pltpu.make_async_copy(source, target, sem)
    copy.start()
    return copy


def blocks_of(total, block):
    return [pl.ds(first, block) for first in range(0, total, block)]


def sems(n):
    return pltpu.SemaphoreType.DMA((n,))


def slot_of(chip, half):
    apart = lax.axis_index("shard") ^ chip
    far, high, low = apart // 4, (apart // 2) % 2, apart % 2
    return jnp.where(half == 0, high * 8 + low * 4, low * 8 + high * 4) + far


def store_piece(source, out_refs, chip, half, col, sem):
    n = source.shape[1]
    for other, ref in enumerate(out_refs):

        @pl.when(lax.axis_index("rep") ^ half == other)
        def _():
            fetch(source, ref.at[slot_of(chip, half), :, pl.ds(col, n)], sem)


def store_rows(buf, first, rows, out_refs, sem, n):
    if len(out_refs) == 1:
        at = pl.ds(pl.multiple_of(first, 16), rows)
        fetch(buf.at[at, :], out_refs[0].at[0, at, :], sem)
        return
    piece = out_refs[0].shape[1]
    for k in range(0, rows, piece):
        at = pl.ds(pl.multiple_of(first + k, 16), piece)
        for half in range(2):
            source = buf.at[at, pl.ds(half * n, n)]
            store_piece(source, out_refs, (first + k) // piece, half, 0, sem)


def store_row_halves(buf, first, rows, out_refs, sem):
    if len(out_refs) == 1:
        at = pl.ds(pl.multiple_of(first, 16), rows)
        fetch(buf.at[at, :], out_refs[0].at[0, at, :], sem)
        return
    piece = out_refs[0].shape[1]
    for n, k in enumerate(range(0, rows, piece)):
        at = pl.ds(pl.multiple_of(first + k, 16), piece)
        store_piece(buf.at[at, :], out_refs, (first + k) // piece // 2, n % 2, 0, sem)


def rows_at(i, block):
    return pl.ds(pl.multiple_of(i * block, block), block)


def wait_all(buf, sem):
    pltpu.make_async_copy(buf, buf, sem).wait()


def count_of(out_refs):
    return sum(ref.shape[0] for ref in out_refs)


def store_pieces(buf, out_refs, sem, n, col, by_rows=False):
    count = count_of(out_refs)
    at = 0
    for ref in out_refs:
        rows = ref.shape[1]
        for i in range(ref.shape[0]):
            chip, half = place(at, count)
            if by_rows:
                chip, half = chip * halves_of(count) + half, 0
            row = aligned(chip * rows, 16)
            pltpu.make_async_copy(
                buf.at[pl.ds(row, rows), pl.ds(aligned(half * n, 128), n)],
                ref.at[i, :, pl.ds(col, n)],
                sem,
            ).start()
            at += 1


def qkv_parts(first, groups):
    return tuple(((first + g) * 384, 384, g * 768) for g in range(groups))


def mid_parts(width, ff):
    return ((0, width // 2, 0), (width // 2, ff // 2, width))


def load_norm(table_ref, row, n):
    return table_ref[row : row + 1, :n]


def note_rows(sizes):
    rows, at = [], 0
    for n in sizes:
        rows.append(at)
        at += -(-n // 128)
    return rows, at


def fill_note(note_ref, index, rows, vectors, chip, sizes):
    for first, vector, n in zip(rows, vectors, sizes):
        for lane in range(0, n, 128):
            m = min(128, n - lane)
            part = vector[:, chip * n + lane : chip * n + lane + m]
            note_ref[index, first + lane // 128 : first + lane // 128 + 1, 0:m] = part.astype(note_ref.dtype)


def send_notes(notes, out_refs, sem):
    at = 0
    for ref in out_refs:
        for i in range(ref.shape[0]):
            chip, _ = place(at, count_of(out_refs))
            pltpu.make_async_copy(
                notes.at[chip], ref.at[i, :, pl.ds(ref.shape[2] - 128, 128)], sem
            ).start()
            at += 1


def wait_notes(notes, out_refs, sem):
    for _ in out_refs:
        pltpu.make_async_copy(notes, notes, sem).wait()


def piece_structs(count, rows, cols):
    halves = halves_of(count)
    return tuple(struct((count // halves, rows, cols)) for _ in range(halves))


def prepare_qkv_kernel(sizes, qkv_ref, *refs):
    vectors, (qkv,) = refs[: len(sizes)], refs[len(sizes) :]
    core = lax.axis_index("rep")
    width = qkv_ref.shape[1] // 3
    for g in range(GROUPS):
        for t in range(3):
            cols = pl.ds(pl.multiple_of(t * width + (2 * g + core) * 128, 128), 128)
            qkv[0, :, g * 384 + t * 128 : g * 384 + (t + 1) * 128] = qkv_ref[:, cols]
    last = qkv.shape[2] - 128
    qkv[0, :, last:] = jnp.zeros((qkv.shape[1], 128), BF)
    rows, _ = note_rows(sizes)
    for first, vector, size in zip(rows, vectors, sizes):
        for lane in range(0, size, 128):
            m = min(128, size - lane)
            row = first + lane // 128
            part = vector[:, lane : lane + m] if len(vector.shape) == 2 else vector[lane : lane + m].reshape(1, m)
            qkv[0, row : row + 1, last : last + m] = part


def prepare_rest_kernel(out_ref, up_ref, down_ref, mid, down):
    core = lax.axis_index("rep")
    n, n2, n3 = out_ref.shape[1] // 2, up_ref.shape[1] // 2, down.shape[1]
    mid[0, :, :n] = out_ref[:, pl.ds(pl.multiple_of(core * n, 128), n)]
    mid[0, :, n:] = up_ref[:, pl.ds(pl.multiple_of(core * n2, 128), n2)]
    down[0] = down_ref[pl.ds(pl.multiple_of(core * n3, 16), n3), :]


def prepare(w_qkv, w_out, w_up, w_down, small):
    rows = w_qkv.shape[0]
    sizes = [v.shape[0] for v in small]
    whole = lambda shape: pl.BlockSpec(shape, lambda i: (0,) * len(shape))
    given = (w_qkv, *[v if v.shape[0] > 128 else v.reshape(1, -1) for v in small])
    shape = (1, rows, w_qkv.shape[1] // 2 + 128)
    qkv = call(
        partial(prepare_qkv_kernel, sizes),
        "prepare_qkv",
        MICROSECOND,
        struct(shape),
        [whole(v.shape) for v in given],
        whole(shape),
        grid=(1,),
    )(*given)
    given = (w_out, w_up, w_down)
    shapes = ((1, rows, (w_out.shape[1] + w_up.shape[1]) // 2), (1, w_down.shape[0] // 2, w_down.shape[1]))
    mid, down = call(
        prepare_rest_kernel,
        "prepare_rest",
        MICROSECOND,
        tuple(struct(shape) for shape in shapes),
        [whole(v.shape) for v in given],
        tuple(whole(shape) for shape in shapes),
        grid=(1,),
    )(*given)
    return qkv, mid, down


def unpack_kernel(sizes, n_arrays, *refs):
    pieces, (table_ref, notes, sem) = refs[:n_arrays], refs[n_arrays:]
    at = 0
    for ref in pieces:
        for i in range(ref.shape[0]):
            chip, _ = place(at, 2 * CHIPS)
            pltpu.make_async_copy(
                ref.at[i, pl.ds(0, NOTE_ROWS), pl.ds(ref.shape[2] - 128, 128)], notes.at[chip], sem
            ).start()
            at += 1
    wait_all(notes, sem)
    table_ref[...] = jnp.zeros_like(table_ref)
    rows, _ = note_rows(sizes)
    for k, (first, n) in enumerate(zip(rows, sizes)):
        for chip in range(CHIPS):
            for lane in range(0, n, 128):
                m = min(128, n - lane)
                row = first + lane // 128
                table_ref[k : k + 1, chip * n + lane : chip * n + lane + m] = notes[
                    chip, row : row + 1, 0:m
                ].astype(F32)


def unpack(sizes, pieces, width):
    return call(
        partial(unpack_kernel, sizes, len(pieces)),
        "unpack",
        0,
        struct((8, width), F32),
        [HBM] * len(pieces),
        VMEM,
        [pltpu.VMEM((CHIPS, NOTE_ROWS, 128), BF), DMA],
    )(*pieces)


def norm_parts(values):
    average = jnp.mean(values, axis=-1, keepdims=True)
    centred = values - average
    inverse = lax.rsqrt(jnp.mean(centred * centred, axis=-1, keepdims=True) + layer_eps)
    return centred * inverse, inverse


def norm_backward(grad_norm, gain_vec, scaled, inverse):
    grad_scaled = grad_norm * gain_vec
    grad_mean = jnp.mean(grad_scaled, axis=-1, keepdims=True)
    second = jnp.mean(grad_scaled * scaled, axis=-1, keepdims=True)
    return inverse * (grad_scaled - grad_mean - scaled * second)


def fold_rows(values):
    rows, cols = values.shape
    return jnp.sum(values.reshape(rows // 8, 8, cols), axis=0)


def one_hot_of(ids_row, dtype):
    slot = lax.broadcasted_iota(jnp.int32, (SLOTS, ids_row.shape[1]), 0)
    return jnp.where(slot == ids_row, 1.0, 0.0).astype(dtype)


def divisor_of(ids_row):
    members = jnp.sum(one_hot_of(ids_row, F32), axis=1, keepdims=True)
    return jnp.sqrt(jnp.maximum(members, 1.0))


def pool_kernel(ids_ref, text_ref, joined_ref):
    text_len = text_ref.shape[1]
    ids_row = ids_ref[pl.ds(pl.program_id(0), 1), :]
    summed = mm(one_hot_of(ids_row, BF), text_ref[0])
    joined_ref[0:text_len, :] = text_ref[0]
    joined_ref[text_len:, :] = (summed / divisor_of(ids_row)).astype(BF)


def pool(slot_ids, text_rows):
    docs, text_len, width = text_rows.shape
    rows = text_len + SLOTS
    return call(
        pool_kernel,
        "pool",
        3 * MICROSECOND,
        struct((docs * rows, width)),
        [VMEM, pl.BlockSpec((1, text_len, width), lambda d: (d, 0, 0))],
        pl.BlockSpec((rows, width), lambda d: (d, 0)),
        grid=(docs,),
    )(slot_ids, text_rows)


QUERIES = 128


def both_heads(rows):
    first = lax.broadcasted_iota(jnp.int32, (1, 128), 1) < 64
    zero = BF(0)
    return jnp.concatenate([jnp.where(first, rows, zero), jnp.where(first, zero, rows)], axis=0)


def own_lanes(product):
    n = product.shape[1] // 2
    first = lax.broadcasted_iota(jnp.int32, (128, 1), 0) < 64
    return jnp.where(first, product[:, :n], product[:, n:])


def masked(scores, count, text_len):
    slot = lax.broadcasted_iota(jnp.int32, (SLOTS, 1), 0)
    tail = jnp.where(slot < count, scores[text_len:, :], masked_score)
    return jnp.concatenate([scores[:text_len, :], tail], axis=0)


def attn_fwd_kernel(docs, rows, group, inside, n_arrays, count_ref, joined_ref, table_ref, *refs):
    pieces = refs[:n_arrays]
    proj_hbm, ctx_ref, lse_ref, wbuf, proj_ref, probs_buf, sem, out_sem = refs[n_arrays:]
    width = joined_ref.shape[1]
    span = width // GROUPS
    load_pieces(pieces, wbuf, sem, qkv_parts(inside, 1))
    bias = []
    for lo in range(group * span, (group + 1) * span, 128):
        bias += [
            table_ref[QV : QV + 1, lo : lo + 128],
            jnp.zeros((1, 128), F32),
            table_ref[QV : QV + 1, width + lo : width + lo + 128],
        ]
    bias = jnp.concatenate(bias, axis=1)
    wait_all(wbuf, sem)
    proj_ref[...] = (mm(joined_ref[...], wbuf[...]) + bias).astype(BF)
    departure = fetch(proj_ref, proj_hbm, out_sem)

    def doc_step(d, carry):
        base = pl.multiple_of(d * rows, 128)
        at = pl.ds(base, rows)
        count = count_ref[d]
        for lo in range(0, span, 128):
            first = 3 * lo
            keys = proj_ref[at, first + 128 : first + 256]
            values = proj_ref[at, first + 256 : first + 384]
            tops = []
            for block in range(0, rows, QUERIES):
                here = pl.ds(pl.multiple_of(base + block, 128), QUERIES)
                queries = both_heads(proj_ref[here, first : first + 128] * BF(score_scale))
                scores = masked(mm(keys, queries, NT), count, rows - SLOTS)
                top = jnp.max(scores, axis=0, keepdims=True)
                weights = jnp.exp(scores - top)
                total = jnp.sum(weights, axis=0, keepdims=True)
                cols = slice(2 * block, 2 * block + 2 * QUERIES)
                probs_buf[lo // 128, :, cols] = (weights * (1.0 / total)).astype(BF)
                tops.append(top + jnp.log(total))
            lse_ref[d, lo // 128] = jnp.concatenate(tops, axis=1)
            context = mm(values.T, probs_buf[lo // 128])
            for block in range(0, rows, QUERIES):
                here = pl.ds(pl.multiple_of(base + block, 128), QUERIES)
                part = own_lanes(context[:, 2 * block : 2 * block + 2 * QUERIES])
                ctx_ref[here, lo : lo + 128] = part.T.astype(BF)
        return carry

    lax.fori_loop(0, docs, doc_step, 0)
    departure.wait()


def attn_fwd(group, inside, seg_count, joined, table, pieces):
    docs = seg_count.shape[0]
    total, width = joined.shape
    rows = total // docs
    span = width // GROUPS
    return call(
        partial(attn_fwd_kernel, docs, rows, group, inside, len(pieces)),
        "attn_fwd",
        10 * MICROSECOND,
        (
            pltpu.HBM((total, width), BF),
            struct((total, span)),
            struct((docs, span // 128, 1, 2 * rows), F32),
        ),
        [SMEM, VMEM, VMEM] + [HBM] * len(pieces),
        (HBM, VMEM, VMEM),
        [
            pltpu.VMEM((width, width), BF),
            pltpu.VMEM((total, width), BF),
            pltpu.VMEM((span // 128, rows, 2 * rows), BF),
            DMA,
            DMA,
        ],
    )(seg_count, joined, table, *pieces)


def load_mid(pieces, wmid, sem):
    width = wmid.shape[0]
    load_pieces(pieces, wmid, sem, mid_parts(width, wmid.shape[1] - width))


def load_down(pieces, wdown, sem):
    load_pieces(pieces, wdown, sem, ((0, wdown.shape[1], 0),), by_rows=True)


def forward_kernel(n_mid, n_down, n_out, n_rows, n_cols, joined_ref, ctx0, ctx1, ctx2, cot_ref, table_ref, *refs):
    pieces, downs, refs = refs[:n_mid], refs[n_mid : n_mid + n_down], refs[n_mid + n_down :]
    low_ref, gup_ref, out_ref, resid_ref, attn_ref, gctx0, gctx1, gctx2, sums_ref, usum_ref = refs[:10]
    gw_refs, refs = refs[10 : 10 + n_out], refs[10 + n_out :]
    wmid, wdown, act, low_buf, gbuf, slope, acc, up_acc, sem, down_sem, gw_sem = refs
    step = pl.program_id(0)
    block, width = joined_ref.shape
    ff = wdown.shape[0]
    tile = ff // n_cols
    chunk = 768
    vec = lambda row: load_norm(table_ref, row, width)

    @pl.when(step == 0)
    def _():
        load_mid(pieces, wmid, sem)
        load_down(downs, wdown, down_sem)
        acc[...] = jnp.zeros_like(acc)
        up_acc[...] = jnp.zeros_like(up_acc)
        wait_all(wmid, sem)

    @pl.when(step < n_rows)
    def _():
        at = rows_at(step, block)
        ctx = jnp.concatenate([ctx0[...], ctx1[...], ctx2[...]], axis=1)
        branch = mm(ctx, wmid[:, :width]) + vec(OUT)
        scaled, inverse = norm_parts(joined_ref[...].astype(F32) + branch)
        normed1 = scaled * vec(GAIN1) + vec(SHIFT1)
        low = normed1.astype(BF)
        low_ref[...] = low
        down = vec(DOWN)
        for c in range(0, ff, chunk):
            cols = slice(c, c + chunk)
            up = mm(low, wmid[:, width + c : width + c + chunk]) + table_ref[UP : UP + 1, cols]
            half = 0.5 + 0.5 * lax.erf(up * math.sqrt(0.5))
            slope[:, cols] = half + up * (
                jnp.exp(-0.5 * (up * up)) * (1.0 / math.sqrt(2.0 * math.pi))
            )
            active = (up * half).astype(BF)
            act[at, cols] = active
            if c == 0:

                @pl.when(step == 0)
                def _():
                    wait_all(wdown, down_sem)

            down = down + mm(active, wdown[cols, :])
        scaled2, inverse2 = norm_parts(normed1 + down)
        out_ref[...] = (scaled2 * vec(GAIN2) + vec(SHIFT2)).astype(BF)
        grad = cot_ref[...].astype(F32)
        resid = norm_backward(grad, vec(GAIN2), scaled2, inverse2)
        rounded = resid.astype(BF)
        low_buf[at, :] = rounded
        acc[0] += fold_rows(grad * scaled2)
        acc[1] += fold_rows(grad)
        acc[2] += fold_rows(rounded.astype(F32))
        for c in range(0, ff, chunk):
            cols = slice(c, c + chunk)
            gup = (mm(rounded, wdown[cols, :], NT) * slope[:, cols]).astype(BF)
            gup_ref[:, cols] = gup
            up_acc[:, cols] += fold_rows(gup.astype(F32))
            resid = resid + mm(gup, wmid[:, width + c : width + c + chunk], NT)
        acc[3] += fold_rows(resid * scaled)
        acc[4] += fold_rows(resid)
        resid1 = norm_backward(resid, vec(GAIN1), scaled, inverse)
        resid_ref[...] = resid1
        attn = resid1.astype(BF)
        attn_ref[...] = attn
        acc[5] += fold_rows(attn.astype(F32))
        gctx = mm(attn, wmid[:, :width], NT).astype(BF)
        span = width // GROUPS
        for g, ref in enumerate((gctx0, gctx1, gctx2)):
            ref[...] = gctx[:, g * span : (g + 1) * span]

    @pl.when(step >= n_rows)
    def _():
        c = step - n_rows
        at = rows_at(c, tile)
        gbuf[at, :] = mm(act[:, at], low_buf[...], TN).astype(BF)
        store_row_halves(gbuf, c * tile, tile, gw_refs, gw_sem)

    @pl.when(step == n_rows + n_cols - 1)
    def _():
        put_sums([acc[i] for i in range(6)], sums_ref)
        usum_ref[...] = jnp.sum(up_acc[...], axis=0, keepdims=True)
        wait_all(gbuf, gw_sem)


def put_sums(sums, sums_ref):
    sums_ref[...] = jnp.zeros_like(sums_ref)
    for i, partial_sums in enumerate(sums):
        sums_ref[i : i + 1, :] = jnp.sum(partial_sums, axis=0, keepdims=True)


def forward_call(joined, ctx, cot, table, pieces, downs, ff, block=256, tile=384):
    total, width = joined.shape
    count = sum(p.shape[0] for p in pieces)
    gw = piece_structs(count, ff // count, width)
    n_rows, n_cols = total // block, ff // tile
    row = lambda i: (jnp.minimum(i, n_rows - 1), 0)
    wide = lambda n: pl.BlockSpec((block, n), row)
    fixed = lambda *shape: pl.BlockSpec(shape, lambda i: (0, 0))
    low, gup, out, resid, attn, gctx0, gctx1, gctx2, sums, usum, *gw = call(
        partial(forward_kernel, len(pieces), len(downs), len(gw), n_rows, n_cols),
        "forward",
        56 * MICROSECOND,
        (
            struct((total, width)),
            struct((total, ff)),
            struct((total, width)),
            struct((total, width), F32),
            struct((total, width)),
        )
        + (struct((total, width // GROUPS)),) * GROUPS
        + (struct((8, width), F32), struct((1, ff), F32))
        + gw,
        [wide(width)] + [wide(width // GROUPS)] * GROUPS + [wide(width), fixed(8, ff)]
        + [HBM] * (len(pieces) + len(downs)),
        (wide(width), wide(ff), wide(width), wide(width), wide(width))
        + (wide(width // GROUPS),) * GROUPS
        + (fixed(8, width), fixed(1, ff))
        + (HBM,) * len(gw),
        [
            pltpu.VMEM((width, width + ff), BF),
            pltpu.VMEM((ff, width), BF),
            pltpu.VMEM((total, ff), BF),
            pltpu.VMEM((total, width), BF),
            pltpu.VMEM((ff, width), BF),
            pltpu.VMEM((block, ff), F32),
            pltpu.VMEM((6, 8, width), F32),
            pltpu.VMEM((8, ff), F32),
            DMA,
            DMA,
            DMA,
        ],
        grid=(n_rows + n_cols,),
    )(joined, *ctx, cot, table, *pieces, *downs)
    return low, gup, out, resid, attn, (gctx0, gctx1, gctx2), sums, usum, gw


def store_tile(buf, out_refs, sem, half, col):
    if len(out_refs) == 1:
        fetch(buf, out_refs[0].at[0, :, pl.ds(col, buf.shape[1])], sem)
        return
    rows = out_refs[0].shape[1]
    for chip in range(buf.shape[0] // rows):
        store_piece(buf.at[pl.ds(chip * rows, rows), :], out_refs, chip, half, col, sem)


def mid_grad_kernel(sizes, n_out, n_up, low_ref, gup_ref, ctx0, ctx1, ctx2, attn_ref, *refs):
    given, refs = (refs[:2], refs[2:]) if sizes else ((), refs)
    gw_refs, refs = refs[:n_out], refs[n_out:]
    buf, gout, sem, out_sem = refs[:4]
    c = pl.program_id(0)
    width = low_ref.shape[1]
    span = width // GROUPS
    per = n_up // n_out

    @pl.when(c < n_up)
    def _():
        buf[c] = mm(low_ref[...], gup_ref[...], TN).astype(BF)
        store_tile(buf.at[c], gw_refs, sem, c // per, pl.multiple_of((c % per) * width, 128))

    @pl.when(c == n_up)
    def _():
        for g, ctx in enumerate((ctx0, ctx1, ctx2)):
            gout[g * span : (g + 1) * span, :] = mm(ctx[...], attn_ref[...], TN).astype(BF)
        store_pieces(gout, gw_refs, out_sem, width // n_out, per * width)
        if sizes:
            notes, nsem = refs[4:]
            sums_ref, usum_ref = given
            notes[...] = jnp.zeros_like(notes)
            vectors = [usum_ref[...]] + [sums_ref[i : i + 1, :] for i in (3, 4, 5, 0, 1, 2)]
            rows, _ = note_rows(sizes)
            for chip in range(CHIPS):
                fill_note(notes, chip, rows, vectors, chip, sizes)
            send_notes(notes, gw_refs, nsem)
            wait_notes(notes, gw_refs, nsem)
        wait_all(gout, out_sem)
        wait_all(buf, sem)


def mid_grad(low, gup, ctx, attn, count, given=()):
    total, width = low.shape
    ff = gup.shape[1]
    halves = halves_of(count)
    n_up = ff // width
    sizes = [ff // CHIPS] + [width // CHIPS] * 6 if given else []
    gw = piece_structs(count, width * halves // count, (width + ff) // halves + (128 if given else 0))
    fixed = lambda *shape: pl.BlockSpec(shape, lambda i: (0, 0))
    scratch = [pltpu.VMEM((n_up, width, width), BF), pltpu.VMEM((width, width), BF), DMA, DMA]
    scratch += [pltpu.VMEM((CHIPS, width // CHIPS, 128), BF), DMA] if given else []
    return call(
        partial(mid_grad_kernel, sizes, len(gw), n_up),
        "mid_grad",
        13 * MICROSECOND,
        gw,
        [fixed(total, width), pl.BlockSpec((total, width), lambda i: (0, jnp.minimum(i, n_up - 1)))]
        + [fixed(total, width // GROUPS)] * GROUPS
        + [fixed(total, width)]
        + [fixed(*v.shape) for v in given],
        (HBM,) * len(gw),
        scratch,
        grid=(n_up + 1,),
    )(low, gup, *ctx, attn, *given)


def attn_back_kernel(docs, rows, n_sums, n_out, count_ref, joined_ref, proj_ref, gctx_ref, lse_ref, *refs):
    earlier, refs = refs[:n_sums], refs[n_sums:]
    gproj_ref, sums_ref = refs[:2]
    gw_refs, refs = refs[2 : 2 + n_out], refs[2 + n_out :]
    gbuf, osem, probs_buf, gscores_buf = refs[:4]
    width = joined_ref.shape[1]
    span = width // GROUPS

    def doc_step(d, carry):
        base = pl.multiple_of(d * rows, 128)
        at = pl.ds(base, rows)
        count = count_ref[d]
        for lo in range(0, span, 128):
            pair, first = lo // 128, 3 * lo
            keys = proj_ref[at, first + 128 : first + 256]
            values = proj_ref[at, first + 256 : first + 384]
            all_queries, all_grads = [], []
            for block in range(0, rows, QUERIES):
                here = pl.ds(pl.multiple_of(base + block, 128), QUERIES)
                cols = slice(2 * block, 2 * block + 2 * QUERIES)
                queries = both_heads(proj_ref[here, first : first + 128] * BF(score_scale))
                grads = both_heads(gctx_ref[here, lo : lo + 128])
                scores = masked(mm(keys, queries, NT), count, rows - SLOTS)
                probs = jnp.exp(scores - lse_ref[d, pair, :, cols])
                gprobs = mm(values, grads, NT)
                dot = jnp.sum(probs * gprobs, axis=0, keepdims=True)
                probs_buf[pair, :, cols] = probs.astype(BF)
                gscores_buf[pair, :, cols] = (probs * (gprobs - dot)).astype(BF)
                all_queries.append(queries)
                all_grads.append(grads)
            gscores = gscores_buf[pair]
            dv = mm(probs_buf[pair], jnp.concatenate(all_grads, axis=0))
            dk = mm(gscores, jnp.concatenate(all_queries, axis=0))
            dq = mm((keys * BF(score_scale)).T, gscores)
            gproj_ref[at, first + 128 : first + 256] = dk.astype(BF)
            gproj_ref[at, first + 256 : first + 384] = dv.astype(BF)
            for block in range(0, rows, QUERIES):
                here = pl.ds(pl.multiple_of(base + block, 128), QUERIES)
                part = own_lanes(dq[:, 2 * block : 2 * block + 2 * QUERIES])
                gproj_ref[here, first : first + 128] = part.T.astype(BF)
        return carry

    lax.fori_loop(0, docs, doc_step, 0)
    half_width = width // 2

    def grad_step(r, carry):
        at = rows_at(r, half_width)
        gbuf[at, :] = mm(joined_ref[:, at], gproj_ref[...], TN).astype(BF)
        store_rows(gbuf, r * half_width, half_width, gw_refs, osem, half_width)
        return carry

    lax.fori_loop(0, 2, grad_step, 0)
    total = jnp.sum(gproj_ref[...].astype(F32), axis=0, keepdims=True)
    sums_ref[...] = total
    if n_sums:
        notes, nsem = refs[4:]
        parts = [ref[...] for ref in earlier] + [total]
        vector = jnp.concatenate(
            [p[:, at + t : at + t + 128] for t in (0, 256) for p in parts for at in range(0, width, 384)],
            axis=1,
        )
        notes[...] = jnp.zeros_like(notes)
        size = 2 * width // CHIPS
        for chip in range(CHIPS):
            notes[chip, 0:1, 0:size] = vector[:, chip * size : (chip + 1) * size].astype(BF)
        send_notes(notes, gw_refs, nsem)
        wait_notes(notes, gw_refs, nsem)
    wait_all(gbuf, osem)


def attn_back(seg_count, joined, proj, gctx, lse, count, sums=()):
    docs = seg_count.shape[0]
    total, width = joined.shape
    rows = total // docs
    span = width // GROUPS
    halves = halves_of(count)
    note = 128 if sums else 0
    scratch = [pltpu.VMEM((width, width), BF), DMA]
    scratch += [pltpu.VMEM((span // 128, rows, 2 * rows), BF)] * 2
    scratch += [pltpu.VMEM((CHIPS, width // CHIPS, 128), BF), DMA] if sums else []
    gw = piece_structs(count, width * halves // count, width // halves + note)
    gproj, total_sums, *gw = call(
        partial(attn_back_kernel, docs, rows, len(sums), len(gw)),
        "attn_back",
        14 * MICROSECOND,
        (
            struct((total, width)),
            struct((1, width), F32),
        )
        + gw,
        [SMEM] + [VMEM] * (4 + len(sums)),
        (VMEM, VMEM) + (HBM,) * len(gw),
        scratch,
    )(seg_count, joined, proj, gctx, lse, *sums)
    return gproj, total_sums, gw


def text_kernel(doc, shape, ids_ref, resid_ref, *refs):
    grads = refs[:GROUPS]
    sets, refs = [], refs[GROUPS:]
    for n_arrays in shape:
        sets.append(refs[:n_arrays])
        refs = refs[n_arrays:]
    n = len(shape)
    out_hbm, out_ref, out_sem = refs[-2 * n - 3 : -2 * n]
    bufs, piece_sems = refs[-2 * n : -n], refs[-n:]
    width = resid_ref.shape[1]
    text_len = out_ref.shape[0]
    at = pl.ds(doc * (text_len + SLOTS), text_len + SLOTS)
    for pieces, buf, sem in zip(sets, bufs, piece_sems):
        load_pieces(pieces, buf, sem, qkv_parts(0, buf.shape[1] // width))
    ids_row = ids_ref[doc : doc + 1, :]
    divisor = divisor_of(ids_row)
    total, g = resid_ref[at, :], 0
    for buf, sem in zip(bufs, piece_sems):
        wait_all(buf, sem)
        for i in range(buf.shape[1] // width):
            total = total + mm(grads[g][at, :], buf[:, i * width : (i + 1) * width], NT)
            g += 1
    summed = (total[text_len:, :] / divisor).astype(BF)
    out_ref[...] = total[:text_len, :] + mm(one_hot_of(ids_row, BF), summed, TN)
    fetch(out_ref, out_hbm.at[doc], out_sem).wait()


def text_grad(doc, slot_ids, resid1, grads, sets, earlier=None):
    docs, text_len = slot_ids.shape
    total, width = resid1.shape
    pieces = [piece for pieces, _ in sets for piece in pieces]
    given = () if earlier is None else (earlier,)
    return call(
        partial(text_kernel, doc, [len(pieces) for pieces, _ in sets]),
        "text_grad",
        7 * MICROSECOND,
        struct((docs, text_len, width), F32),
        [VMEM] * (2 + len(grads)) + [HBM] * len(pieces) + [HBM] * len(given),
        HBM,
        [pltpu.VMEM((text_len, width), F32), DMA]
        + [pltpu.VMEM((width, groups * width), BF) for _, groups in sets]
        + [DMA] * len(sets),
        room=6,
        aliases={2 + len(grads) + len(pieces): 0} if given else {},
    )(slot_ids, resid1, *grads, *pieces, *given)


AXES = ("rep", "shard")


def flips(core):
    return (1, 2) if core == 0 else (2, 1)


def pairs(flip_of):
    return [
        (core * CHIPS + s, core * CHIPS + (s ^ flip_of(core)))
        for core in range(2)
        for s in range(CHIPS)
    ]


Z_PERMS = [pairs(lambda core, k=k: k << 2) for k in (1, 2, 3)]
FIRST = pairs(lambda core: flips(core)[0])
SECOND = pairs(lambda core: flips(core)[1])
SWAP = [(core * CHIPS + s, (1 - core) * CHIPS + s) for core in range(2) for s in range(CHIPS)]


def send(array, perm):
    return lax.ppermute(array, AXES, perm)


def after(value, *earlier):
    return lax.optimization_barrier((value, *earlier))[0] if earlier else value


def add(left, right):
    return (left.astype(F32) + right.astype(F32)).astype(BF)


class Gather:
    def __init__(self, own):
        self.own = own

    def far(self, *earlier):
        self.own = after(self.own, *earlier)
        self.got = [send(self.own, perm) for perm in Z_PERMS]

    def first(self, *earlier):
        self.got_first = self.got[0]
        self.column = jnp.concatenate([self.own] + [after(part, *earlier) for part in self.got], axis=0)
        self.got = send(self.column, FIRST)
        self.swapped = [send(self.column, SWAP)]

    def second(self, *earlier):
        self.near = after(self.got, *earlier)
        self.got = [send(self.column, SECOND), send(self.near, SECOND)]
        self.swapped += [send(self.near, SWAP)]

    def swap(self, *earlier):
        self.got = [after(part, *earlier) for part in self.got]
        self.swapped += [send(part, SWAP) for part in self.got]
        self.all = [self.column, self.near] + self.got + self.swapped


class Scatter:
    def __init__(self):
        self.parts, self.widths = [], []

    def swap(self, pair):
        self.parts.append([(pair[0], 0), (send(pair[1], SWAP), 0)])
        self.widths.append(pair[0].shape[2])

    def join(self, other):
        self.parts += other.parts
        self.widths += other.widths

    def receive(self, *earlier):
        got, col = after(self.got, *earlier), 0
        for part, n in zip(self.parts, self.widths):
            part.append((got, col))
            col += n

    def summed(self, at, dtype=BF):
        sums = [
            sum(term[at, :, col : col + n].astype(F32) for term, col in part).astype(dtype)
            for part, n in zip(self.parts, self.widths)
        ]
        return sums[0] if len(sums) == 1 else jnp.concatenate(sums, axis=2)

    def pass_on(self, at, perm):
        self.away = self.summed(at)
        self.got = send(self.away, perm)

    def second(self, *earlier):
        for part in self.parts:
            part[1] = (after(part[1][0], *earlier), 0)
        self.pass_on(slice(8, 16), SECOND)

    def first(self, *earlier):
        self.receive(*earlier)
        self.pass_on(slice(4, 8), FIRST)

    def far(self, *earlier):
        self.receive(*earlier)
        self.away = [self.summed(slice(k, k + 1)) for k in (1, 2, 3)]
        self.got = [send(part, perm) for part, perm in zip(self.away, Z_PERMS)]

    def total(self, *earlier):
        mine = self.summed(slice(0, 1), F32)
        for part in self.got:
            mine = mine + after(part, *earlier).astype(F32)
        self.mine = mine[0]
        self.theirs = send(self.mine, SWAP)


def to_pairs(array):
    width = array.shape[1] // 3
    return jnp.concatenate(
        [array[:, t * width + p : t * width + p + 128] for p in range(0, width, 128) for t in range(3)],
        axis=1,
    )


def from_pairs(array):
    width = array.shape[1] // 3
    return jnp.concatenate(
        [array[:, 3 * p + t * 128 : 3 * p + t * 128 + 128] for t in range(3) for p in range(0, width, 128)],
        axis=1,
    )


def finish_mid_kernel(sizes, mine_ref, theirs_ref, out_ref, up_ref, *vector_refs):
    core = lax.axis_index("rep")
    n = out_ref.shape[1] // 2
    m = up_ref.shape[1] // 2
    for ref, half in ((mine_ref, core), (theirs_ref, 1 - core)):
        up_ref[:, pl.ds(pl.multiple_of(half * m, 128), m)] = ref[:, :m]
        out_ref[:, pl.ds(pl.multiple_of(half * n, 128), n)] = ref[:, m : m + n]
    rows, total = note_rows(sizes)
    note = jnp.where(core == 0, mine_ref[0:NOTE_ROWS, n + m :], theirs_ref[0:NOTE_ROWS, n + m :])
    for first, size, ref in zip(rows, sizes, vector_refs):
        for lane in range(0, size, 128):
            k = min(128, size - lane)
            ref[0:1, lane : lane + k] = note[first + lane // 128 : first + lane // 128 + 1, 0:k]


def finish_mid(mine, theirs, width, ff):
    rows = mine.shape[0]
    sizes = [ff // CHIPS] + [width // CHIPS] * 6
    return call(
        partial(finish_mid_kernel, sizes),
        "finish_mid",
        0,
        (struct((rows, width), F32), struct((rows, ff), F32)) + tuple(struct((1, n), F32) for n in sizes),
        [VMEM, VMEM],
        (VMEM,) * (2 + len(sizes)),
    )(mine, theirs)


def finish_qkv_kernel(groups, *refs):
    pairs_of = [(refs[2 * i], refs[2 * i + 1]) for i in range(len(groups))]
    out_ref, bias_ref = refs[2 * len(groups) :]
    core = lax.axis_index("rep")
    width = out_ref.shape[1] // 3
    g = 0
    for n, (mine_ref, theirs_ref) in zip(groups, pairs_of):
        for i in range(n):
            for ref, half in ((mine_ref, core), (theirs_ref, 1 - core)):
                for t in range(3):
                    to = pl.ds(pl.multiple_of(t * width + (2 * g + half) * 128, 128), 128)
                    out_ref[:, to] = ref[:, i * 384 + t * 128 : i * 384 + (t + 1) * 128]
            g += 1
    mine_ref, theirs_ref = pairs_of[-1]
    k = bias_ref.shape[1]
    at = mine_ref.shape[1] - 128
    bias_ref[...] = jnp.where(core == 0, mine_ref[0:1, at : at + k], theirs_ref[0:1, at : at + k])


def finish_qkv(parts, groups, width):
    rows = parts[0].shape[0]
    return call(
        partial(finish_qkv_kernel, groups),
        "finish_qkv",
        0,
        (struct((rows, 3 * width), F32), struct((1, 2 * width // CHIPS), F32)),
        [VMEM] * len(parts),
        (VMEM, VMEM),
    )(*parts)


def body(
    text_rows,
    slot_ids,
    seg_count,
    w_qkv,
    qv_bias,
    w_out,
    out_bias,
    ln1_gain,
    ln1_shift,
    w_up,
    up_bias,
    w_down,
    down_bias,
    ln2_gain,
    ln2_shift,
    cotangent,
):
    docs, text_len, width = text_rows.shape
    rows = text_len + SLOTS
    ff = w_up.shape[1]
    chips = lax.axis_size("shard")
    small = (qv_bias, out_bias, ln1_gain, ln1_shift, up_bias, down_bias, ln2_gain, ln2_shift)
    sizes = [v.shape[0] for v in small]
    cot = cotangent.reshape(docs * rows, width)
    if chips != CHIPS or lax.axis_size("rep") != 2:
        return plain(text_rows, slot_ids, seg_count, w_qkv, w_out, w_up, w_down, small, cot)

    core = lax.axis_index("rep")
    own_qkv, own_mid, own_down = prepare(w_qkv, w_out, w_up, w_down, small)
    qkv, mid, down = Gather(own_qkv), Gather(own_mid), Gather(own_down)
    qkv.far()
    mid.far()
    joined = pool(slot_ids, text_rows)
    qkv.first(joined, mid.got[0])
    down.far(qkv.column)
    qkv.second(*mid.got[1:])
    mid.first()
    qkv.swap()
    table = unpack(sizes, [qkv.column, qkv.near] + qkv.got, ff)
    mid.second(*down.got)
    down.first()
    proj0, ctx0, lse0 = attn_fwd(0, 0, seg_count, after(joined, mid.near, down.column), table, qkv.all)
    proj1, ctx1, lse1 = attn_fwd(1, 1, seg_count, after(joined, ctx0), table, qkv.all)
    proj2, ctx2, lse2 = attn_fwd(2, 2, seg_count, after(joined, ctx1), table, qkv.all)
    down.second(ctx2)
    mid.swap()
    down.swap()
    ctx = (ctx0, ctx1, ctx2)
    low, grad_up, layer_out, resid_one, attn, grad_ctx, sums, sums_up, gw_down = forward_call(
        joined, ctx, cot, table, mid.all, down.all, ff
    )
    s_down, s_mid, s_qkv = Scatter(), Scatter(), Scatter()
    s_down.swap(gw_down)
    gw_mid = mid_grad(low, grad_up, ctx, attn, 2 * CHIPS, (sums, sums_up))
    s_down.second(gw_mid[0])
    s_mid.swap(gw_mid)
    gp0, sp0, gw0 = attn_back(
        seg_count, joined, proj0, after(grad_ctx[0], s_down.away), lse0, 2 * CHIPS
    )
    s_mid.second(gp0)
    s_down.first(gp0)
    s_qkv.swap(gw0)
    gp1, sp1, gw1 = attn_back(
        seg_count, joined, proj1, after(grad_ctx[1], gp0, s_down.away, s_mid.away), lse1, 2 * CHIPS
    )
    s_down.far(gp1)
    s_mid.first(gp1)
    s_qkv.swap(gw1)
    gp2, sp2, gw2 = attn_back(
        seg_count, joined, proj2, after(grad_ctx[2], gp1, *s_down.away, s_mid.away), lse2, 2 * CHIPS, (sp0, sp1)
    )
    s_mid.far(gp2)
    s_down.total(gp2)
    s_qkv.swap(gw2)
    s_qkv.second(gp2)
    grads, sets = (gp0, gp1, gp2), ((qkv.all, 3),)
    grad_text = text_grad(0, slot_ids, after(resid_one, *s_mid.away, s_qkv.away, s_down.mine), grads, sets)
    s_qkv.first(grad_text)
    grad_text = text_grad(1, slot_ids, after(resid_one, s_qkv.away), grads, sets, grad_text)
    s_mid.total(grad_text)
    s_qkv.far(grad_text)
    s_qkv.total()
    low_half = jnp.where(core == 0, s_down.mine, s_down.theirs)
    high_half = jnp.where(core == 0, s_down.theirs, s_down.mine)
    g_down = jnp.concatenate([low_half, high_half], axis=0)
    g_out, g_up, *vectors = finish_mid(s_mid.mine, s_mid.theirs, width, ff)
    b_up, b_out, b_gain1, b_shift1, b_down, b_gain2, b_shift2 = [
        vectors[i][0] for i in (0, 3, 1, 2, 6, 4, 5)
    ]
    g_qkv, g_bias = finish_qkv([s_qkv.mine, s_qkv.theirs], (3,), width)
    return (
        layer_out.reshape(docs, rows, width),
        grad_text,
        g_qkv,
        g_bias[0],
        g_out,
        b_out,
        b_gain1,
        b_shift1,
        g_up,
        b_up,
        g_down,
        b_down,
        b_gain2,
        b_shift2,
    )


def plain(text_rows, slot_ids, seg_count, w_qkv, w_out, w_up, w_down, small, cot):
    docs, text_len, width = text_rows.shape
    rows = text_len + SLOTS
    ff = w_up.shape[1]
    chips = lax.axis_size("shard")
    shard = lax.axis_index("shard")
    whole = lambda w: [lax.all_gather(w, "shard", axis=0, tiled=True)[None]]
    qkv, down = whole(to_pairs(w_qkv)), whole(w_down)
    mid = whole(jnp.concatenate([w_out, w_up], axis=1))
    sizes = [v.shape[0] for v in small]
    starts = [sum(sizes[:i]) for i in range(len(sizes))]
    notes = lax.all_gather(jnp.concatenate(small)[None], "shard", axis=0, tiled=True).astype(F32)
    full = [notes[:, a : a + n].reshape(1, chips * n) for a, n in zip(starts, sizes)]
    table = jnp.concatenate([jnp.pad(v, ((0, 0), (0, ff - v.shape[1]))) for v in full], axis=0)
    joined = pool(slot_ids, text_rows)
    proj, ctx, lse = zip(*[attn_fwd(g, g, seg_count, joined, table, qkv) for g in range(GROUPS)])
    low, grad_up, layer_out, resid_one, attn, grad_ctx, sums, sums_up, gw_down = forward_call(
        joined, ctx, cot, table, mid, down, ff
    )
    gw_mid = mid_grad(low, grad_up, ctx, attn, 1)
    back = [attn_back(seg_count, joined, proj[g], grad_ctx[g], lse[g], 1) for g in range(GROUPS)]
    grad_text = None
    for doc in range(docs):
        grads = [b[0] for b in back]
        grad_text = text_grad(doc, slot_ids, resid_one, grads, ((qkv, GROUPS),), grad_text)
    spread = lambda g: lax.psum(
        lax.psum_scatter(g.astype(F32), "shard", scatter_dimension=0, tiled=True), "rep"
    )
    g_down, g_mid = spread(gw_down[0][0]), spread(gw_mid[0][0])
    g_qkv = from_pairs(spread(jnp.concatenate([b[2][0][0] for b in back], axis=1)))
    sums, sums_up = lax.psum((sums, sums_up), AXES)
    sums_proj = from_pairs(lax.psum(jnp.concatenate([b[1] for b in back], axis=1), AXES))
    mine = lambda v: lax.dynamic_slice_in_dim(v, shard * (v.shape[0] // chips), v.shape[0] // chips, 0)
    return (
        layer_out.reshape(docs, rows, width),
        grad_text,
        g_qkv,
        mine(jnp.concatenate([sums_proj[0, :width], sums_proj[0, 2 * width :]])),
        g_mid[:, ff:],
        mine(sums[5]),
        mine(sums[3]),
        mine(sums[4]),
        g_mid[:, :ff],
        mine(sums_up[0]),
        g_down,
        mine(sums[2]),
        mine(sums[0]),
        mine(sums[1]),
    )


def solution(mesh):
    in_specs = (
        P(("rep", "shard"), None, None),
        P(("rep", "shard"), None),
        P(("rep", "shard")),
        P("shard", None),
        P("shard"),
        P("shard", None),
        P("shard"),
        P("shard"),
        P("shard"),
        P("shard", None),
        P("shard"),
        P("shard", None),
        P("shard"),
        P("shard"),
        P("shard"),
        P(("rep", "shard"), None, None),
    )
    out_specs = (
        P(("rep", "shard"), None, None),
        P(("rep", "shard"), None, None),
        P("shard", None),
        P("shard"),
        P("shard", None),
        P("shard"),
        P("shard"),
        P("shard"),
        P("shard", None),
        P("shard"),
        P("shard", None),
        P("shard"),
        P("shard"),
        P("shard"),
    )
    return jax.shard_map(body, mesh=mesh, in_specs=in_specs, out_specs=out_specs, check_vma=False)
```

```python
import math
from functools import partial

import jax
import jax.numpy as jnp
from jax import lax
from jax.experimental import pallas as pl
from jax.experimental.pallas import tpu as pltpu
from jax.sharding import PartitionSpec as P

HEADS = 12
SLOTS = 128
GROUPS = 3
CHIPS = 16
NOTE_ROWS = 16

layer_eps = 1e-05
score_scale = 0.125
masked_score = -1000000000.0
BF = jnp.bfloat16
F32 = jnp.float32
MICROSECOND = 2500 * 10**6

NT = (((1,), (1,)), ((), ()))
NN = (((1,), (0,)), ((), ()))
TN = (((0,), (0,)), ((), ()))

QV, OUT, GAIN1, SHIFT1, UP, DOWN, GAIN2, SHIFT2 = range(8)


def mm(left, right, dims=NN):
    return lax.dot_general(left, right, dims, preferred_element_type=F32)


def call(kernel, name, cost, out_shape, in_specs, out_specs, scratch=(), room=3, aliases={}, grid=()):
    held = sum(math.prod(m.shape) * m.dtype.itemsize for m in scratch if m.memory_space == pltpu.VMEM)
    limit = 60 * 2**20 if grid else held + room * 2**20
    shapes = jax.tree.leaves(out_shape)
    moved = sum(math.prod(s.shape) * s.dtype.itemsize for s in shapes)
    return pl.pallas_call(
        kernel,
        out_shape=out_shape,
        grid=grid,
        in_specs=in_specs,
        out_specs=out_specs,
        scratch_shapes=list(scratch),
        input_output_aliases=aliases,
        compiler_params=pltpu.CompilerParams(vmem_limit_bytes=limit),
        cost_estimate=pl.CostEstimate(flops=int(cost), transcendentals=0, bytes_accessed=2 * moved),
        name=name,
    )


def struct(shape, dtype=BF):
    return jax.ShapeDtypeStruct(shape, dtype)


ANY = pl.BlockSpec(memory_space=pl.ANY)
HBM = pl.BlockSpec(memory_space=pltpu.HBM)
SMEM = pl.BlockSpec(memory_space=pltpu.SMEM)
VMEM = pl.BlockSpec(memory_space=pltpu.VMEM)
DMA = pltpu.SemaphoreType.DMA(())


def halves_of(count):
    return 1 if count == 1 else 2


def place(at, count):
    if count == 1:
        return 0, 0
    other, second, first, far = at // 16, (at // 8) % 2, (at // 4) % 2, at % 4
    half = lax.axis_index("rep") ^ other
    bits = jnp.where(half == 0, second * 2 + first, first * 2 + second)
    return lax.axis_index("shard") ^ (far * 4) ^ bits, half


def aligned(value, by):
    return value if isinstance(value, int) else pl.multiple_of(value, by)


def load_pieces(piece_refs, buf, sem, parts, by_rows=False):
    count = sum(ref.shape[0] for ref in piece_refs)
    whole = 2 // halves_of(count)
    at = 0
    for ref in piece_refs:
        rows = ref.shape[1]
        for i in range(ref.shape[0]):
            chip, half = place(at, count)
            if by_rows:
                chip, half = chip * halves_of(count) + half, 0
            row = aligned(chip * rows, 16)
            for col, n, first in parts:
                if not by_rows:
                    col, n = col * whole, n * whole
                to = aligned(half * n + first, 128)
                pltpu.make_async_copy(
                    ref.at[i, :, pl.ds(col, n)], buf.at[pl.ds(row, rows), pl.ds(to, n)], sem
                ).start()
            at += 1


def fetch(source, target, sem):
    copy = pltpu.make_async_copy(source, target, sem)
    copy.start()
    return copy


def blocks_of(total, block):
    return [pl.ds(first, block) for first in range(0, total, block)]


def sems(n):
    return pltpu.SemaphoreType.DMA((n,))


def slot_of(chip, half):
    apart = lax.axis_index("shard") ^ chip
    far, high, low = apart // 4, (apart // 2) % 2, apart % 2
    return jnp.where(half == 0, high * 8 + low * 4, low * 8 + high * 4) + far


def store_piece(source, out_refs, chip, half, col, sem):
    n = source.shape[1]
    for other, ref in enumerate(out_refs):

        @pl.when(lax.axis_index("rep") ^ half == other)
        def _():
            fetch(source, ref.at[slot_of(chip, half), :, pl.ds(col, n)], sem)


def store_rows(buf, first, rows, out_refs, sem, n):
    if len(out_refs) == 1:
        at = pl.ds(pl.multiple_of(first, 16), rows)
        fetch(buf.at[at, :], out_refs[0].at[0, at, :], sem)
        return
    piece = out_refs[0].shape[1]
    for k in range(0, rows, piece):
        at = pl.ds(pl.multiple_of(first + k, 16), piece)
        for half in range(2):
            source = buf.at[at, pl.ds(half * n, n)]
            store_piece(source, out_refs, (first + k) // piece, half, 0, sem)


def store_row_halves(buf, first, rows, out_refs, sem):
    if len(out_refs) == 1:
        at = pl.ds(pl.multiple_of(first, 16), rows)
        fetch(buf.at[at, :], out_refs[0].at[0, at, :], sem)
        return
    piece = out_refs[0].shape[1]
    for n, k in enumerate(range(0, rows, piece)):
        at = pl.ds(pl.multiple_of(first + k, 16), piece)
        store_piece(buf.at[at, :], out_refs, (first + k) // piece // 2, n % 2, 0, sem)


def rows_at(i, block):
    return pl.ds(pl.multiple_of(i * block, block), block)


def wait_all(buf, sem):
    pltpu.make_async_copy(buf, buf, sem).wait()


def count_of(out_refs):
    return sum(ref.shape[0] for ref in out_refs)


def store_pieces(buf, out_refs, sem, n, col, by_rows=False):
    count = count_of(out_refs)
    at = 0
    for ref in out_refs:
        rows = ref.shape[1]
        for i in range(ref.shape[0]):
            chip, half = place(at, count)
            if by_rows:
                chip, half = chip * halves_of(count) + half, 0
            row = aligned(chip * rows, 16)
            pltpu.make_async_copy(
                buf.at[pl.ds(row, rows), pl.ds(aligned(half * n, 128), n)],
                ref.at[i, :, pl.ds(col, n)],
                sem,
            ).start()
            at += 1


def qkv_parts(first, groups):
    return tuple(((first + g) * 384, 384, g * 768) for g in range(groups))


def mid_parts(width, ff):
    return ((0, width // 2, 0), (width // 2, ff // 2, width))


def load_norm(table_ref, row, n):
    return table_ref[row : row + 1, :n]


def note_rows(sizes):
    rows, at = [], 0
    for n in sizes:
        rows.append(at)
        at += -(-n // 128)
    return rows, at


def fill_note(note_ref, index, rows, vectors, chip, sizes):
    for first, vector, n in zip(rows, vectors, sizes):
        for lane in range(0, n, 128):
            m = min(128, n - lane)
            part = vector[:, chip * n + lane : chip * n + lane + m]
            note_ref[index, first + lane // 128 : first + lane // 128 + 1, 0:m] = part.astype(note_ref.dtype)


def send_notes(notes, out_refs, sem):
    at = 0
    for ref in out_refs:
        for i in range(ref.shape[0]):
            chip, _ = place(at, count_of(out_refs))
            pltpu.make_async_copy(
                notes.at[chip], ref.at[i, :, pl.ds(ref.shape[2] - 128, 128)], sem
            ).start()
            at += 1


def wait_notes(notes, out_refs, sem):
    for _ in out_refs:
        pltpu.make_async_copy(notes, notes, sem).wait()


def piece_structs(count, rows, cols):
    halves = halves_of(count)
    return tuple(struct((count // halves, rows, cols)) for _ in range(halves))


def prepare_qkv_kernel(sizes, qkv_ref, *refs):
    vectors, (qkv,) = refs[: len(sizes)], refs[len(sizes) :]
    core = lax.axis_index("rep")
    width = qkv_ref.shape[1] // 3
    for g in range(GROUPS):
        for t in range(3):
            cols = pl.ds(pl.multiple_of(t * width + (2 * g + core) * 128, 128), 128)
            qkv[0, :, g * 384 + t * 128 : g * 384 + (t + 1) * 128] = qkv_ref[:, cols]
    last = qkv.shape[2] - 128
    qkv[0, :, last:] = jnp.zeros((qkv.shape[1], 128), BF)
    rows, _ = note_rows(sizes)
    for first, vector, size in zip(rows, vectors, sizes):
        for lane in range(0, size, 128):
            m = min(128, size - lane)
            row = first + lane // 128
            part = vector[:, lane : lane + m] if len(vector.shape) == 2 else vector[lane : lane + m].reshape(1, m)
            qkv[0, row : row + 1, last : last + m] = part


def prepare_rest_kernel(out_ref, up_ref, down_ref, mid, down):
    core = lax.axis_index("rep")
    n, n2, n3 = out_ref.shape[1] // 2, up_ref.shape[1] // 2, down.shape[1]
    mid[0, :, :n] = out_ref[:, pl.ds(pl.multiple_of(core * n, 128), n)]
    mid[0, :, n:] = up_ref[:, pl.ds(pl.multiple_of(core * n2, 128), n2)]
    down[0] = down_ref[pl.ds(pl.multiple_of(core * n3, 16), n3), :]


def prepare(w_qkv, w_out, w_up, w_down, small):
    rows = w_qkv.shape[0]
    sizes = [v.shape[0] for v in small]
    whole = lambda shape: pl.BlockSpec(shape, lambda i: (0,) * len(shape))
    given = (w_qkv, *[v if v.shape[0] > 128 else v.reshape(1, -1) for v in small])
    shape = (1, rows, w_qkv.shape[1] // 2 + 128)
    qkv = call(
        partial(prepare_qkv_kernel, sizes),
        "prepare_qkv",
        MICROSECOND,
        struct(shape),
        [whole(v.shape) for v in given],
        whole(shape),
        grid=(1,),
    )(*given)
    given = (w_out, w_up, w_down)
    shapes = ((1, rows, (w_out.shape[1] + w_up.shape[1]) // 2), (1, w_down.shape[0] // 2, w_down.shape[1]))
    mid, down = call(
        prepare_rest_kernel,
        "prepare_rest",
        MICROSECOND,
        tuple(struct(shape) for shape in shapes),
        [whole(v.shape) for v in given],
        tuple(whole(shape) for shape in shapes),
        grid=(1,),
    )(*given)
    return qkv, mid, down


def unpack_kernel(sizes, n_arrays, *refs):
    pieces, (table_ref, notes, sem) = refs[:n_arrays], refs[n_arrays:]
    at = 0
    for ref in pieces:
        for i in range(ref.shape[0]):
            chip, _ = place(at, 2 * CHIPS)
            pltpu.make_async_copy(
                ref.at[i, pl.ds(0, NOTE_ROWS), pl.ds(ref.shape[2] - 128, 128)], notes.at[chip], sem
            ).start()
            at += 1
    wait_all(notes, sem)
    table_ref[...] = jnp.zeros_like(table_ref)
    rows, _ = note_rows(sizes)
    for k, (first, n) in enumerate(zip(rows, sizes)):
        for chip in range(CHIPS):
            for lane in range(0, n, 128):
                m = min(128, n - lane)
                row = first + lane // 128
                table_ref[k : k + 1, chip * n + lane : chip * n + lane + m] = notes[
                    chip, row : row + 1, 0:m
                ].astype(F32)


def unpack(sizes, pieces, width):
    return call(
        partial(unpack_kernel, sizes, len(pieces)),
        "unpack",
        0,
        struct((8, width), F32),
        [HBM] * len(pieces),
        VMEM,
        [pltpu.VMEM((CHIPS, NOTE_ROWS, 128), BF), DMA],
    )(*pieces)


def norm_parts(values):
    average = jnp.mean(values, axis=-1, keepdims=True)
    centred = values - average
    inverse = lax.rsqrt(jnp.mean(centred * centred, axis=-1, keepdims=True) + layer_eps)
    return centred * inverse, inverse


def norm_backward(grad_norm, gain_vec, scaled, inverse):
    grad_scaled = grad_norm * gain_vec
    grad_mean = jnp.mean(grad_scaled, axis=-1, keepdims=True)
    second = jnp.mean(grad_scaled * scaled, axis=-1, keepdims=True)
    return inverse * (grad_scaled - grad_mean - scaled * second)


def fold_rows(values):
    rows, cols = values.shape
    return jnp.sum(values.reshape(rows // 8, 8, cols), axis=0)


def one_hot_of(ids_row, dtype):
    slot = lax.broadcasted_iota(jnp.int32, (SLOTS, ids_row.shape[1]), 0)
    return jnp.where(slot == ids_row, 1.0, 0.0).astype(dtype)


def divisor_of(ids_row):
    members = jnp.sum(one_hot_of(ids_row, F32), axis=1, keepdims=True)
    return jnp.sqrt(jnp.maximum(members, 1.0))


def pool_kernel(ids_ref, text_ref, joined_ref):
    text_len = text_ref.shape[1]
    ids_row = ids_ref[pl.ds(pl.program_id(0), 1), :]
    summed = mm(one_hot_of(ids_row, BF), text_ref[0])
    joined_ref[0:text_len, :] = text_ref[0]
    joined_ref[text_len:, :] = (summed / divisor_of(ids_row)).astype(BF)


def pool(slot_ids, text_rows):
    docs, text_len, width = text_rows.shape
    rows = text_len + SLOTS
    return call(
        pool_kernel,
        "pool",
        3 * MICROSECOND,
        struct((docs * rows, width)),
        [VMEM, pl.BlockSpec((1, text_len, width), lambda d: (d, 0, 0))],
        pl.BlockSpec((rows, width), lambda d: (d, 0)),
        grid=(docs,),
    )(slot_ids, text_rows)


QUERIES = 128


def both_heads(rows):
    first = lax.broadcasted_iota(jnp.int32, (1, 128), 1) < 64
    zero = BF(0)
    return jnp.concatenate([jnp.where(first, rows, zero), jnp.where(first, zero, rows)], axis=0)


def own_lanes(product):
    n = product.shape[1] // 2
    first = lax.broadcasted_iota(jnp.int32, (128, 1), 0) < 64
    return jnp.where(first, product[:, :n], product[:, n:])


def masked(scores, count, text_len):
    slot = lax.broadcasted_iota(jnp.int32, (SLOTS, 1), 0)
    tail = jnp.where(slot < count, scores[text_len:, :], masked_score)
    return jnp.concatenate([scores[:text_len, :], tail], axis=0)


def attn_fwd_kernel(docs, rows, group, inside, n_arrays, count_ref, joined_ref, table_ref, *refs):
    pieces = refs[:n_arrays]
    proj_hbm, ctx_ref, lse_ref, wbuf, proj_ref, probs_buf, sem, out_sem = refs[n_arrays:]
    width = joined_ref.shape[1]
    span = width // GROUPS
    load_pieces(pieces, wbuf, sem, qkv_parts(inside, 1))
    bias = []
    for lo in range(group * span, (group + 1) * span, 128):
        bias += [
            table_ref[QV : QV + 1, lo : lo + 128],
            jnp.zeros((1, 128), F32),
            table_ref[QV : QV + 1, width + lo : width + lo + 128],
        ]
    bias = jnp.concatenate(bias, axis=1)
    wait_all(wbuf, sem)
    proj_ref[...] = (mm(joined_ref[...], wbuf[...]) + bias).astype(BF)
    departure = fetch(proj_ref, proj_hbm, out_sem)

    def doc_step(d, carry):
        base = pl.multiple_of(d * rows, 128)
        at = pl.ds(base, rows)
        count = count_ref[d]
        for lo in range(0, span, 128):
            first = 3 * lo
            keys = proj_ref[at, first + 128 : first + 256]
            values = proj_ref[at, first + 256 : first + 384]
            tops = []
            for block in range(0, rows, QUERIES):
                here = pl.ds(pl.multiple_of(base + block, 128), QUERIES)
                queries = both_heads(proj_ref[here, first : first + 128] * BF(score_scale))
                scores = masked(mm(keys, queries, NT), count, rows - SLOTS)
                top = jnp.max(scores, axis=0, keepdims=True)
                weights = jnp.exp(scores - top)
                total = jnp.sum(weights, axis=0, keepdims=True)
                cols = slice(2 * block, 2 * block + 2 * QUERIES)
                probs_buf[lo // 128, :, cols] = (weights * (1.0 / total)).astype(BF)
                tops.append(top + jnp.log(total))
            lse_ref[d, lo // 128] = jnp.concatenate(tops, axis=1)
            context = mm(values.T, probs_buf[lo // 128])
            for block in range(0, rows, QUERIES):
                here = pl.ds(pl.multiple_of(base + block, 128), QUERIES)
                part = own_lanes(context[:, 2 * block : 2 * block + 2 * QUERIES])
                ctx_ref[here, lo : lo + 128] = part.T.astype(BF)
        return carry

    lax.fori_loop(0, docs, doc_step, 0)
    departure.wait()


def attn_fwd(group, inside, seg_count, joined, table, pieces):
    docs = seg_count.shape[0]
    total, width = joined.shape
    rows = total // docs
    span = width // GROUPS
    return call(
        partial(attn_fwd_kernel, docs, rows, group, inside, len(pieces)),
        "attn_fwd",
        10 * MICROSECOND,
        (
            pltpu.HBM((total, width), BF),
            struct((total, span)),
            struct((docs, span // 128, 1, 2 * rows), F32),
        ),
        [SMEM, VMEM, VMEM] + [HBM] * len(pieces),
        (HBM, VMEM, VMEM),
        [
            pltpu.VMEM((width, width), BF),
            pltpu.VMEM((total, width), BF),
            pltpu.VMEM((span // 128, rows, 2 * rows), BF),
            DMA,
            DMA,
        ],
    )(seg_count, joined, table, *pieces)


def load_mid(pieces, wmid, sem):
    width = wmid.shape[0]
    load_pieces(pieces, wmid, sem, mid_parts(width, wmid.shape[1] - width))


def load_down(pieces, wdown, sem):
    load_pieces(pieces, wdown, sem, ((0, wdown.shape[1], 0),), by_rows=True)


def forward_kernel(n_mid, n_down, n_out, n_rows, n_cols, joined_ref, ctx0, ctx1, ctx2, cot_ref, table_ref, *refs):
    pieces, downs, refs = refs[:n_mid], refs[n_mid : n_mid + n_down], refs[n_mid + n_down :]
    low_ref, gup_ref, out_ref, resid_ref, attn_ref, gctx0, gctx1, gctx2, sums_ref, usum_ref = refs[:10]
    gw_refs, refs = refs[10 : 10 + n_out], refs[10 + n_out :]
    wmid, wdown, act, low_buf, gbuf, slope, acc, up_acc, sem, down_sem, gw_sem = refs
    step = pl.program_id(0)
    block, width = joined_ref.shape
    ff = wdown.shape[0]
    tile = ff // n_cols
    chunk = 768
    vec = lambda row: load_norm(table_ref, row, width)

    @pl.when(step == 0)
    def _():
        load_mid(pieces, wmid, sem)
        load_down(downs, wdown, down_sem)
        acc[...] = jnp.zeros_like(acc)
        up_acc[...] = jnp.zeros_like(up_acc)
        wait_all(wmid, sem)

    @pl.when(step < n_rows)
    def _():
        at = rows_at(step, block)
        ctx = jnp.concatenate([ctx0[...], ctx1[...], ctx2[...]], axis=1)
        branch = mm(ctx, wmid[:, :width]) + vec(OUT)
        scaled, inverse = norm_parts(joined_ref[...].astype(F32) + branch)
        normed1 = scaled * vec(GAIN1) + vec(SHIFT1)
        low = normed1.astype(BF)
        low_ref[...] = low
        down = vec(DOWN)
        for c in range(0, ff, chunk):
            cols = slice(c, c + chunk)
            up = mm(low, wmid[:, width + c : width + c + chunk]) + table_ref[UP : UP + 1, cols]
            half = 0.5 + 0.5 * lax.erf(up * math.sqrt(0.5))
            slope[:, cols] = half + up * (
                jnp.exp(-0.5 * (up * up)) * (1.0 / math.sqrt(2.0 * math.pi))
            )
            active = (up * half).astype(BF)
            act[at, cols] = active
            if c == 0:

                @pl.when(step == 0)
                def _():
                    wait_all(wdown, down_sem)

            down = down + mm(active, wdown[cols, :])
        scaled2, inverse2 = norm_parts(normed1 + down)
        out_ref[...] = (scaled2 * vec(GAIN2) + vec(SHIFT2)).astype(BF)
        grad = cot_ref[...].astype(F32)
        resid = norm_backward(grad, vec(GAIN2), scaled2, inverse2)
        rounded = resid.astype(BF)
        low_buf[at, :] = rounded
        acc[0] += fold_rows(grad * scaled2)
        acc[1] += fold_rows(grad)
        acc[2] += fold_rows(rounded.astype(F32))
        for c in range(0, ff, chunk):
            cols = slice(c, c + chunk)
            gup = (mm(rounded, wdown[cols, :], NT) * slope[:, cols]).astype(BF)
            gup_ref[:, cols] = gup
            up_acc[:, cols] += fold_rows(gup.astype(F32))
            resid = resid + mm(gup, wmid[:, width + c : width + c + chunk], NT)
        acc[3] += fold_rows(resid * scaled)
        acc[4] += fold_rows(resid)
        resid1 = norm_backward(resid, vec(GAIN1), scaled, inverse)
        resid_ref[...] = resid1
        attn = resid1.astype(BF)
        attn_ref[...] = attn
        acc[5] += fold_rows(attn.astype(F32))
        gctx = mm(attn, wmid[:, :width], NT).astype(BF)
        span = width // GROUPS
        for g, ref in enumerate((gctx0, gctx1, gctx2)):
            ref[...] = gctx[:, g * span : (g + 1) * span]

    @pl.when(step >= n_rows)
    def _():
        c = step - n_rows
        at = rows_at(c, tile)
        gbuf[at, :] = mm(act[:, at], low_buf[...], TN).astype(BF)
        store_row_halves(gbuf, c * tile, tile, gw_refs, gw_sem)

    @pl.when(step == n_rows + n_cols - 1)
    def _():
        put_sums([acc[i] for i in range(6)], sums_ref)
        usum_ref[...] = jnp.sum(up_acc[...], axis=0, keepdims=True)
        wait_all(gbuf, gw_sem)


def put_sums(sums, sums_ref):
    sums_ref[...] = jnp.zeros_like(sums_ref)
    for i, partial_sums in enumerate(sums):
        sums_ref[i : i + 1, :] = jnp.sum(partial_sums, axis=0, keepdims=True)


def forward_call(joined, ctx, cot, table, pieces, downs, ff, block=256, tile=384):
    total, width = joined.shape
    count = sum(p.shape[0] for p in pieces)
    gw = piece_structs(count, ff // count, width)
    n_rows, n_cols = total // block, ff // tile
    row = lambda i: (jnp.minimum(i, n_rows - 1), 0)
    wide = lambda n: pl.BlockSpec((block, n), row)
    fixed = lambda *shape: pl.BlockSpec(shape, lambda i: (0, 0))
    low, gup, out, resid, attn, gctx0, gctx1, gctx2, sums, usum, *gw = call(
        partial(forward_kernel, len(pieces), len(downs), len(gw), n_rows, n_cols),
        "forward",
        56 * MICROSECOND,
        (
            struct((total, width)),
            struct((total, ff)),
            struct((total, width)),
            struct((total, width), F32),
            struct((total, width)),
        )
        + (struct((total, width // GROUPS)),) * GROUPS
        + (struct((8, width), F32), struct((1, ff), F32))
        + gw,
        [wide(width)] + [wide(width // GROUPS)] * GROUPS + [wide(width), fixed(8, ff)]
        + [HBM] * (len(pieces) + len(downs)),
        (wide(width), wide(ff), wide(width), wide(width), wide(width))
        + (wide(width // GROUPS),) * GROUPS
        + (fixed(8, width), fixed(1, ff))
        + (HBM,) * len(gw),
        [
            pltpu.VMEM((width, width + ff), BF),
            pltpu.VMEM((ff, width), BF),
            pltpu.VMEM((total, ff), BF),
            pltpu.VMEM((total, width), BF),
            pltpu.VMEM((ff, width), BF),
            pltpu.VMEM((block, ff), F32),
            pltpu.VMEM((6, 8, width), F32),
            pltpu.VMEM((8, ff), F32),
            DMA,
            DMA,
            DMA,
        ],
        grid=(n_rows + n_cols,),
    )(joined, *ctx, cot, table, *pieces, *downs)
    return low, gup, out, resid, attn, (gctx0, gctx1, gctx2), sums, usum, gw


def store_tile(buf, out_refs, sem, half, col):
    if len(out_refs) == 1:
        fetch(buf, out_refs[0].at[0, :, pl.ds(col, buf.shape[1])], sem)
        return
    rows = out_refs[0].shape[1]
    for chip in range(buf.shape[0] // rows):
        store_piece(buf.at[pl.ds(chip * rows, rows), :], out_refs, chip, half, col, sem)


def mid_grad_kernel(sizes, n_out, n_up, low_ref, gup_ref, ctx0, ctx1, ctx2, attn_hbm, *refs):
    given, refs = (refs[:2], refs[2:]) if sizes else ((), refs)
    gw_refs, refs = refs[:n_out], refs[n_out:]
    buf, gout, ctx_ref, attn_ref, sem, out_sem, in_sem = refs[:7]
    c = pl.program_id(0)
    width = low_ref.shape[1]
    span = width // GROUPS
    per = n_up // n_out
    arrivals = [
        pltpu.make_async_copy(ctx, ctx_ref.at[:, pl.ds(g * span, span)], in_sem.at[g])
        for g, ctx in enumerate((ctx0, ctx1, ctx2))
    ]
    arrivals.append(pltpu.make_async_copy(attn_hbm, attn_ref, in_sem.at[GROUPS]))

    @pl.when(c == 0)
    def _():
        for arrival in arrivals:
            arrival.start()

    @pl.when(c < n_up)
    def _():
        buf[c] = mm(low_ref[...], gup_ref[...], TN).astype(BF)
        store_tile(buf.at[c], gw_refs, sem, c // per, pl.multiple_of((c % per) * width, 128))

    @pl.when(c == n_up)
    def _():
        for arrival in arrivals:
            arrival.wait()
        gout[...] = mm(ctx_ref[...], attn_ref[...], TN).astype(BF)
        store_pieces(gout, gw_refs, out_sem, width // n_out, per * width)
        if sizes:
            notes, nsem = refs[7:]
            sums_ref, usum_ref = given
            notes[...] = jnp.zeros_like(notes)
            vectors = [usum_ref[...]] + [sums_ref[i : i + 1, :] for i in (3, 4, 5, 0, 1, 2)]
            rows, _ = note_rows(sizes)
            for chip in range(CHIPS):
                fill_note(notes, chip, rows, vectors, chip, sizes)
            send_notes(notes, gw_refs, nsem)
            wait_notes(notes, gw_refs, nsem)
        wait_all(gout, out_sem)
        wait_all(buf, sem)


def mid_grad(low, gup, ctx, attn, count, given=()):
    total, width = low.shape
    ff = gup.shape[1]
    halves = halves_of(count)
    n_up = ff // width
    sizes = [ff // CHIPS] + [width // CHIPS] * 6 if given else []
    gw = piece_structs(count, width * halves // count, (width + ff) // halves + (128 if given else 0))
    fixed = lambda *shape: pl.BlockSpec(shape, lambda i: (0, 0))
    scratch = [pltpu.VMEM((n_up, width, width), BF), pltpu.VMEM((width, width), BF)]
    scratch += [pltpu.VMEM((total, width), BF)] * 2 + [DMA, DMA, sems(GROUPS + 1)]
    scratch += [pltpu.VMEM((CHIPS, width // CHIPS, 128), BF), DMA] if given else []
    return call(
        partial(mid_grad_kernel, sizes, len(gw), n_up),
        "mid_grad",
        13 * MICROSECOND,
        gw,
        [fixed(total, width), pl.BlockSpec((total, width), lambda i: (0, jnp.minimum(i, n_up - 1)))]
        + [HBM] * (GROUPS + 1)
        + [fixed(*v.shape) for v in given],
        (HBM,) * len(gw),
        scratch,
        grid=(n_up + 1,),
    )(low, gup, *ctx, attn, *given)


def attn_back_kernel(docs, rows, n_sums, n_out, count_ref, joined_ref, proj_ref, gctx_ref, lse_ref, *refs):
    earlier, refs = refs[:n_sums], refs[n_sums:]
    gproj_ref, sums_ref = refs[:2]
    gw_refs, refs = refs[2 : 2 + n_out], refs[2 + n_out :]
    gbuf, osem, probs_buf, gscores_buf = refs[:4]
    width = joined_ref.shape[1]
    span = width // GROUPS

    def doc_step(d, carry):
        base = pl.multiple_of(d * rows, 128)
        at = pl.ds(base, rows)
        count = count_ref[d]
        for lo in range(0, span, 128):
            pair, first = lo // 128, 3 * lo
            keys = proj_ref[at, first + 128 : first + 256]
            values = proj_ref[at, first + 256 : first + 384]
            all_queries, all_grads = [], []
            for block in range(0, rows, QUERIES):
                here = pl.ds(pl.multiple_of(base + block, 128), QUERIES)
                cols = slice(2 * block, 2 * block + 2 * QUERIES)
                queries = both_heads(proj_ref[here, first : first + 128] * BF(score_scale))
                grads = both_heads(gctx_ref[here, lo : lo + 128])
                scores = masked(mm(keys, queries, NT), count, rows - SLOTS)
                probs = jnp.exp(scores - lse_ref[d, pair, :, cols])
                gprobs = mm(values, grads, NT)
                dot = jnp.sum(probs * gprobs, axis=0, keepdims=True)
                probs_buf[pair, :, cols] = probs.astype(BF)
                gscores_buf[pair, :, cols] = (probs * (gprobs - dot)).astype(BF)
                all_queries.append(queries)
                all_grads.append(grads)
            gscores = gscores_buf[pair]
            dv = mm(probs_buf[pair], jnp.concatenate(all_grads, axis=0))
            dk = mm(gscores, jnp.concatenate(all_queries, axis=0))
            dq = mm((keys * BF(score_scale)).T, gscores)
            gproj_ref[at, first + 128 : first + 256] = dk.astype(BF)
            gproj_ref[at, first + 256 : first + 384] = dv.astype(BF)
            for block in range(0, rows, QUERIES):
                here = pl.ds(pl.multiple_of(base + block, 128), QUERIES)
                part = own_lanes(dq[:, 2 * block : 2 * block + 2 * QUERIES])
                gproj_ref[here, first : first + 128] = part.T.astype(BF)
        return carry

    lax.fori_loop(0, docs, doc_step, 0)
    half_width = width // 2

    def grad_step(r, carry):
        at = rows_at(r, half_width)
        gbuf[at, :] = mm(joined_ref[:, at], gproj_ref[...], TN).astype(BF)
        store_rows(gbuf, r * half_width, half_width, gw_refs, osem, half_width)
        return carry

    lax.fori_loop(0, 2, grad_step, 0)
    total = jnp.sum(gproj_ref[...].astype(F32), axis=0, keepdims=True)
    sums_ref[...] = total
    if n_sums:
        notes, nsem = refs[4:]
        parts = [ref[...] for ref in earlier] + [total]
        vector = jnp.concatenate(
            [p[:, at + t : at + t + 128] for t in (0, 256) for p in parts for at in range(0, width, 384)],
            axis=1,
        )
        notes[...] = jnp.zeros_like(notes)
        size = 2 * width // CHIPS
        for chip in range(CHIPS):
            notes[chip, 0:1, 0:size] = vector[:, chip * size : (chip + 1) * size].astype(BF)
        send_notes(notes, gw_refs, nsem)
        wait_notes(notes, gw_refs, nsem)
    wait_all(gbuf, osem)


def attn_back(seg_count, joined, proj, gctx, lse, count, sums=()):
    docs = seg_count.shape[0]
    total, width = joined.shape
    rows = total // docs
    span = width // GROUPS
    halves = halves_of(count)
    note = 128 if sums else 0
    scratch = [pltpu.VMEM((width, width), BF), DMA]
    scratch += [pltpu.VMEM((span // 128, rows, 2 * rows), BF)] * 2
    scratch += [pltpu.VMEM((CHIPS, width // CHIPS, 128), BF), DMA] if sums else []
    gw = piece_structs(count, width * halves // count, width // halves + note)
    gproj, total_sums, *gw = call(
        partial(attn_back_kernel, docs, rows, len(sums), len(gw)),
        "attn_back",
        14 * MICROSECOND,
        (
            struct((total, width)),
            struct((1, width), F32),
        )
        + gw,
        [SMEM] + [VMEM] * (4 + len(sums)),
        (VMEM, VMEM) + (HBM,) * len(gw),
        scratch,
    )(seg_count, joined, proj, gctx, lse, *sums)
    return gproj, total_sums, gw


def text_kernel(doc, shape, ids_ref, resid_ref, *refs):
    grads = refs[:GROUPS]
    sets, refs = [], refs[GROUPS:]
    for n_arrays in shape:
        sets.append(refs[:n_arrays])
        refs = refs[n_arrays:]
    n = len(shape)
    out_hbm, out_ref, out_sem = refs[-2 * n - 3 : -2 * n]
    bufs, piece_sems = refs[-2 * n : -n], refs[-n:]
    width = resid_ref.shape[1]
    text_len = out_ref.shape[0]
    at = pl.ds(doc * (text_len + SLOTS), text_len + SLOTS)
    for pieces, buf, sem in zip(sets, bufs, piece_sems):
        load_pieces(pieces, buf, sem, qkv_parts(0, buf.shape[1] // width))
    ids_row = ids_ref[doc : doc + 1, :]
    divisor = divisor_of(ids_row)
    total, g = resid_ref[at, :], 0
    for buf, sem in zip(bufs, piece_sems):
        wait_all(buf, sem)
        for i in range(buf.shape[1] // width):
            total = total + mm(grads[g][at, :], buf[:, i * width : (i + 1) * width], NT)
            g += 1
    summed = (total[text_len:, :] / divisor).astype(BF)
    out_ref[...] = total[:text_len, :] + mm(one_hot_of(ids_row, BF), summed, TN)
    fetch(out_ref, out_hbm.at[doc], out_sem).wait()


def text_grad(doc, slot_ids, resid1, grads, sets, earlier=None):
    docs, text_len = slot_ids.shape
    total, width = resid1.shape
    pieces = [piece for pieces, _ in sets for piece in pieces]
    given = () if earlier is None else (earlier,)
    return call(
        partial(text_kernel, doc, [len(pieces) for pieces, _ in sets]),
        "text_grad",
        7 * MICROSECOND,
        struct((docs, text_len, width), F32),
        [VMEM] * (2 + len(grads)) + [HBM] * len(pieces) + [HBM] * len(given),
        HBM,
        [pltpu.VMEM((text_len, width), F32), DMA]
        + [pltpu.VMEM((width, groups * width), BF) for _, groups in sets]
        + [DMA] * len(sets),
        room=6,
        aliases={2 + len(grads) + len(pieces): 0} if given else {},
    )(slot_ids, resid1, *grads, *pieces, *given)


AXES = ("rep", "shard")


def flips(core):
    return (1, 2) if core == 0 else (2, 1)


def pairs(flip_of):
    return [
        (core * CHIPS + s, core * CHIPS + (s ^ flip_of(core)))
        for core in range(2)
        for s in range(CHIPS)
    ]


Z_PERMS = [pairs(lambda core, k=k: k << 2) for k in (1, 2, 3)]
FIRST = pairs(lambda core: flips(core)[0])
SECOND = pairs(lambda core: flips(core)[1])
SWAP = [(core * CHIPS + s, (1 - core) * CHIPS + s) for core in range(2) for s in range(CHIPS)]


def send(array, perm):
    return lax.ppermute(array, AXES, perm)


def after(value, *earlier):
    return lax.optimization_barrier((value, *earlier))[0] if earlier else value


def add(left, right):
    return (left.astype(F32) + right.astype(F32)).astype(BF)


class Gather:
    def __init__(self, own):
        self.own = own

    def far(self, *earlier):
        self.own = after(self.own, *earlier)
        self.got = [send(self.own, perm) for perm in Z_PERMS]

    def first(self, *earlier):
        self.got_first = self.got[0]
        self.column = jnp.concatenate([self.own] + [after(part, *earlier) for part in self.got], axis=0)
        self.got = send(self.column, FIRST)
        self.swapped = [send(self.column, SWAP)]

    def second(self, *earlier):
        self.near = after(self.got, *earlier)
        self.got = [send(self.column, SECOND), send(self.near, SECOND)]
        self.swapped += [send(self.near, SWAP)]

    def swap(self, *earlier):
        self.got = [after(part, *earlier) for part in self.got]
        self.swapped += [send(part, SWAP) for part in self.got]
        self.all = [self.column, self.near] + self.got + self.swapped


class Scatter:
    def __init__(self):
        self.parts, self.widths = [], []

    def swap(self, pair):
        self.parts.append([(pair[0], 0), (send(pair[1], SWAP), 0)])
        self.widths.append(pair[0].shape[2])

    def join(self, other):
        self.parts += other.parts
        self.widths += other.widths

    def receive(self, *earlier):
        got, col = after(self.got, *earlier), 0
        for part, n in zip(self.parts, self.widths):
            part.append((got, col))
            col += n

    def summed(self, at, dtype=BF):
        sums = [
            sum(term[at, :, col : col + n].astype(F32) for term, col in part).astype(dtype)
            for part, n in zip(self.parts, self.widths)
        ]
        return sums[0] if len(sums) == 1 else jnp.concatenate(sums, axis=2)

    def pass_on(self, at, perm):
        self.away = self.summed(at)
        self.got = send(self.away, perm)

    def second(self, *earlier):
        for part in self.parts:
            part[1] = (after(part[1][0], *earlier), 0)
        self.pass_on(slice(8, 16), SECOND)

    def first(self, *earlier):
        self.receive(*earlier)
        self.pass_on(slice(4, 8), FIRST)

    def far(self, *earlier):
        self.receive(*earlier)
        self.away = [self.summed(slice(k, k + 1)) for k in (1, 2, 3)]
        self.got = [send(part, perm) for part, perm in zip(self.away, Z_PERMS)]

    def total(self, *earlier):
        mine = self.summed(slice(0, 1), F32)
        for part in self.got:
            mine = mine + after(part, *earlier).astype(F32)
        self.mine = mine[0]
        self.theirs = send(self.mine, SWAP)


def to_pairs(array):
    width = array.shape[1] // 3
    return jnp.concatenate(
        [array[:, t * width + p : t * width + p + 128] for p in range(0, width, 128) for t in range(3)],
        axis=1,
    )


def from_pairs(array):
    width = array.shape[1] // 3
    return jnp.concatenate(
        [array[:, 3 * p + t * 128 : 3 * p + t * 128 + 128] for t in range(3) for p in range(0, width, 128)],
        axis=1,
    )


def finish_mid_kernel(sizes, mine_ref, theirs_ref, out_ref, up_ref, *vector_refs):
    core = lax.axis_index("rep")
    n = out_ref.shape[1] // 2
    m = up_ref.shape[1] // 2
    for ref, half in ((mine_ref, core), (theirs_ref, 1 - core)):
        up_ref[:, pl.ds(pl.multiple_of(half * m, 128), m)] = ref[:, :m]
        out_ref[:, pl.ds(pl.multiple_of(half * n, 128), n)] = ref[:, m : m + n]
    rows, total = note_rows(sizes)
    note = jnp.where(core == 0, mine_ref[0:NOTE_ROWS, n + m :], theirs_ref[0:NOTE_ROWS, n + m :])
    for first, size, ref in zip(rows, sizes, vector_refs):
        for lane in range(0, size, 128):
            k = min(128, size - lane)
            ref[0:1, lane : lane + k] = note[first + lane // 128 : first + lane // 128 + 1, 0:k]


def finish_mid(mine, theirs, width, ff):
    rows = mine.shape[0]
    sizes = [ff // CHIPS] + [width // CHIPS] * 6
    return call(
        partial(finish_mid_kernel, sizes),
        "finish_mid",
        0,
        (struct((rows, width), F32), struct((rows, ff), F32)) + tuple(struct((1, n), F32) for n in sizes),
        [VMEM, VMEM],
        (VMEM,) * (2 + len(sizes)),
    )(mine, theirs)


def finish_qkv_kernel(groups, *refs):
    pairs_of = [(refs[2 * i], refs[2 * i + 1]) for i in range(len(groups))]
    out_ref, bias_ref = refs[2 * len(groups) :]
    core = lax.axis_index("rep")
    width = out_ref.shape[1] // 3
    g = 0
    for n, (mine_ref, theirs_ref) in zip(groups, pairs_of):
        for i in range(n):
            for ref, half in ((mine_ref, core), (theirs_ref, 1 - core)):
                for t in range(3):
                    to = pl.ds(pl.multiple_of(t * width + (2 * g + half) * 128, 128), 128)
                    out_ref[:, to] = ref[:, i * 384 + t * 128 : i * 384 + (t + 1) * 128]
            g += 1
    mine_ref, theirs_ref = pairs_of[-1]
    k = bias_ref.shape[1]
    at = mine_ref.shape[1] - 128
    bias_ref[...] = jnp.where(core == 0, mine_ref[0:1, at : at + k], theirs_ref[0:1, at : at + k])


def finish_qkv(parts, groups, width):
    rows = parts[0].shape[0]
    return call(
        partial(finish_qkv_kernel, groups),
        "finish_qkv",
        0,
        (struct((rows, 3 * width), F32), struct((1, 2 * width // CHIPS), F32)),
        [VMEM] * len(parts),
        (VMEM, VMEM),
    )(*parts)


def body(
    text_rows,
    slot_ids,
    seg_count,
    w_qkv,
    qv_bias,
    w_out,
    out_bias,
    ln1_gain,
    ln1_shift,
    w_up,
    up_bias,
    w_down,
    down_bias,
    ln2_gain,
    ln2_shift,
    cotangent,
):
    docs, text_len, width = text_rows.shape
    rows = text_len + SLOTS
    ff = w_up.shape[1]
    chips = lax.axis_size("shard")
    small = (qv_bias, out_bias, ln1_gain, ln1_shift, up_bias, down_bias, ln2_gain, ln2_shift)
    sizes = [v.shape[0] for v in small]
    cot = cotangent.reshape(docs * rows, width)
    if chips != CHIPS or lax.axis_size("rep") != 2:
        return plain(text_rows, slot_ids, seg_count, w_qkv, w_out, w_up, w_down, small, cot)

    core = lax.axis_index("rep")
    own_qkv, own_mid, own_down = prepare(w_qkv, w_out, w_up, w_down, small)
    qkv, mid, down = Gather(own_qkv), Gather(own_mid), Gather(own_down)
    qkv.far()
    mid.far()
    joined = pool(slot_ids, text_rows)
    qkv.first(joined, mid.got[0])
    down.far(qkv.column)
    qkv.second(*mid.got[1:])
    mid.first()
    qkv.swap()
    table = unpack(sizes, [qkv.column, qkv.near] + qkv.got, ff)
    mid.second(*down.got)
    down.first()
    proj0, ctx0, lse0 = attn_fwd(0, 0, seg_count, after(joined, mid.near, down.column), table, qkv.all)
    proj1, ctx1, lse1 = attn_fwd(1, 1, seg_count, after(joined, ctx0), table, qkv.all)
    proj2, ctx2, lse2 = attn_fwd(2, 2, seg_count, after(joined, ctx1), table, qkv.all)
    down.second(ctx2)
    mid.swap()
    down.swap()
    ctx = (ctx0, ctx1, ctx2)
    low, grad_up, layer_out, resid_one, attn, grad_ctx, sums, sums_up, gw_down = forward_call(
        joined, ctx, cot, table, mid.all, down.all, ff
    )
    s_down, s_mid, s_qkv = Scatter(), Scatter(), Scatter()
    s_down.swap(gw_down)
    gw_mid = mid_grad(low, grad_up, ctx, attn, 2 * CHIPS, (sums, sums_up))
    s_down.second(gw_mid[0])
    s_mid.swap(gw_mid)
    gp0, sp0, gw0 = attn_back(
        seg_count, joined, proj0, after(grad_ctx[0], s_down.away), lse0, 2 * CHIPS
    )
    s_mid.second(gp0)
    s_down.first(gp0)
    s_qkv.swap(gw0)
    gp1, sp1, gw1 = attn_back(
        seg_count, joined, proj1, after(grad_ctx[1], gp0, s_down.away, s_mid.away), lse1, 2 * CHIPS
    )
    s_down.far(gp1)
    s_mid.first(gp1)
    s_qkv.swap(gw1)
    gp2, sp2, gw2 = attn_back(
        seg_count, joined, proj2, after(grad_ctx[2], gp1, *s_down.away, s_mid.away), lse2, 2 * CHIPS, (sp0, sp1)
    )
    s_mid.far(gp2)
    s_down.total(gp2)
    s_qkv.swap(gw2)
    s_qkv.second(gp2)
    grads, sets = (gp0, gp1, gp2), ((qkv.all, 3),)
    grad_text = text_grad(0, slot_ids, after(resid_one, *s_mid.away, s_qkv.away, s_down.mine), grads, sets)
    s_qkv.first(grad_text)
    grad_text = text_grad(1, slot_ids, after(resid_one, s_qkv.away), grads, sets, grad_text)
    s_mid.total(grad_text)
    s_qkv.far(grad_text)
    s_qkv.total()
    low_half = jnp.where(core == 0, s_down.mine, s_down.theirs)
    high_half = jnp.where(core == 0, s_down.theirs, s_down.mine)
    g_down = jnp.concatenate([low_half, high_half], axis=0)
    g_out, g_up, *vectors = finish_mid(s_mid.mine, s_mid.theirs, width, ff)
    b_up, b_out, b_gain1, b_shift1, b_down, b_gain2, b_shift2 = [
        vectors[i][0] for i in (0, 3, 1, 2, 6, 4, 5)
    ]
    g_qkv, g_bias = finish_qkv([s_qkv.mine, s_qkv.theirs], (3,), width)
    return (
        layer_out.reshape(docs, rows, width),
        grad_text,
        g_qkv,
        g_bias[0],
        g_out,
        b_out,
        b_gain1,
        b_shift1,
        g_up,
        b_up,
        g_down,
        b_down,
        b_gain2,
        b_shift2,
    )


def plain(text_rows, slot_ids, seg_count, w_qkv, w_out, w_up, w_down, small, cot):
    docs, text_len, width = text_rows.shape
    rows = text_len + SLOTS
    ff = w_up.shape[1]
    chips = lax.axis_size("shard")
    shard = lax.axis_index("shard")
    whole = lambda w: [lax.all_gather(w, "shard", axis=0, tiled=True)[None]]
    qkv, down = whole(to_pairs(w_qkv)), whole(w_down)
    mid = whole(jnp.concatenate([w_out, w_up], axis=1))
    sizes = [v.shape[0] for v in small]
    starts = [sum(sizes[:i]) for i in range(len(sizes))]
    notes = lax.all_gather(jnp.concatenate(small)[None], "shard", axis=0, tiled=True).astype(F32)
    full = [notes[:, a : a + n].reshape(1, chips * n) for a, n in zip(starts, sizes)]
    table = jnp.concatenate([jnp.pad(v, ((0, 0), (0, ff - v.shape[1]))) for v in full], axis=0)
    joined = pool(slot_ids, text_rows)
    proj, ctx, lse = zip(*[attn_fwd(g, g, seg_count, joined, table, qkv) for g in range(GROUPS)])
    low, grad_up, layer_out, resid_one, attn, grad_ctx, sums, sums_up, gw_down = forward_call(
        joined, ctx, cot, table, mid, down, ff
    )
    gw_mid = mid_grad(low, grad_up, ctx, attn, 1)
    back = [attn_back(seg_count, joined, proj[g], grad_ctx[g], lse[g], 1) for g in range(GROUPS)]
    grad_text = None
    for doc in range(docs):
        grads = [b[0] for b in back]
        grad_text = text_grad(doc, slot_ids, resid_one, grads, ((qkv, GROUPS),), grad_text)
    spread = lambda g: lax.psum(
        lax.psum_scatter(g.astype(F32), "shard", scatter_dimension=0, tiled=True), "rep"
    )
    g_down, g_mid = spread(gw_down[0][0]), spread(gw_mid[0][0])
    g_qkv = from_pairs(spread(jnp.concatenate([b[2][0][0] for b in back], axis=1)))
    sums, sums_up = lax.psum((sums, sums_up), AXES)
    sums_proj = from_pairs(lax.psum(jnp.concatenate([b[1] for b in back], axis=1), AXES))
    mine = lambda v: lax.dynamic_slice_in_dim(v, shard * (v.shape[0] // chips), v.shape[0] // chips, 0)
    return (
        layer_out.reshape(docs, rows, width),
        grad_text,
        g_qkv,
        mine(jnp.concatenate([sums_proj[0, :width], sums_proj[0, 2 * width :]])),
        g_mid[:, ff:],
        mine(sums[5]),
        mine(sums[3]),
        mine(sums[4]),
        g_mid[:, :ff],
        mine(sums_up[0]),
        g_down,
        mine(sums[2]),
        mine(sums[0]),
        mine(sums[1]),
    )


def solution(mesh):
    in_specs = (
        P(("rep", "shard"), None, None),
        P(("rep", "shard"), None),
        P(("rep", "shard")),
        P("shard", None),
        P("shard"),
        P("shard", None),
        P("shard"),
        P("shard"),
        P("shard"),
        P("shard", None),
        P("shard"),
        P("shard", None),
        P("shard"),
        P("shard"),
        P("shard"),
        P(("rep", "shard"), None, None),
    )
    out_specs = (
        P(("rep", "shard"), None, None),
        P(("rep", "shard"), None, None),
        P("shard", None),
        P("shard"),
        P("shard", None),
        P("shard"),
        P("shard"),
        P("shard"),
        P("shard", None),
        P("shard"),
        P("shard", None),
        P("shard"),
        P("shard"),
        P("shard"),
    )
    return jax.shard_map(body, mesh=mesh, in_specs=in_specs, out_specs=out_specs, check_vma=False)
```
